256 devices in a mesh: rows: 256 (over z, y, x, core).
Axes of the slice: x: 4, y: 4, z: 8, core: 2. Of those that a mesh axis runs over, the one named last changes fastest.
Arguments:
- trailing: float32 [131072, 1024], P('rows'), may hold values from -50 to 50
- leaf_vectors: float32 [131072, 256], P('rows'), may hold values from -2 to 2, as said below
- leaf_factors: float32 [65536, 256], P('rows'), may hold values from -2 to 2, as said below
- tree_vectors: float32 [65536, 256], P('rows'), may hold values from -2 to 2, as said below
- tree_factors: float32 [65536, 256], P('rows'), may hold values from -2 to 2, as said below
- inverse_factor: float32 [256, 256], replicated, may hold values from -2 to 2, as said below
Outputs:
- updated: float32 [131072, 1024], P('rows')
- panel_basis: float32 [131072, 256], P('rows')
- panel_gram: float32 [256, 256], replicated
The draws below stay inside these ranges and needn't reach their ends.
Inputs may be any that keep to these rules, and one draw needn't show every extreme that they name: Within each leaf, rows 0 to 255 of leaf_vectors form a unit lower triangular matrix (ones on the diagonal, zeros above); leaf_factors_p is the upper triangular factor for which I - leaf_vectors_p leaf_factors_p leaf_vectors_p^T is orthogonal. `leaf_factors`: each block is upper triangular and is the factor described for leaf_vectors. `tree_vectors`: each block is upper triangular, diagonal included; with Y = [I; tree_vectors_q], I - Y tree_factors_q Y^T is orthogonal. `tree_factors`: each block is upper triangular and is the factor described for tree_vectors. `inverse_factor`: upper triangular with a positive diagonal.
All inputs are finite; a program needn't handle non-finite values.
Results may differ from the reference program's by a relative error of at most 0.00018.
Values sent between devices are 32-bit elements; how exact they have to be, the bound alone decides.
A program may use at most 64 MiB of HBM per device.

```python
import math
import jax
import jax.numpy as jnp
from jax import lax

PANEL = 256
NC = 1024
ROWS_DEV = 512
LEVELS = 8
ROWS_ALL = 131072
TREE_ROWS = 65536


def factor_from(gram_part):
    diagonal_part = jnp.diagonal(gram_part, axis1=1, axis2=2)
    upper_part = jnp.triu(gram_part, 1) + jax.vmap(jnp.diag)(diagonal_part * 0.5)
    identity = jnp.eye(PANEL, dtype=jnp.float32)
    return jax.vmap(lambda m: jax.scipy.linalg.solve_triangular(m, identity, lower=False))(upper_part)


def leaf_pair(key):
    draw_key = jax.random.fold_in(key, 11)
    block_count = ROWS_ALL // ROWS_DEV
    samples = jax.random.truncated_normal(draw_key, -6.0, 6.0, (block_count, ROWS_DEV, PANEL), jnp.float32) / math.sqrt(ROWS_DEV)
    row_index = lax.broadcasted_iota(jnp.int32, (ROWS_DEV, PANEL), 0)
    col_index = lax.broadcasted_iota(jnp.int32, (ROWS_DEV, PANEL), 1)
    vectors = jnp.where(row_index > col_index, samples, jnp.where(row_index == col_index, 1.0, 0.0))
    gram_part = jnp.einsum('brp,brq->bpq', vectors, vectors, precision=lax.Precision.HIGHEST)
    return (vectors, factor_from(gram_part))


def tree_pair(key):
    draw_key = jax.random.fold_in(key, 23)
    block_count = TREE_ROWS // PANEL
    samples = jax.random.truncated_normal(draw_key, -6.0, 6.0, (block_count, PANEL, PANEL), jnp.float32) / math.sqrt(PANEL)
    row_index = lax.broadcasted_iota(jnp.int32, (PANEL, PANEL), 0)
    col_index = lax.broadcasted_iota(jnp.int32, (PANEL, PANEL), 1)
    vectors = jnp.where(row_index <= col_index, samples, 0.0)
    gram_part = jnp.eye(PANEL, dtype=jnp.float32) + jnp.einsum('brp,brq->bpq', vectors, vectors, precision=lax.Precision.HIGHEST)
    return (vectors, factor_from(gram_part))


def draw_trailing(key, part):
    block_count = ROWS_ALL // ROWS_DEV
    leaf_index = jnp.arange(ROWS_ALL, dtype=jnp.int32) // ROWS_DEV
    row_ramp = 0.5 + leaf_index.astype(jnp.float32) / max(block_count - 1, 1)
    values = jax.random.truncated_normal(key, -6.0, 6.0, (ROWS_ALL, NC), jnp.float32)
    return values * row_ramp[:, None]


def draw_leaf_vectors(key, part):
    vectors, factors = leaf_pair(key)
    return vectors.reshape(ROWS_ALL, PANEL)


def draw_leaf_factors(key, part):
    vectors, factors = leaf_pair(key)
    return factors.reshape(TREE_ROWS, PANEL)


def draw_tree_vectors(key, part):
    vectors, factors = tree_pair(key)
    return vectors.reshape(TREE_ROWS, PANEL)


def draw_tree_factors(key, part):
    vectors, factors = tree_pair(key)
    return factors.reshape(TREE_ROWS, PANEL)


def draw_inverse_factor(key, part):
    key_a, key_b = jax.random.split(jax.random.fold_in(key, 37))
    diagonal_part = jnp.exp(jax.random.uniform(key_a, (PANEL,), jnp.float32, math.log(0.5), math.log(2.0)))
    samples = jax.random.truncated_normal(key_b, -6.0, 6.0, (PANEL, PANEL), jnp.float32) * (0.5 / math.sqrt(PANEL))
    return jnp.triu(samples, 1) + jnp.diag(diagonal_part)


def setup_inputs(seed: int = 0) -> dict:
    streams_of = jax.random.split(jax.random.key(seed), 7)
    trailing = draw_trailing(jax.random.fold_in(streams_of[6], 71), 0)
    leaf_vectors = draw_leaf_vectors(jax.random.fold_in(streams_of[6], 71), 0)
    leaf_factors = draw_leaf_factors(jax.random.fold_in(streams_of[6], 71), 0)
    tree_vectors = draw_tree_vectors(jax.random.fold_in(streams_of[6], 71), 0)
    tree_factors = draw_tree_factors(jax.random.fold_in(streams_of[6], 71), 0)
    inverse_factor = draw_inverse_factor(jax.random.fold_in(streams_of[6], 71), 0)
    return {"trailing": trailing, "leaf_vectors": leaf_vectors, "leaf_factors": leaf_factors, "tree_vectors": tree_vectors, "tree_factors": tree_factors, "inverse_factor": inverse_factor}


HIGHEST = lax.Precision.HIGHEST

def multiply(left_side, right_side):
    return jnp.dot(left_side.astype(jnp.float32), right_side.astype(jnp.float32), precision=HIGHEST, preferred_element_type=jnp.float32)

def leaf_apply(inputs):
    piece, vectors, factors = inputs
    coeffs = multiply(factors.T, multiply(vectors.T, piece))
    return piece - multiply(vectors, coeffs)

def reference(trailing, leaf_vectors, leaf_factors, tree_vectors, tree_factors, inverse_factor):
    block_count = ROWS_ALL // ROWS_DEV
    pieces = trailing.reshape(block_count, ROWS_DEV, NC)
    leaf_out = lax.map(leaf_apply, (pieces, leaf_vectors.reshape(block_count, ROWS_DEV, PANEL), leaf_factors.reshape(block_count, PANEL, PANEL)))
    head_rows = leaf_out[:, :PANEL, :]
    all_vectors = tree_vectors.reshape(block_count, PANEL, PANEL)
    all_factors = tree_factors.reshape(block_count, PANEL, PANEL)
    for tree_level in range(LEVELS):
        stride = 2 ** tree_level
        groups = block_count // (2 * stride)
        grouped = head_rows.reshape(groups, 2, stride, PANEL, NC)
        low_rows = grouped[:, 0, 0]
        high_rows = grouped[:, 1, 0]
        pair_vectors = all_vectors.reshape(groups, 2, stride, PANEL, PANEL)[:, 1, 0]
        pair_factors = all_factors.reshape(groups, 2, stride, PANEL, PANEL)[:, 1, 0]
        inner = low_rows + jnp.einsum('gqp,gqn->gpn', pair_vectors, high_rows, precision=HIGHEST)
        coeffs = jnp.einsum('gqp,gqn->gpn', pair_factors, inner, precision=HIGHEST)
        low_rows = low_rows - coeffs
        high_rows = high_rows - jnp.einsum('gpq,gqn->gpn', pair_vectors, coeffs, precision=HIGHEST)
        grouped = grouped.at[:, 0, 0].set(low_rows).at[:, 1, 0].set(high_rows)
        head_rows = grouped.reshape(block_count, PANEL, NC)
    result_rows = leaf_out.at[:, :PANEL, :].set(head_rows).reshape(ROWS_ALL, NC)
    panel_cols = result_rows[:, :PANEL]
    lower_cols = panel_cols[PANEL:]
    gram_sum = multiply(lower_cols.T, lower_cols) / ROWS_ALL
    row_index = lax.broadcasted_iota(jnp.int32, (ROWS_ALL, PANEL), 0)
    basis = jnp.where(row_index >= PANEL, multiply(panel_cols, inverse_factor), 0.0)
    return (result_rows, basis, gram_sum)
```

```python
import functools

import jax
import jax.numpy as jnp
from jax import lax
from jax.experimental import pallas as pl
from jax.experimental.pallas import tpu as pltpu
from jax.sharding import PartitionSpec as P

HIGH = lax.Precision.HIGH
F32 = jnp.float32
BF16 = jnp.bfloat16
ROW = 8
YDIM = 4


def product(left_side, right_side):
    return jnp.dot(left_side, right_side, precision=HIGH, preferred_element_type=F32)


def across(left_side, right_side):
    return lax.dot_general(
        left_side,
        right_side,
        (((0,), (0,)), ((), ())),
        precision=HIGH,
        preferred_element_type=F32,
    )


def halves(value):
    high = value.astype(BF16)
    low = (value - high.astype(F32)).astype(BF16)
    return high, low


def dot3(left_side, right_side, transposed=False):
    dims = (((1,), (1 if transposed else 0,)), ((), ()))
    left_high, left_low = halves(left_side)
    right_high, right_low = halves(right_side)

    def one(a, b):
        return lax.dot_general(a, b, dims, preferred_element_type=F32)

    return one(left_high, right_high) + (
        one(left_high, right_low) + one(left_low, right_high)
    )


def tree_kernel(
    devices,
    total_rows,
    head_ref,
    pack_ref,
    gram_ref,
    head_out,
    gram_out,
    ops,
    bop,
    cur0,
    cur1,
    cur2,
    z0, in0, w0, wb0,
    z1, in1, w1, wb1,
    z2, in2, w2, wb2,
    send3,
    recv3,
    back3,
    wback3,
    res1,
    res2,
    res3,
    gathered,
    gram_in,
    gram_piece,
    gram_level,
    panel,
    full,
    gram_all,
    send_sems,
    recv_sems,
):
    b = pack_ref.shape[1]
    nc = head_ref.shape[1]
    half, quarter, eighth = nc // 2, nc // 4, nc // 8
    rows = devices // ROW
    row_levels = rows.bit_length() - 1
    zdim = rows // YDIM
    piece = b // ROW
    me = lax.axis_index("rows")
    r = me % ROW
    g = me // ROW
    core = r % 2
    x0 = (r // 2) % 2
    x1 = r // 4
    base = g * ROW
    neighbour = base + (r + 1) % ROW
    y = g % YDIM
    first_y = y == 0

    def is_low(k):
        return g % (2 << k) == 0

    def is_member(other):
        return r == other

    def is_high(k):
        return g % (2 << k) == (1 << k)

    slot = [ops.at[i] for i in range(4 + row_levels)]
    wback = [wback3.at[k] for k in range(row_levels)]

    barrier = pltpu.get_barrier_semaphore()

    def meet(condition, other):
        @pl.when(condition)
        def _():
            pl.semaphore_signal(
                barrier, inc=1, device_id=(other,),
                device_id_type=pl.DeviceIdType.MESH,
            )

        return condition

    met = []
    for j in range(1, ROW):
        pl.semaphore_signal(
            barrier, inc=1, device_id=(base + (r + j) % ROW,),
            device_id_type=pl.DeviceIdType.MESH,
        )
    for k in range(row_levels):
        met.append(meet(is_low(k), me + (ROW << k)))
        met.append(meet(is_high(k), me - (ROW << k)))
    for z in range(1, zdim):
        if z & (z - 1):
            met.append(meet(g == 0, me + z * YDIM * ROW))
            met.append(meet(g == z * YDIM, me - z * YDIM * ROW))
    met.append(meet(first_y, me + 3 * ROW))
    met.append(meet(y == 3, me - 3 * ROW))
    peers = ROW - 1
    for condition in met:
        peers = peers + condition.astype(jnp.int32)
    pl.semaphore_wait(barrier, peers)

    counter = [0]
    pending = []

    def copy(source, target, number, other, condition=None):
        sem = counter[0]
        counter[0] += 1
        pltpu.make_async_remote_copy(
            src_ref=source,
            dst_ref=target,
            send_sem=send_sems.at[sem],
            recv_sem=recv_sems.at[number],
            device_id=(other,),
            device_id_type=pl.DeviceIdType.MESH,
        ).start()
        pending.append((condition, source, sem))

    def arrived(target, number):
        pltpu.make_async_remote_copy(
            src_ref=target,
            dst_ref=target,
            send_sem=send_sems.at[0],
            recv_sem=recv_sems.at[number],
            device_id=(neighbour,),
            device_id_type=pl.DeviceIdType.MESH,
        ).wait_recv()

    def when(condition, action):
        @pl.when(condition)
        def _():
            action()

    OPS, X0, W0, X1, W1, X2, W2, Z3, W3, GATHER, GROW, GLEV, PANEL, GZ, GY, GX = (
        0, 9, 10, 11, 12, 13, 14, 15, 20, 21, 29, 37, 42, 44, 45, 46,
    )

    row_id = lax.broadcasted_iota(jnp.int32, (b, b), 0)
    col_id = lax.broadcasted_iota(jnp.int32, (b, b), 1)

    def v_of(ref):
        return jnp.where(row_id <= col_id, ref[:b, :], 0.0)

    def a_of(ref):
        diagonal = jnp.where(row_id == col_id, ref[b : b + 1, :], 0.0)
        return jnp.where(row_id > col_id, ref[:b, :], diagonal)

    @pl.when(core == 1)
    def _():
        copy(pack_ref, slot[0], OPS + 0, me - 1, lambda: core == 1)
        ops[0] = pack_ref[...]

    @pl.when((r == 2) | (r == 6))
    def _():
        c = lambda: (r == 2) | (r == 6)
        copy(pack_ref, slot[1], OPS + 1, me - 2, c)
        copy(pack_ref, slot[1], OPS + 1, me + 1, c)
        ops[1] = pack_ref[...]

    @pl.when(r == 4)
    def _():
        for other in (0, 2, 6, 5):
            copy(pack_ref, slot[2], OPS + 2, base + other, lambda: r == 4)
        ops[2] = pack_ref[...]

    @pl.when(core == 0)
    def _():
        c = lambda: core == 0
        copy(head_ref.at[:, pl.ds(half, half)], in0, X0, me + 1, c)

    @pl.when(core == 1)
    def _():
        c = lambda: core == 1
        bop[0] = dot3(a_of(slot[0]), v_of(slot[0]), True)
        z0[...] = dot3(bop[0], head_ref[:, :half])
        copy(z0, in0, X0, me - 1, c)

    @pl.when(core == 0)
    def _():
        c = lambda: core == 0
        arrived(slot[0], OPS + 0)
        update = dot3(a_of(slot[0]), head_ref[:, :half])
        arrived(in0, X0)
        update = update + in0[...]
        cur0[...] = head_ref[:, :half] - update
        w0[...] = update

    @pl.when(core == 1)
    def _():
        arrived(in0, X0)
        update = dot3(a_of(slot[0]), in0[...]) + dot3(bop[0], head_ref[:, half:])
        cur0[...] = in0[...] - update
        w0[...] = update

    @pl.when(x0 == 0)
    def _():
        c = lambda: x0 == 0
        copy(cur0.at[:, pl.ds(quarter, quarter)], in1, X1, me + 2, c)

    @pl.when((r == 0) | (r == 4))
    def _():
        c = lambda: (r == 0) | (r == 4)
        arrived(slot[1], OPS + 1)
        copy(slot[1], slot[1], OPS + 1, me + 1, c)

    @pl.when((core == 1))
    def _():
        arrived(slot[1], OPS + 1)

    @pl.when(x0 == 1)
    def _():
        c = lambda: x0 == 1
        bop[1] = dot3(a_of(slot[1]), v_of(slot[1]), True)
        z1[...] = dot3(bop[1], cur0[:, :quarter])
        copy(z1, in1, X1, me - 2, c)

    @pl.when(core == 0)
    def _():
        c = lambda: core == 0
        copy(w0, wb0, W0, me + 1, c)

    for j in range(1, ROW):
        other = (r + j) % ROW
        copy(
            gram_ref.at[pl.ds(pl.multiple_of(other * piece, 8), piece), :],
            gram_in.at[ROW - j],
            GROW + ROW - j,
            base + other,
        )

    @pl.when((r == 0) & (g > 0))
    def _():
        c = lambda: (r == 0) & (g > 0)
        for other in (4, 2, 6, 1):
            copy(pack_ref, slot[3], OPS + 3, base + other, c)
        ops[3] = pack_ref[...]

    @pl.when((r == 0) | (r == 2) | (r == 6))
    def _():
        c = lambda: (r == 0) | (r == 2) | (r == 6)
        arrived(slot[2], OPS + 2)
        copy(slot[2], slot[2], OPS + 2, me + 1, c)

    @pl.when(x0 == 0)
    def _():
        c = lambda: x0 == 0
        update = dot3(a_of(slot[1]), cur0[:, :quarter])
        arrived(in1, X1)
        update = update + in1[...]
        cur1[...] = cur0[:, :quarter] - update
        w1[...] = update

    @pl.when(x0 == 1)
    def _():
        arrived(in1, X1)
        update = dot3(a_of(slot[1]), in1[...]) + dot3(bop[1], cur0[:, quarter:])
        cur1[...] = in1[...] - update
        w1[...] = update

    @pl.when(x1 == 0)
    def _():
        c = lambda: x1 == 0
        copy(cur1.at[:, pl.ds(eighth, eighth)], in2, X2, me + 4, c)

    @pl.when(core == 1)
    def _():
        arrived(slot[2], OPS + 2)

    @pl.when(x1 == 1)
    def _():
        c = lambda: x1 == 1
        bop[2] = dot3(a_of(slot[2]), v_of(slot[2]), True)
        z2[...] = dot3(bop[2], cur1[:, :eighth])
        copy(z2, in2, X2, me - 4, c)

    @pl.when(x0 == 0)
    def _():
        c = lambda: x0 == 0
        copy(w1, wb1, W1, me + 2, c)

    @pl.when((g > 0) & (core == 0))
    def _():
        c = lambda: (g > 0) & (core == 0) & (r > 0)

        @pl.when(r > 0)
        def _():
            arrived(slot[3], OPS + 3)
            copy(slot[3], slot[3], OPS + 3, me + 1, c)

    @pl.when((g > 0) & (core == 1))
    def _():
        arrived(slot[3], OPS + 3)

    for k in range(row_levels):
        @pl.when(is_high(k))
        def _():
            copy(slot[3], slot[4 + k], OPS + 4 + k, me - (ROW << k), functools.partial(is_high, k))

    @pl.when(core == 1)
    def _():
        v = v_of(slot[0])
        gathered[:, half:] = head_ref[:, half:] - dot3(v, w0[...])
        arrived(wb0, W0)
        gathered[:, :half] = head_ref[:, :half] - dot3(v, wb0[...])

    @pl.when(x1 == 0)
    def _():
        update = dot3(a_of(slot[2]), cur1[:, :eighth])
        arrived(in2, X2)
        update = update + in2[...]
        cur2[...] = cur1[:, :eighth] - update
        w2[...] = update

    @pl.when(x1 == 1)
    def _():
        arrived(in2, X2)
        update = dot3(a_of(slot[2]), in2[...]) + dot3(bop[2], cur1[:, eighth:])
        cur2[...] = in2[...] - update
        w2[...] = update

    for j in range(1, ROW):
        arrived(gram_in.at[ROW - j], GROW + ROW - j)
    own = gram_ref[pl.ds(pl.multiple_of(r * piece, 8), piece), :]
    for j in range(1, ROW):
        own = own + gram_in[j]
    gram_piece[...] = own

    @pl.when(g > 0)
    def _():
        bop[3] = dot3(a_of(slot[3]), v_of(slot[3]), True)

    for k in range(row_levels):
        @pl.when(is_high(k))
        def _():
            c = functools.partial(is_high, k)
            send3[...] = dot3(bop[3], cur2[...])
            copy(send3, recv3.at[k], Z3 + k, me - (ROW << k), c)
            copy(gram_piece, gram_level.at[k], GLEV + k, me - (ROW << k), c)

        if k == 0:
            @pl.when(x1 == 0)
            def _():
                c = lambda: x1 == 0
                copy(w2, wb2, W2, me + 4, c)

            @pl.when(x0 == 1)
            def _():
                v = v_of(slot[1])
                res1[:, quarter:] = cur0[:, quarter:] - dot3(v, w1[...])
                arrived(wb1, W1)
                res1[:, :quarter] = cur0[:, :quarter] - dot3(v, wb1[...])

            @pl.when((x0 == 1) & (core == 1))
            def _():
                c = lambda: (x0 == 1) & (core == 1)
                copy(res1, gathered.at[:, pl.ds(half, half)], GATHER + 1, me - 1, c)

            @pl.when((x0 == 1) & (core == 0))
            def _():
                gathered[:, :half] = res1[...]

        @pl.when(is_low(k))
        def _():
            c = functools.partial(is_low, k)
            arrived(slot[4 + k], OPS + 4 + k)
            update = dot3(a_of(slot[4 + k]), cur2[...])
            arrived(recv3.at[k], Z3 + k)
            update = update + recv3[k]
            cur2[...] = cur2[...] - update
            wback3[k] = update
            copy(wback[k], back3, W3, me + (ROW << k), c)
            arrived(gram_level.at[k], GLEV + k)
            gram_piece[...] = gram_piece[...] + gram_level[k]

        if k == 0:
            @pl.when(x1 == 1)
            def _():
                v = v_of(slot[2])
                res2[:, eighth:] = cur1[:, eighth:] - dot3(v, w2[...])
                arrived(wb2, W2)
                res2[:, :eighth] = cur1[:, :eighth] - dot3(v, wb2[...])

            for other, at in ((5, half), (6, quarter), (7, half + quarter)):
                @pl.when(r == other)
                def _():
                    copy(
                        res2, gathered.at[:, pl.ds(at, quarter)],
                        GATHER + other, base + 4, functools.partial(is_member, other),
                    )

            @pl.when(r == 4)
            def _():
                gathered[:, :quarter] = res2[...]

    for source, at in ((0, 0), (4, eighth)):
        @pl.when((g == 0) & (r == source))
        def _():
            c = functools.partial(lambda s: (g == 0) & (r == s), source)
            for j in range(1, ROW):
                copy(
                    cur2, panel.at[:, pl.ds(at, eighth)],
                    PANEL + source // 4, base + (r + j) % ROW, c,
                )
            panel[:, at : at + eighth] = cur2[...]

    @pl.when(g > 0)
    def _():
        arrived(back3, W3)
        res3[...] = cur2[...] - dot3(v_of(slot[3]), back3[...])

    @pl.when(g == 0)
    def _():
        res3[...] = cur2[...]

    for other in range(1, ROW):
        at = (other % 2) * half + (other // 2 % 2) * quarter + other // 4 * eighth

        @pl.when(r == other)
        def _():
            copy(
                res3, gathered.at[:, pl.ds(at, eighth)],
                GATHER + other, base, functools.partial(is_member, other),
            )

    @pl.when(r == 0)
    def _():
        gathered[:, :eighth] = res3[...]

    mine = pl.ds(pl.multiple_of(r * piece, 8), piece)

    @pl.when(g == 0)
    def _():
        @pl.when(r != 0)
        def _():
            arrived(panel.at[:, pl.ds(0, eighth)], PANEL)

        @pl.when(r != 4)
        def _():
            arrived(panel.at[:, pl.ds(eighth, eighth)], PANEL + 1)

        turned = panel[...].T
        full[...] = dot3(turned, turned, True)
        gram_all[mine, :] = (gram_piece[...] - full[mine, :]) / float(total_rows)
        for z in range(1, zdim):
            copy(
                gram_all.at[mine, :], gram_all.at[mine, :],
                GZ, me + z * YDIM * ROW, lambda: g == 0,
            )

    @pl.when(first_y)
    def _():
        @pl.when(g > 0)
        def _():
            arrived(gram_all.at[mine, :], GZ)

        for step in range(1, YDIM):
            copy(
                gram_all.at[mine, :], gram_all.at[mine, :],
                GY, me + step * ROW, lambda: y == 0,
            )

    @pl.when(y != 0)
    def _():
        arrived(gram_all.at[mine, :], GY)

    for j in range(1, ROW):
        copy(
            gram_all.at[mine, :], gram_all.at[mine, :],
            GX + ROW - j, base + (r + j) % ROW,
        )

    @pl.when((x0 == 1) & (core == 0))
    def _():
        arrived(gathered.at[:, pl.ds(half, half)], GATHER + 1)

    @pl.when(r == 4)
    def _():
        for other, at in ((5, half), (6, quarter), (7, half + quarter)):
            arrived(gathered.at[:, pl.ds(at, quarter)], GATHER + other)

    @pl.when(r == 0)
    def _():
        for other in range(1, ROW):
            at = (other % 2) * half + (other // 2 % 2) * quarter + other // 4 * eighth
            arrived(gathered.at[:, pl.ds(at, eighth)], GATHER + other)

    head_out[...] = gathered[...]
    for j in range(1, ROW):
        rows_j = pl.ds(pl.multiple_of((r + j) % ROW * piece, 8), piece)
        arrived(gram_all.at[rows_j, :], GX + j)
    gram_out[...] = gram_all[...]

    def sent(source, sem):
        pltpu.make_async_remote_copy(
            src_ref=source,
            dst_ref=source,
            send_sem=send_sems.at[sem],
            recv_sem=recv_sems.at[0],
            device_id=(neighbour,),
            device_id_type=pl.DeviceIdType.MESH,
        ).wait_send()

    for condition, source, sem in pending:
        if condition is None:
            sent(source, sem)
        else:
            when(condition(), functools.partial(sent, source, sem))


def tree(head, pack, gram, devices, total_rows):
    b, nc = pack.shape[1], head.shape[1]
    half, quarter, eighth = nc // 2, nc // 4, nc // 8
    piece = b // ROW
    levels = (devices // ROW).bit_length() - 1
    vmem = lambda *shape: pltpu.VMEM(shape, F32)
    whole = pl.BlockSpec(memory_space=pltpu.VMEM)
    scratch = [vmem(4 + levels, b + 8, b), vmem(4, b, b)]
    scratch += [vmem(b, half), vmem(b, quarter), vmem(b, eighth)]
    for width in (half, quarter, eighth):
        scratch += [vmem(b, width)] * 4
    scratch += [
        vmem(b, eighth),
        vmem(levels, b, eighth),
        vmem(b, eighth),
        vmem(levels, b, eighth),
        vmem(b, half),
        vmem(b, quarter),
        vmem(b, eighth),
        vmem(b, nc),
        vmem(ROW, piece, b),
        vmem(piece, b),
        vmem(levels, piece, b),
        vmem(b, b),
        vmem(b, b),
        vmem(b, b),
        pltpu.SemaphoreType.DMA((112,)),
        pltpu.SemaphoreType.DMA((64,)),
    ]
    return pl.pallas_call(
        functools.partial(tree_kernel, devices, total_rows),
        out_shape=(
            jax.ShapeDtypeStruct(head.shape, F32),
            jax.ShapeDtypeStruct((b, b), F32),
        ),
        in_specs=[whole] * 3,
        out_specs=(whole, whole),
        scratch_shapes=scratch,
        compiler_params=pltpu.CompilerParams(
            collective_id=0,
            has_side_effects=True,
            vmem_limit_bytes=48 * 1024 * 1024,
        ),
        name="tree",
    )(head, pack, gram)


def body(trailing, leaf_vectors, leaf_factors, tree_vectors, tree_factors, inverse_factor):
    b = leaf_vectors.shape[1]
    devices = lax.axis_size("rows")
    total_rows = trailing.shape[0] * devices
    coeffs = across(leaf_factors, across(leaf_vectors, trailing))
    head_rows = trailing[:b] - product(leaf_vectors[:b], coeffs)
    rest_rows = trailing[b:] - product(leaf_vectors[b:], coeffs)
    panel = trailing[:, :b]
    row_id = lax.broadcasted_iota(jnp.int32, (b, b), 0)
    col_id = lax.broadcasted_iota(jnp.int32, (b, b), 1)
    turned = tree_factors.T
    diagonal = jnp.sum(jnp.where(row_id == col_id, turned, 0.0), axis=0, keepdims=True)
    pack = jnp.concatenate(
        [
            jnp.where(row_id <= col_id, tree_vectors, turned),
            jnp.broadcast_to(diagonal, (8, b)),
        ],
        axis=0,
    )
    head_rows, panel_gram = tree(head_rows, pack, across(panel, panel), devices, total_rows)
    is_first = lax.axis_index("rows") == 0
    head_basis = jnp.where(is_first, 0.0, product(head_rows[:, :b], inverse_factor))
    rest_basis = product(rest_rows[:, :b], inverse_factor)
    panel_basis = jnp.concatenate([head_basis, rest_basis], axis=0)
    updated = jnp.concatenate([head_rows, rest_rows], axis=0)
    return (updated, panel_basis, panel_gram)


def solution(mesh):
    rows = P("rows", None)
    return jax.shard_map(
        body,
        mesh=mesh,
        in_specs=(rows, rows, rows, rows, rows, P()),
        out_specs=(rows, rows, P()),
        check_vma=False,
    )
```

```python
import functools

import jax
import jax.numpy as jnp
from jax import lax
from jax.experimental import pallas as pl
from jax.experimental.pallas import tpu as pltpu
from jax.sharding import PartitionSpec as P

F32 = jnp.float32
BF16 = jnp.bfloat16
ROW = 8
YDIM = 4
MESH = pl.DeviceIdType.MESH


def halves(value):
    high = value.astype(BF16)
    low = (value - high.astype(F32)).astype(BF16)
    return high, low


def dot_pairs(left, right, transposed=False):
    dims = (((1,), (1 if transposed else 0,)), ((), ()))

    def one(a, b):
        return lax.dot_general(a, b, dims, preferred_element_type=F32)

    return one(left[0], right[0]) + (one(left[0], right[1]) + one(left[1], right[0]))


def dot3(left_side, right_side, transposed=False):
    return dot_pairs(halves(left_side), halves(right_side), transposed)


def tree_kernel(
    devices,
    total_rows,
    c_ref, lv_ref, lt_ref, tv_ref, tt_ref, inv_ref,
    upd_out, basis_out, gram_out,
    pack,
    ops,
    bt_high, bt_low,
    head,
    cur0, cur1, cur2,
    z0, z1, z2, in0, in1, in2, w0, w1, w2, wb0, wb1, wb2,
    zr, inr, wr, wbr,
    res1, res2, res3,
    gathered,
    coef, rest, rest_basis, head_rows, head_basis,
    lvt_high, lvt_low,
    gram_own, gram_in, gram_piece, gram_level, panel, gram_all,
    send_sems, recv_sems, local_sems,
):
    b = pack.shape[1]
    nc = c_ref.shape[1]
    row_count = devices // ROW
    row_levels = row_count.bit_length() - 1
    zdim = row_count // YDIM
    piece = b // ROW
    me = lax.axis_index("rows")
    r = me % ROW
    g = me // ROW
    core = r % 2
    x0 = (r // 2) % 2
    x1 = r // 4
    bits = (core, x0, x1)
    base = g * ROW
    y = g % YDIM
    neighbour = base + (r + 1) % ROW
    cur = (cur0, cur1, cur2)
    zs, ins, ws, wbs = (z0, z1, z2), (in0, in1, in2), (w0, w1, w2), (wb0, wb1, wb2)
    slot = [ops.at[i] for i in range(4 + row_levels)]
    CHUNKS = (0, 1)

    def slice_of(rank):
        return rank % 2 * 4 + rank // 2 % 2 * 2 + rank // 4

    def piece_of(rank):
        return pl.ds(pl.multiple_of(slice_of(rank) * piece, piece), piece)

    mine = piece_of(r)

    def size(level, chunk):
        return ((nc - b) // 2 if chunk else b // 2) >> level

    def own(level, chunk):
        return pl.ds((b // 2 >> level) if chunk else 0, size(level, chunk))

    def part(level, chunk, upper):
        start = (b >> level) if chunk else 0
        return pl.ds(start + (size(level, chunk) if upper else 0), size(level, chunk))

    def parent(level):
        return cur[level - 1] if level else head

    def is_low(k):
        return g % (2 << k) == 0

    def is_high(k):
        return g % (2 << k) == (1 << k)

    barrier = pltpu.get_barrier_semaphore()

    def greet(other):
        pl.semaphore_signal(barrier, inc=1, device_id=(other,), device_id_type=MESH)

    met = []

    def meet(condition, other):
        @pl.when(condition)
        def _():
            greet(other)

        met.append(condition)

    for j in range(1, ROW):
        greet(base + (r + j) % ROW)
    for k in range(row_levels):
        meet(is_low(k), me + (ROW << k))
        meet(is_high(k), me - (ROW << k))
    for z in range(1, zdim):
        if z & (z - 1):
            meet(g == 0, me + z * YDIM * ROW)
            meet(g == z * YDIM, me - z * YDIM * ROW)
    meet(y == 0, me + 3 * ROW)
    meet(y == 3, me - 3 * ROW)

    def entered():
        peers = ROW - 1
        for condition in met:
            peers = peers + condition.astype(jnp.int32)
        pl.semaphore_wait(barrier, peers)

    numbers = {}
    pending = []

    def number(*name):
        return numbers.setdefault(name, len(numbers))

    def remote(source, target, send, receive, other):
        return pltpu.make_async_remote_copy(
            src_ref=source,
            dst_ref=target,
            send_sem=send_sems.at[send],
            recv_sem=recv_sems.at[receive],
            device_id=(other,),
            device_id_type=MESH,
        )

    def copy(source, target, name, other, condition=None):
        remote(source, target, len(pending), number(*name), other).start()
        pending.append((condition, source))

    def arrived(target, name):
        remote(target, target, 0, number(*name), neighbour).wait_recv()

    row_id = lax.broadcasted_iota(jnp.int32, (b, b), 0)
    col_id = lax.broadcasted_iota(jnp.int32, (b, b), 1)

    def t_of(ref):
        return jnp.where(row_id <= col_id, ref[:b, :], 0.0)

    def vt_of(ref):
        diagonal = jnp.where(row_id == col_id, ref[b : b + 1, :], 0.0)
        return jnp.where(row_id > col_id, ref[:b, :], diagonal)

    def make_bt(index):
        high, low = halves(dot3(vt_of(slot[index]).T, t_of(slot[index])))
        bt_high[index] = high
        bt_low[index] = low

    def times_bt(value, index):
        return dot_pairs(halves(value), (bt_high[index], bt_low[index]))

    tv = tv_ref[...]
    pack[:b, :] = jnp.where(row_id <= col_id, tt_ref[...], tv.T)
    diagonal = jnp.sum(jnp.where(row_id == col_id, tv, 0.0), axis=0, keepdims=True)
    pack[b:, :] = jnp.broadcast_to(diagonal, (8, b))

    for condition, index in (
        (core == 1, 0), ((r == 2) | (r == 6), 1), (r == 4, 2), ((r == 0) & (g > 0), 3),
    ):
        @pl.when(condition)
        def _():
            ops[index] = pack[...]
            make_bt(index)

    high, low = halves(lv_ref[...].T)
    lvt_high[...] = high
    lvt_low[...] = low

    def leaf_tile(tile):
        columns = pl.ds(tile * b, b)
        inner = dot_pairs((lvt_high[...], lvt_low[...]), halves(c_ref[:, columns]))
        coeffs = dot3(lt_ref[...].T, inner)
        coef[:, columns] = coeffs
        result = c_ref[:b, columns] - dot3(lv_ref[:b, :], coeffs)
        head[columns, :] = result.T

    leaf_tile(0)
    entered()

    @pl.when(core == 1)
    def _():
        copy(pack, slot[0], ("ops", 0), me - 1, lambda: core == 1)

    @pl.when((r == 2) | (r == 6))
    def _():
        c = lambda: (r == 2) | (r == 6)
        copy(pack, slot[1], ("ops", 1), me + 1, c)
        copy(pack, slot[1], ("ops", 1), me - 2, c)

    @pl.when(r == 4)
    def _():
        for other in (5, 0, 2, 6):
            copy(pack, slot[2], ("ops", 2), base + other, lambda: r == 4)

    def send(level, chunk):
        bit, far = bits[level], 1 << level
        rows, name = own(level, chunk), ("x", level, chunk)
        target = ins[level].at[rows, :]
        low_rows, high_rows = part(level, chunk, False), part(level, chunk, True)

        @pl.when(bit == 0)
        def _():
            copy(
                parent(level).at[high_rows, :], target, name, me + far,
                lambda: bits[level] == 0,
            )

        source = zs[level].at[rows, :]

        @pl.when(bit == 1)
        def _():
            zs[level][rows, :] = times_bt(parent(level)[low_rows, :], level)
            copy(source, target, name, me - far, lambda: bits[level] == 1)

    def finish(level, chunk):
        bit = bits[level]
        rows, name = own(level, chunk), ("x", level, chunk)
        low_rows, high_rows = part(level, chunk, False), part(level, chunk, True)

        @pl.when(bit == 0)
        def _():
            value = parent(level)[low_rows, :]
            update = dot3(value, t_of(slot[level]))
            arrived(ins[level].at[rows, :], name)
            update = update + ins[level][rows, :]
            cur[level][rows, :] = value - update
            ws[level][rows, :] = update

        @pl.when(bit == 1)
        def _():
            update = times_bt(parent(level)[high_rows, :], level)
            arrived(ins[level].at[rows, :], name)
            value = ins[level][rows, :]
            update = update + dot3(value, t_of(slot[level]))
            cur[level][rows, :] = value - update
            ws[level][rows, :] = update

    def give_back(level, chunk):
        rows = own(level, chunk)

        @pl.when(bits[level] == 0)
        def _():
            copy(
                ws[level].at[rows, :], wbs[level].at[rows, :], ("w", level, chunk),
                me + (1 << level), lambda: bits[level] == 0,
            )

    def residual(level, result):
        @pl.when(bits[level] == 1)
        def _():
            vt = halves(vt_of(slot[level]))
            for chunk in CHUNKS:
                rows = own(level, chunk)
                low_rows, high_rows = part(level, chunk, False), part(level, chunk, True)
                result[high_rows, :] = parent(level)[high_rows, :] - dot_pairs(
                    halves(ws[level][rows, :]), vt
                )
                arrived(wbs[level].at[rows, :], ("w", level, chunk))
                result[low_rows, :] = parent(level)[low_rows, :] - dot_pairs(
                    halves(wbs[level][rows, :]), vt
                )

    def place(level, rank, chunk):
        shape = size(level - 1, chunk)
        start = b if chunk else 0
        for bit in range(level):
            start += (rank >> bit & 1) * size(bit, chunk)
        return pl.ds(start, shape)

    def buffer_rows(level, chunk):
        return pl.ds((b >> level) if chunk else 0, size(level - 1, chunk))

    def gather(level, result, rank, into):
        for chunk in CHUNKS:
            if rank == into:
                gathered[place(level, rank, chunk), :] = result[buffer_rows(level, chunk), :]
            else:
                copy(
                    result.at[buffer_rows(level, chunk), :],
                    gathered.at[place(level, rank, chunk), :],
                    ("gather", rank % 4 if level == 1 else rank, chunk),
                    base + into, lambda: r == rank,
                )

    def gather_wait(level, rank):
        for chunk in CHUNKS:
            arrived(
                gathered.at[place(level, rank, chunk), :],
                ("gather", rank % 4 if level == 1 else rank, chunk),
            )

    send(0, 0)
    for tile in range(1, nc // b):
        leaf_tile(tile)
    send(0, 1)

    @pl.when(core == 0)
    def _():
        arrived(slot[0], ("ops", 0))

    finish(0, 0)

    @pl.when((r == 3) | (r == 7))
    def _():
        arrived(slot[1], ("ops", 1))
        make_bt(1)

    send(1, 0)

    @pl.when((r == 0) & (g > 0))
    def _():
        for other in (1, 2, 6, 4):
            copy(pack, slot[3], ("ops", 3), base + other, lambda: (r == 0) & (g > 0))

    finish(0, 1)
    send(1, 1)

    @pl.when((r == 0) | (r == 4))
    def _():
        arrived(slot[1], ("ops", 1))
        copy(slot[1], slot[1], ("ops", 1), me + 1, lambda: (r == 0) | (r == 4))

    columns = c_ref[:, :b]
    gram_own[...] = dot3(columns.T, columns)
    for j in range(1, ROW):
        other = (r + j) % ROW
        copy(
            gram_own.at[piece_of(other), :], gram_in.at[ROW - j],
            ("gram", ROW - j), base + other,
        )
    give_back(0, 0)
    give_back(0, 1)

    @pl.when((r == 1) | (r == 5))
    def _():
        arrived(slot[1], ("ops", 1))

    @pl.when((r == 0) | (r == 2) | (r == 6))
    def _():
        arrived(slot[2], ("ops", 2))
        copy(slot[2], slot[2], ("ops", 2), me + 1, lambda: (r == 0) | (r == 2) | (r == 6))

    finish(1, 0)

    @pl.when(core == 1)
    def _():
        arrived(slot[2], ("ops", 2))

    @pl.when((x1 == 1) & (r > 4))
    def _():
        make_bt(2)

    send(2, 0)
    finish(1, 1)
    send(2, 1)
    give_back(1, 0)
    give_back(1, 1)

    @pl.when((g > 0) & (core == 0) & (r > 0))
    def _():
        arrived(slot[3], ("ops", 3))
        copy(
            slot[3], slot[3], ("ops", 3), me + 1,
            lambda: (g > 0) & (core == 0) & (r > 0),
        )

    for k in range(row_levels):
        @pl.when(is_high(k) & (core == 0))
        def _():
            copy(
                slot[3], slot[4 + k], ("ops", 4 + k), me - (ROW << k),
                functools.partial(lambda k: is_high(k) & (core == 0), k),
            )

    def rest_tile(tile):
        columns = pl.ds(tile * b, b)
        rest[:, columns] = c_ref[b:, columns] - dot3(lv_ref[b:, :], coef[:, columns])

    rest_tile(0)
    rest_basis[...] = dot3(rest[:, :b], inv_ref[...])
    for tile in range(1, nc // b):
        rest_tile(tile)
    local = [
        pltpu.make_async_copy(rest, upd_out.at[pl.ds(b, b), :], local_sems.at[0]),
        pltpu.make_async_copy(rest_basis, basis_out.at[pl.ds(b, b), :], local_sems.at[1]),
    ]
    for made in local:
        made.start()

    @pl.when((g > 0) & (core == 1))
    def _():
        arrived(slot[3], ("ops", 3))

    @pl.when((g > 0) & (r > 0))
    def _():
        make_bt(3)

    def send_row(k, chunk):
        rows = own(2, chunk)
        source = zr.at[rows, :]

        @pl.when(is_high(k))
        def _():
            zr[rows, :] = times_bt(cur2[rows, :], 3)
            copy(
                source, inr.at[k, rows, :], ("z", k, chunk), me - (ROW << k),
                functools.partial(is_high, k),
            )

    def finish_row(k, chunk):
        rows = own(2, chunk)
        source = wr.at[k, rows, :]

        @pl.when(is_low(k))
        def _():
            value = cur2[rows, :]
            update = dot3(value, t_of(slot[4 + k]))
            arrived(inr.at[k, rows, :], ("z", k, chunk))
            update = update + inr[k, rows, :]
            cur2[rows, :] = value - update
            wr[k, rows, :] = update
            copy(
                source, wbr.at[rows, :], ("wr", chunk), me + (ROW << k),
                functools.partial(is_low, k),
            )

    def row_operators(k):
        @pl.when(is_low(k) & (core == 0))
        def _():
            arrived(slot[4 + k], ("ops", 4 + k))
            copy(
                slot[4 + k], slot[4 + k], ("ops", 4 + k), me + 1,
                functools.partial(lambda k: is_low(k) & (core == 0), k),
            )

        @pl.when(is_low(k) & (core == 1))
        def _():
            arrived(slot[4 + k], ("ops", 4 + k))

    finish(2, 0)
    send_row(0, 0)
    finish(2, 1)
    send_row(0, 1)
    give_back(2, 0)
    give_back(2, 1)

    residual(0, gathered)

    for j in range(1, ROW):
        arrived(gram_in.at[ROW - j], ("gram", ROW - j))
    total = gram_own[mine, :]
    for j in range(1, ROW):
        total = total + gram_in[j]
    gram_piece[...] = total

    for k in range(row_levels):
        row_operators(k)
        finish_row(k, 0)
        if k + 1 < row_levels:
            send_row(k + 1, 0)
        else:
            @pl.when(g == 0)
            def _():
                panel[mine, :] = cur2[own(2, 0), :]
                for j in range(1, ROW):
                    copy(
                        cur2.at[own(2, 0), :], panel.at[mine, :],
                        ("panel", ROW - j), base + (r + j) % ROW, lambda: g == 0,
                    )

        finish_row(k, 1)
        if k + 1 < row_levels:
            send_row(k + 1, 1)

        @pl.when(is_high(k))
        def _():
            copy(
                gram_piece, gram_level.at[k], ("level", k), me - (ROW << k),
                functools.partial(is_high, k),
            )

        @pl.when(is_low(k))
        def _():
            arrived(gram_level.at[k], ("level", k))
            gram_piece[...] = gram_piece[...] + gram_level[k]

        if k == 0:
            residual(1, res1)
            for rank, into in ((2, 2), (3, 2), (6, 6), (7, 6)):
                @pl.when(r == rank)
                def _():
                    gather(1, res1, rank, into)
        if k == 1 or row_levels == 1:
            residual(2, res2)
            for rank in range(4, ROW):
                @pl.when(r == rank)
                def _():
                    gather(2, res2, rank, 4)

    @pl.when(g > 0)
    def _():
        vt = halves(vt_of(slot[3]))
        for chunk in CHUNKS:
            rows = own(2, chunk)
            arrived(wbr.at[rows, :], ("wr", chunk))
            res3[rows, :] = cur2[rows, :] - dot_pairs(halves(wbr[rows, :]), vt)

    @pl.when(g == 0)
    def _():
        res3[...] = cur2[...]

    for rank in range(ROW):
        @pl.when(r == rank)
        def _():
            gather(3, res3, rank, 0)

    @pl.when(g == 0)
    def _():
        for j in range(1, ROW):
            arrived(panel.at[piece_of((r + j) % ROW), :], ("panel", j))
        square = dot3(panel[mine, :], panel[...], True)
        gram_all[mine, :] = (gram_piece[...] - square) / float(total_rows)
        for z in range(1, zdim):
            copy(
                gram_all.at[mine, :], gram_all.at[mine, :], ("gz",),
                me + z * YDIM * ROW, lambda: g == 0,
            )

    @pl.when(y == 0)
    def _():
        @pl.when(g > 0)
        def _():
            arrived(gram_all.at[mine, :], ("gz",))

        for step in range(1, YDIM):
            copy(
                gram_all.at[mine, :], gram_all.at[mine, :], ("gy",),
                me + step * ROW, lambda: y == 0,
            )

    @pl.when(y != 0)
    def _():
        arrived(gram_all.at[mine, :], ("gy",))

    for j in range(1, ROW):
        copy(
            gram_all.at[mine, :], gram_all.at[mine, :], ("gx", ROW - j),
            base + (r + j) % ROW,
        )

    @pl.when((x0 == 1) & (core == 0))
    def _():
        gather_wait(1, 3)

    @pl.when(r == 4)
    def _():
        for rank in (5, 6, 7):
            gather_wait(2, rank)

    @pl.when(r == 0)
    def _():
        for rank in range(1, ROW):
            gather_wait(3, rank)

    head_rows[...] = gathered[...].T
    head_basis[...] = jnp.where(me == 0, 0.0, dot3(head_rows[:, :b], inv_ref[...]))
    local += [
        pltpu.make_async_copy(head_rows, upd_out.at[pl.ds(0, b), :], local_sems.at[2]),
        pltpu.make_async_copy(head_basis, basis_out.at[pl.ds(0, b), :], local_sems.at[3]),
    ]
    for made in local[2:]:
        made.start()
    for j in range(1, ROW):
        arrived(gram_all.at[piece_of((r + j) % ROW), :], ("gx", j))
    local.append(pltpu.make_async_copy(gram_all, gram_out, local_sems.at[4]))
    local[-1].start()

    for index, (condition, source) in enumerate(pending):
        made = functools.partial(
            lambda source, index: remote(source, source, index, 0, neighbour).wait_send(),
            source, index,
        )
        if condition is None:
            made()
        else:
            @pl.when(condition())
            def _():
                made()
    for made in local:
        made.wait()


def body(trailing, leaf_vectors, leaf_factors, tree_vectors, tree_factors, inverse_factor):
    b, nc = leaf_vectors.shape[1], trailing.shape[1]
    devices = lax.axis_size("rows")
    total_rows = trailing.shape[0] * devices
    levels = (devices // ROW).bit_length() - 1
    piece = b // ROW

    def vmem(*shape, dtype=F32):
        return pltpu.VMEM(shape, dtype)

    per_level = [vmem(nc >> level, b) for level in (1, 2, 3)]
    scratch = [
        vmem(b + 8, b),
        vmem(4 + levels, b + 8, b),
        vmem(4, b, b, dtype=BF16),
        vmem(4, b, b, dtype=BF16),
        vmem(nc, b),
        *per_level,
        *per_level, *per_level, *per_level, *per_level,
        vmem(nc // 8, b), vmem(levels, nc // 8, b), vmem(levels, nc // 8, b),
        vmem(nc // 8, b),
        *per_level,
        vmem(nc, b),
        vmem(b, nc), vmem(b, nc), vmem(b, b), vmem(b, nc), vmem(b, b),
        vmem(b, 2 * b, dtype=BF16), vmem(b, 2 * b, dtype=BF16),
        vmem(b, b), vmem(ROW, piece, b), vmem(piece, b), vmem(levels, piece, b),
        vmem(b, b), vmem(b, b),
        pltpu.SemaphoreType.DMA((200,)),
        pltpu.SemaphoreType.DMA((96,)),
        pltpu.SemaphoreType.DMA((5,)),
    ]
    return pl.pallas_call(
        functools.partial(tree_kernel, devices, total_rows),
        out_shape=(
            jax.ShapeDtypeStruct(trailing.shape, F32),
            jax.ShapeDtypeStruct(leaf_vectors.shape, F32),
            jax.ShapeDtypeStruct((b, b), F32),
        ),
        in_specs=[pl.BlockSpec(memory_space=pltpu.VMEM)] * 6,
        out_specs=[pl.BlockSpec(memory_space=pl.ANY)] * 3,
        scratch_shapes=scratch,
        compiler_params=pltpu.CompilerParams(
            collective_id=0,
            has_side_effects=True,
            vmem_limit_bytes=48 * 1024 * 1024,
        ),
        name="tree",
    )(trailing, leaf_vectors, leaf_factors, tree_vectors, tree_factors, inverse_factor)


def solution(mesh):
    rows = P("rows", None)
    return jax.shard_map(
        body,
        mesh=mesh,
        in_specs=(rows, rows, rows, rows, rows, P()),
        out_specs=(rows, rows, P()),
        check_vma=False,
    )
```

```python
import functools

import jax
import jax.numpy as jnp
from jax import lax
from jax.experimental import pallas as pl
from jax.experimental.pallas import tpu as pltpu
from jax.sharding import PartitionSpec as P

F32 = jnp.float32
BF16 = jnp.bfloat16
ROW = 8
YDIM = 4
MESH = pl.DeviceIdType.MESH
RECEIVES = 56


def halves(value):
    high = value.astype(BF16)
    low = (value - high.astype(F32)).astype(BF16)
    return high, low


def dot_pairs(left, right, transposed=False):
    dims = (((1,), (1 if transposed else 0,)), ((), ()))

    def one(a, b):
        return lax.dot_general(a, b, dims, preferred_element_type=F32)

    return one(left[0], right[0]) + (one(left[0], right[1]) + one(left[1], right[0]))


def dot3(left_side, right_side, transposed=False):
    return dot_pairs(halves(left_side), halves(right_side), transposed)


def tree_kernel(
    devices,
    total_rows,
    c_hbm, lv_hbm, lt_hbm, tv_hbm, tt_hbm, inv_hbm,
    upd_out, basis_out, gram_out,
    c_ref, lv_ref, lt_ref, tv_ref, tt_ref, inv_ref,
    pack,
    folded,
    slot0, slot1, slot2, slot3,
    fold,
    row_fold,
    t_high, t_low,
    bt_high, bt_low,
    head,
    cur0, cur1, cur2,
    z0, z1, z2, in0, in1, in2, w0, w1, w2, wb0, wb1, wb2,
    zr, inr, wr, wbr,
    res1, res2, res3,
    gathered,
    coef, rest, rest_basis, head_rows, head_basis,
    lvt_high, lvt_low,
    gram_own, gram_in, gram_piece, gram_level, panel, gram_all,
    send_sem, recv_sems, local_sems,
):
    b = pack.shape[1]
    hb = b // 2
    nc = c_ref.shape[1]
    row_count = devices // ROW
    row_levels = row_count.bit_length() - 1
    zdim = row_count // YDIM
    piece = b // ROW
    me = lax.axis_index("rows")
    r = me % ROW
    g = me // ROW
    core = r % 2
    x0 = (r // 2) % 2
    x1 = r // 4
    bits = (core, x0, x1)
    base = g * ROW
    y = g % YDIM
    neighbour = base + (r + 1) % ROW
    cur = (cur0, cur1, cur2)
    zs, ins, ws, wbs = (z0, z1, z2), (in0, in1, in2), (w0, w1, w2), (wb0, wb1, wb2)
    slot = (slot0, slot1, slot2, slot3)
    folds = [fold.at[i] for i in range(3 + row_levels)]
    CHUNKS = (0, 1)
    eighth_b = (nc - b) // 8
    ROW_CHUNKS = (
        pl.ds(0, piece),
        pl.ds(piece, eighth_b // 2),
        pl.ds(piece + eighth_b // 2, eighth_b // 2),
    )

    def slice_of(rank):
        return rank % 2 * 4 + rank // 2 % 2 * 2 + rank // 4

    def piece_of(rank):
        return pl.ds(pl.multiple_of(slice_of(rank) * piece, piece), piece)

    mine = piece_of(r)

    def size(level, chunk):
        return ((nc - b) // 2 if chunk else b // 2) >> level

    def own(level, chunk):
        return pl.ds((b // 2 >> level) if chunk else 0, size(level, chunk))

    def part(level, chunk, upper):
        start = (b >> level) if chunk else 0
        return pl.ds(start + (size(level, chunk) if upper else 0), size(level, chunk))

    def parent(level):
        return cur[level - 1] if level else head

    def is_low(k):
        return g % (2 << k) == 0

    def is_high(k):
        return g % (2 << k) == (1 << k)

    loads = {}
    for name, source, target in (
        ("tv", tv_hbm, tv_ref),
        ("tt", tt_hbm, tt_ref),
        ("lv", lv_hbm, lv_ref),
        ("c0", c_hbm.at[:, pl.ds(0, b)], c_ref.at[:, pl.ds(0, b)]),
        ("lt", lt_hbm, lt_ref),
        ("c1", c_hbm.at[:, pl.ds(b, nc - b)], c_ref.at[:, pl.ds(b, nc - b)]),
        ("inv", inv_hbm, inv_ref),
    ):
        loads[name] = pltpu.make_async_copy(source, target, local_sems.at[len(loads)])
        loads[name].start()

    barrier = pltpu.get_barrier_semaphore()

    def greet(other):
        pl.semaphore_signal(barrier, inc=1, device_id=(other,), device_id_type=MESH)

    met = []

    def meet(condition, other):
        @pl.when(condition)
        def _():
            greet(other)

        met.append(condition)

    for j in range(1, ROW):
        greet(base + (r + j) % ROW)
    for k in range(row_levels):
        meet(is_low(k), me + (ROW << k))
        meet(is_high(k), me - (ROW << k))
    for z in range(1, zdim):
        if z & (z - 1):
            meet(g == 0, me + z * YDIM * ROW)
            meet(g == z * YDIM, me - z * YDIM * ROW)
    meet(y == 0, me + 3 * ROW)
    meet(y == 3, me - 3 * ROW)

    def entered():
        peers = ROW - 1
        for condition in met:
            peers = peers + condition.astype(jnp.int32)
        pl.semaphore_wait(barrier, peers)

    numbers = {}
    pending = []

    def number(*name):
        return numbers.setdefault(name, len(numbers))

    def remote(source, target, receive, other):
        return pltpu.make_async_remote_copy(
            src_ref=source,
            dst_ref=target,
            send_sem=send_sem,
            recv_sem=recv_sems.at[receive],
            device_id=(other,),
            device_id_type=MESH,
        )

    def copy(source, target, name, other, condition=None):
        remote(source, target, number(*name), other).start()
        pending.append((condition, source))

    def arrived(target, name):
        remote(target, target, number(*name), neighbour).wait_recv()

    row_id = lax.broadcasted_iota(jnp.int32, (b, b), 0)
    col_id = lax.broadcasted_iota(jnp.int32, (b, b), 1)
    row_half = lax.broadcasted_iota(jnp.int32, (hb, hb), 0)
    col_half = lax.broadcasted_iota(jnp.int32, (hb, hb), 1)

    def t_of(ref):
        return jnp.where(row_id <= col_id, ref[:b, :], 0.0)

    def vt_of(ref):
        diagonal = jnp.where(row_id == col_id, ref[b : b + 1, :], 0.0)
        return jnp.where(row_id > col_id, ref[:b, :], diagonal)

    def make_fold(target, t):
        last = t[hb:, hb:]
        target[:hb, :hb] = jnp.where(row_half <= col_half, t[:hb, :hb], last.T)
        target[:hb, hb:] = t[:hb, hb:]
        diagonal = jnp.sum(
            jnp.where(row_half == col_half, last, 0.0), axis=0, keepdims=True
        )
        target[hb:, :hb] = jnp.broadcast_to(diagonal, (8, hb))
        target[hb:, hb:] = jnp.zeros((8, hb), F32)

    def store_t(index, value, rows, columns):
        high, low = halves(value)
        t_high[index, rows, columns] = high
        t_low[index, rows, columns] = low

    FIRST, LAST = pl.ds(0, hb), pl.ds(hb, hb)

    def t_from_fold(index):
        first = fold[index, :hb, :hb]
        store_t(index, jnp.where(row_half <= col_half, first, 0.0), FIRST, FIRST)
        store_t(index, fold[index, :hb, hb:], FIRST, LAST)
        store_t(index, jnp.zeros((hb, hb), F32), LAST, FIRST)
        diagonal = jnp.where(row_half == col_half, fold[index, hb : hb + 1, :hb], 0.0)
        last = jnp.where(row_half < col_half, first.T, diagonal)
        store_t(index, last, LAST, LAST)

    def t_from_slot(index):
        store_t(index, t_of(slot[index]), pl.ds(0, b), pl.ds(0, b))

    def make_bt(index):
        high, low = halves(dot3(vt_of(slot[index]).T, t_of(slot[index])))
        bt_high[index] = high
        bt_low[index] = low

    def times_bt(value, index):
        return dot_pairs(halves(value), (bt_high[index], bt_low[index]))

    def times_t(value, index):
        return dot_pairs(halves(value), (t_high[index], t_low[index]))

    loads["tv"].wait()
    loads["tt"].wait()
    tv = tv_ref[...]
    tt = tt_ref[...]
    pack[:b, :] = jnp.where(row_id <= col_id, tt, tv.T)
    diagonal = jnp.sum(jnp.where(row_id == col_id, tv, 0.0), axis=0, keepdims=True)
    pack[b:, :] = jnp.broadcast_to(diagonal, (8, b))
    make_fold(folded, tt)

    for condition, index in (
        (core == 1, 0), ((r == 2) | (r == 6), 1), (r == 4, 2), ((r == 0) & (g > 0), 3),
    ):
        @pl.when(condition)
        def _():
            slot[index][...] = pack[...]
            make_bt(index)
            if index < 3:
                t_from_slot(index)

    loads["lv"].wait()
    high, low = halves(lv_ref[...].T)
    lvt_high[...] = high
    lvt_low[...] = low

    def leaf_tile(tile):
        columns = pl.ds(tile * b, b)
        inner = dot_pairs((lvt_high[...], lvt_low[...]), halves(c_ref[:, columns]))
        coeffs = dot3(lt_ref[...].T, inner)
        coef[:, columns] = coeffs
        result = c_ref[:b, columns] - dot3(lv_ref[:b, :], coeffs)
        head[columns, :] = result.T

    loads["c0"].wait()
    loads["lt"].wait()
    leaf_tile(0)
    entered()

    @pl.when(core == 1)
    def _():
        copy(folded, folds[0], ("fold", 0), me - 1, lambda: core == 1)

    @pl.when((r == 2) | (r == 6))
    def _():
        c = lambda: (r == 2) | (r == 6)
        copy(pack, slot1, ("slot", 1), me + 1, c)
        copy(folded, folds[1], ("fold", 1), me - 2, c)

    @pl.when(r == 4)
    def _():
        copy(pack, slot2, ("slot", 2), base + 5, lambda: r == 4)
        copy(folded, folds[2], ("fold", 2), base + 2, lambda: r == 4)
        copy(pack, slot2, ("slot", 2), base + 6, lambda: r == 4)

    @pl.when((r == 0) & (g > 0))
    def _():
        for other in (1, 2, 6):
            copy(pack, slot3, ("slot", 3), base + other, lambda: (r == 0) & (g > 0))

    def send(level, chunk):
        bit, far = bits[level], 1 << level
        rows, name = own(level, chunk), ("x", level, chunk)
        target = ins[level].at[rows, :]
        low_rows, high_rows = part(level, chunk, False), part(level, chunk, True)

        @pl.when(bit == 0)
        def _():
            copy(
                parent(level).at[high_rows, :], target, name, me + far,
                lambda: bits[level] == 0,
            )

        source = zs[level].at[rows, :]

        @pl.when(bit == 1)
        def _():
            zs[level][rows, :] = times_bt(parent(level)[low_rows, :], level)
            copy(source, target, name, me - far, lambda: bits[level] == 1)

    def finish(level, chunk):
        bit = bits[level]
        rows, name = own(level, chunk), ("x", level, chunk)
        low_rows, high_rows = part(level, chunk, False), part(level, chunk, True)

        @pl.when(bit == 0)
        def _():
            value = parent(level)[low_rows, :]
            update = times_t(value, level)
            arrived(ins[level].at[rows, :], name)
            update = update + ins[level][rows, :]
            cur[level][rows, :] = value - update
            ws[level][rows, :] = update

        @pl.when(bit == 1)
        def _():
            update = times_bt(parent(level)[high_rows, :], level)
            arrived(ins[level].at[rows, :], name)
            value = ins[level][rows, :]
            update = update + times_t(value, level)
            cur[level][rows, :] = value - update
            ws[level][rows, :] = update

    def give_back(level, chunk):
        rows = own(level, chunk)

        @pl.when(bits[level] == 0)
        def _():
            copy(
                ws[level].at[rows, :], wbs[level].at[rows, :], ("w", level, chunk),
                me + (1 << level), lambda: bits[level] == 0,
            )

    def residual(level, result):
        @pl.when(bits[level] == 1)
        def _():
            vt = halves(vt_of(slot[level]))
            for chunk in CHUNKS:
                rows = own(level, chunk)
                low_rows, high_rows = part(level, chunk, False), part(level, chunk, True)
                result[high_rows, :] = parent(level)[high_rows, :] - dot_pairs(
                    halves(ws[level][rows, :]), vt
                )
                arrived(wbs[level].at[rows, :], ("w", level, chunk))
                result[low_rows, :] = parent(level)[low_rows, :] - dot_pairs(
                    halves(wbs[level][rows, :]), vt
                )

    def place(level, rank, chunk):
        start = b if chunk else 0
        for bit in range(level):
            start += (rank >> bit & 1) * size(bit, chunk)
        return pl.ds(start, size(level - 1, chunk))

    def buffer_rows(level, chunk):
        return pl.ds((b >> level) if chunk else 0, size(level - 1, chunk))

    def gather(level, result, rank, into, chunks, condition):
        for chunk in chunks:
            if rank == into:
                gathered[place(level, rank, chunk), :] = result[buffer_rows(level, chunk), :]
            else:
                copy(
                    result.at[buffer_rows(level, chunk), :],
                    gathered.at[place(level, rank, chunk), :],
                    ("gather",), base + into, condition,
                )

    send(0, 0)
    loads["c1"].wait()
    for tile in range(1, nc // b):
        leaf_tile(tile)
    send(0, 1)

    @pl.when(core == 0)
    def _():
        arrived(folds[0], ("fold", 0))
        t_from_fold(0)

    finish(0, 0)

    @pl.when((r == 3) | (r == 7))
    def _():
        arrived(slot1, ("slot", 1))
        make_bt(1)
        t_from_slot(1)

    send(1, 0)

    @pl.when(r == 4)
    def _():
        copy(folded, folds[2], ("fold", 2), base, lambda: r == 4)

    finish(0, 1)
    send(1, 1)

    @pl.when((r == 0) & (g > 0))
    def _():
        copy(pack, slot3, ("slot", 3), base + 4, lambda: (r == 0) & (g > 0))

    @pl.when((r == 0) | (r == 4))
    def _():
        arrived(folds[1], ("fold", 1))
        copy(folds[1], folds[1], ("fold", 1), me + 1, lambda: (r == 0) | (r == 4))
        t_from_fold(1)

    give_back(0, 0)
    give_back(0, 1)

    @pl.when(r == 6)
    def _():
        arrived(slot2, ("slot", 2))
        copy(slot2, slot2, ("slot", 2), me + 1, lambda: r == 6)
        make_bt(2)
        t_from_slot(2)

    @pl.when((r == 5) | (r == 7))
    def _():
        arrived(slot2, ("slot", 2))
        make_bt(2)
        t_from_slot(2)

    @pl.when((r == 1) | (r == 5))
    def _():
        arrived(folds[1], ("fold", 1))
        t_from_fold(1)

    finish(1, 0)
    send(2, 0)

    @pl.when((r == 0) | (r == 2))
    def _():
        arrived(folds[2], ("fold", 2))
        copy(folds[2], folds[2], ("fold", 2), me + 1, lambda: (r == 0) | (r == 2))
        t_from_fold(2)

    finish(1, 1)
    send(2, 1)

    @pl.when((g > 0) & (core == 0))
    def _():
        @pl.when(r > 0)
        def _():
            arrived(slot3, ("slot", 3))
            copy(
                slot3, slot3, ("slot", 3), me + 1,
                lambda: (g > 0) & (core == 0) & (r > 0),
            )

        make_fold(row_fold, t_of(slot3))
        for k in range(row_levels):
            @pl.when(is_high(k))
            def _():
                copy(
                    row_fold, folds[3 + k], ("fold", 3 + k), me - (ROW << k),
                    functools.partial(lambda k: is_high(k) & (core == 0), k),
                )

    give_back(1, 0)
    give_back(1, 1)

    @pl.when((r == 1) | (r == 3))
    def _():
        arrived(folds[2], ("fold", 2))
        t_from_fold(2)

    def rest_tile(tile):
        columns = pl.ds(tile * b, b)
        rest[:, columns] = c_ref[b:, columns] - dot3(lv_ref[b:, :], coef[:, columns])

    rest_tile(0)
    loads["inv"].wait()
    rest_basis[...] = dot3(rest[:, :b], inv_ref[...])
    for tile in range(1, nc // b):
        rest_tile(tile)
    local = [
        pltpu.make_async_copy(rest, upd_out.at[pl.ds(b, b), :], local_sems.at[7]),
        pltpu.make_async_copy(rest_basis, basis_out.at[pl.ds(b, b), :], local_sems.at[8]),
    ]
    for made in local:
        made.start()

    @pl.when((g > 0) & (core == 1))
    def _():
        arrived(slot3, ("slot", 3))

    @pl.when((g > 0) & (r > 0))
    def _():
        make_bt(3)

    def send_row(k, chunk):
        rows = ROW_CHUNKS[chunk]
        source = zr.at[rows, :]

        @pl.when(is_high(k))
        def _():
            zr[rows, :] = times_bt(cur2[rows, :], 3)
            copy(
                source, inr.at[k, rows, :], ("z", k, chunk), me - (ROW << k),
                functools.partial(is_high, k),
            )

    def finish_row(k, chunk):
        rows = ROW_CHUNKS[chunk]
        source = wr.at[k, rows, :]

        @pl.when(is_low(k))
        def _():
            value = cur2[rows, :]
            update = times_t(value, 3 + k)
            arrived(inr.at[k, rows, :], ("z", k, chunk))
            update = update + inr[k, rows, :]
            cur2[rows, :] = value - update
            wr[k, rows, :] = update
            copy(
                source, wbr.at[rows, :], ("wr", chunk), me + (ROW << k),
                functools.partial(is_low, k),
            )

    def row_operators(k):
        @pl.when(is_low(k))
        def _():
            arrived(folds[3 + k], ("fold", 3 + k))

            @pl.when(core == 0)
            def _():
                copy(
                    folds[3 + k], folds[3 + k], ("fold", 3 + k), me + 1,
                    functools.partial(lambda k: is_low(k) & (core == 0), k),
                )

            t_from_fold(3 + k)

    finish(2, 0)
    send_row(0, 0)
    finish(2, 1)
    send_row(0, 1)
    send_row(0, 2)
    give_back(2, 0)
    give_back(2, 1)

    columns = c_ref[:, :b]
    gram_own[...] = dot3(columns.T, columns)
    for j in range(1, ROW):
        other = (r + j) % ROW
        copy(
            gram_own.at[piece_of(other), :], gram_in.at[ROW - j - 1],
            ("gram",), base + other,
        )

    def chain(k):
        @pl.when(is_high(k))
        def _():
            copy(
                gram_piece, gram_level.at[k], ("level", k), me - (ROW << k),
                functools.partial(is_high, k),
            )

        @pl.when(is_low(k))
        def _():
            arrived(gram_level.at[k], ("level", k))
            gram_piece[...] = gram_piece[...] + gram_level[k]

    def gram_sum():
        arrived(gram_in, ("gram",))
        total = gram_own[mine, :]
        for j in range(ROW - 1):
            total = total + gram_in[j]
        gram_piece[...] = total

    def panel_out():
        @pl.when(g == 0)
        def _():
            panel[mine, :] = cur2[ROW_CHUNKS[0], :]
            for j in range(1, ROW):
                copy(
                    cur2.at[ROW_CHUNKS[0], :], panel.at[mine, :],
                    ("panel",), base + (r + j) % ROW, lambda: g == 0,
                )

    def gram_out_z():
        @pl.when(g == 0)
        def _():
            arrived(panel.at[pl.ds(0, b - piece), :], ("panel",))
            square = dot3(panel[mine, :], panel[...], True)
            gram_all[mine, :] = (gram_piece[...] - square) / float(total_rows)
            for z in range(1, zdim):
                copy(
                    gram_all.at[mine, :], gram_all.at[mine, :], ("gz",),
                    me + z * YDIM * ROW, lambda: g == 0,
                )

    events = []
    for k in range(row_levels):
        events += [(2.9 * k, k, 0), (2.0 + 4.2 * k, k, 1), (2.9 + 4.2 * k, k, 2)]
    done = set()
    last = row_levels - 1
    for _, k, chunk in sorted(events):
        if chunk == 0:
            row_operators(k)
        finish_row(k, chunk)
        if k < last:
            send_row(k + 1, chunk)
        done.add((k, chunk))
        if (k, chunk) == (last, 0):
            panel_out()
        if (k, chunk) == (0, 2):
            residual(0, gathered)
            residual(1, res1)
            for rank, into in ((2, 2), (3, 2), (6, 6), (7, 6)):
                @pl.when(r == rank)
                def _():
                    gather(1, res1, rank, into, CHUNKS, functools.partial(lambda o: r == o, rank))
        if (k, chunk) == (1, 2):
            residual(2, res2)
            for rank in range(4, ROW):
                @pl.when(r == rank)
                def _():
                    gather(2, res2, rank, 4, CHUNKS, functools.partial(lambda o: r == o, rank))
            gram_sum()
            chain(0)
            chain(1)
        if (k, chunk) == (2, 2):
            chain(2)
            if last > 2:
                chain(3)
        if last > 3 and (k, chunk) == (4, 0):
            chain(4)
        if last > 3 and (k, chunk) == (last - 1, 2):
            gram_out_z()
    if last <= 3:
        gram_out_z()

    def row_result(condition):
        @pl.when(condition())
        def _():
            vt = halves(vt_of(slot3))
            for chunk, rows in enumerate(ROW_CHUNKS):
                arrived(wbr.at[rows, :], ("wr", chunk))
                res3[rows, :] = cur2[rows, :] - dot_pairs(halves(wbr[rows, :]), vt)
                if chunk == 1:
                    continue
                for rank in range(ROW):
                    @pl.when(r == rank)
                    def _():
                        gather(
                            3, res3, rank, 0, (min(chunk, 1),),
                            functools.partial(lambda o: condition() & (r == o), rank),
                        )

    half_way = row_count // 2
    row_result(lambda: (g > 0) & (g != half_way))

    @pl.when(g == 0)
    def _():
        for rank in range(ROW):
            @pl.when(r == rank)
            def _():
                gather(
                    3, cur2, rank, 0, CHUNKS,
                    functools.partial(lambda o: (g == 0) & (r == o), rank),
                )

    @pl.when(y == 0)
    def _():
        @pl.when(g > 0)
        def _():
            arrived(gram_all.at[mine, :], ("gz",))

        for step in range(1, YDIM):
            copy(
                gram_all.at[mine, :], gram_all.at[mine, :], ("gy",),
                me + step * ROW, lambda: y == 0,
            )

    row_result(lambda: g == half_way)

    @pl.when(y != 0)
    def _():
        arrived(gram_all.at[mine, :], ("gy",))

    for j in range(1, ROW):
        copy(
            gram_all.at[mine, :], gram_all.at[mine, :], ("gx",),
            base + (r + j) % ROW,
        )

    @pl.when((r == 2) | (r == 6))
    def _():
        arrived(gathered.at[pl.ds(0, nc // 2), :], ("gather",))

    @pl.when(r == 4)
    def _():
        arrived(gathered.at[pl.ds(0, 3 * nc // 4), :], ("gather",))

    @pl.when(r == 0)
    def _():
        arrived(gathered.at[pl.ds(0, 7 * nc // 8), :], ("gather",))

    head_rows[...] = gathered[...].T
    head_basis[...] = jnp.where(me == 0, 0.0, dot3(head_rows[:, :b], inv_ref[...]))
    local += [
        pltpu.make_async_copy(head_rows, upd_out.at[pl.ds(0, b), :], local_sems.at[9]),
        pltpu.make_async_copy(head_basis, basis_out.at[pl.ds(0, b), :], local_sems.at[10]),
    ]
    for made in local[2:]:
        made.start()
    arrived(gram_all.at[pl.ds(0, b - piece), :], ("gx",))
    local.append(pltpu.make_async_copy(gram_all, gram_out, local_sems.at[11]))
    local[-1].start()

    for condition, source in pending:
        made = functools.partial(
            lambda source: remote(source, source, 0, neighbour).wait_send(), source
        )
        if condition is None:
            made()
        else:
            @pl.when(condition())
            def _():
                made()
    for made in local:
        made.wait()
    assert len(numbers) <= recv_sems.shape[0]


def body(trailing, leaf_vectors, leaf_factors, tree_vectors, tree_factors, inverse_factor):
    b, nc = leaf_vectors.shape[1], trailing.shape[1]
    devices = lax.axis_size("rows")
    total_rows = trailing.shape[0] * devices
    levels = (devices // ROW).bit_length() - 1
    piece = b // ROW

    def vmem(*shape, dtype=F32):
        return pltpu.VMEM(shape, dtype)

    arguments = (
        trailing, leaf_vectors, leaf_factors, tree_vectors, tree_factors, inverse_factor
    )
    per_level = [vmem(nc >> level, b) for level in (1, 2, 3)]
    scratch = [
        *[vmem(*argument.shape) for argument in arguments],
        vmem(b + 8, b),
        vmem(b // 2 + 8, b),
        *[vmem(b + 8, b)] * 4,
        vmem(3 + levels, b // 2 + 8, b),
        vmem(b // 2 + 8, b),
        vmem(3 + levels, b, b, dtype=BF16),
        vmem(3 + levels, b, b, dtype=BF16),
        vmem(4, b, b, dtype=BF16),
        vmem(4, b, b, dtype=BF16),
        vmem(nc, b),
        *per_level,
        *per_level, *per_level, *per_level, *per_level,
        vmem(nc // 8, b), vmem(levels, nc // 8, b), vmem(levels, nc // 8, b),
        vmem(nc // 8, b),
        *per_level,
        vmem(nc, b),
        vmem(b, nc), vmem(b, nc), vmem(b, b), vmem(b, nc), vmem(b, b),
        vmem(b, 2 * b, dtype=BF16), vmem(b, 2 * b, dtype=BF16),
        vmem(b, b), vmem(ROW - 1, piece, b), vmem(piece, b), vmem(levels, piece, b),
        vmem(b, b), vmem(b, b),
        pltpu.SemaphoreType.DMA,
        pltpu.SemaphoreType.DMA((RECEIVES,)),
        pltpu.SemaphoreType.DMA((12,)),
    ]
    return pl.pallas_call(
        functools.partial(tree_kernel, devices, total_rows),
        out_shape=(
            jax.ShapeDtypeStruct(trailing.shape, F32),
            jax.ShapeDtypeStruct(leaf_vectors.shape, F32),
            jax.ShapeDtypeStruct((b, b), F32),
        ),
        in_specs=[pl.BlockSpec(memory_space=pl.ANY)] * 6,
        out_specs=[pl.BlockSpec(memory_space=pl.ANY)] * 3,
        scratch_shapes=scratch,
        compiler_params=pltpu.CompilerParams(
            collective_id=0,
            has_side_effects=True,
            vmem_limit_bytes=56 * 1024 * 1024,
        ),
        name="tree",
    )(*arguments)


def solution(mesh):
    rows = P("rows", None)
    return jax.shard_map(
        body,
        mesh=mesh,
        in_specs=(rows, rows, rows, rows, rows, P()),
        out_specs=(rows, rows, P()),
        check_vma=False,
    )
```

```python
import functools

import jax
import jax.numpy as jnp
from jax import lax
from jax.experimental import pallas as pl
from jax.experimental.pallas import tpu as pltpu
from jax.sharding import PartitionSpec as P

F32 = jnp.float32
BF16 = jnp.bfloat16
ROW = 8
YDIM = 4
MESH = pl.DeviceIdType.MESH
RECEIVES = 56


def halves(value):
    high = value.astype(BF16)
    low = (value - high.astype(F32)).astype(BF16)
    return high, low


def dot_pairs(left, right, transposed=False):
    dims = (((1,), (1 if transposed else 0,)), ((), ()))

    def one(a, b):
        return lax.dot_general(a, b, dims, preferred_element_type=F32)

    return one(left[0], right[0]) + (one(left[0], right[1]) + one(left[1], right[0]))


def dot3(left_side, right_side, transposed=False):
    return dot_pairs(halves(left_side), halves(right_side), transposed)


def tree_kernel(
    devices,
    total_rows,
    c_hbm, lv_hbm, lt_hbm, tv_hbm, tt_hbm, inv_hbm,
    upd_out, basis_out, gram_out,
    c_ref, lv_ref, lt_ref, tv_ref, tt_ref, inv_ref,
    pack,
    folded,
    slot0, slot1, slot2, slot3,
    fold,
    row_fold, row_fold_bt,
    t_high, t_low,
    bt_high, bt_low,
    head,
    cur0, cur1, cur2,
    z0, z1, z2, in0, in1, in2, w0, w1, w2, wb0, wb1, wb2,
    zr, inr, wr, wbr,
    res1, res2, res3,
    gathered,
    coef, rest, rest_basis, head_rows, head_basis,
    lvt_high, lvt_low,
    gram_own, gram_piece, gram_y, gram_z, gram_x, panel, gram_all, gram_total, wback,
    send_sem, recv_sems, local_sems,
):
    b = pack.shape[1]
    hb = b // 2
    nc = c_ref.shape[1]
    row_count = devices // ROW
    row_levels = row_count.bit_length() - 1
    zdim = row_count // YDIM
    piece = b // ROW
    me = lax.axis_index("rows")
    r = me % ROW
    g = me // ROW
    core = r % 2
    x0 = (r // 2) % 2
    x1 = r // 4
    bits = (core, x0, x1)
    base = g * ROW
    y = g % YDIM
    z = g // YDIM
    neighbour = base + (r + 1) % ROW

    def y_mate(j):
        return (z * YDIM + (y + j) % YDIM) * ROW + r

    def z_mate(j):
        return ((z + j) % zdim * YDIM + y) * ROW + r

    cur = (cur0, cur1, cur2)
    zs, ins, ws, wbs = (z0, z1, z2), (in0, in1, in2), (w0, w1, w2), (wb0, wb1, wb2)
    slot = (slot0, slot1, slot2, slot3)
    folds = [fold.at[i] for i in range(3 + row_levels)]
    CHUNKS = (0, 1)
    eighth_b = (nc - b) // 8
    ROW_CHUNKS = (
        pl.ds(0, piece),
        pl.ds(piece, eighth_b // 2),
        pl.ds(piece + eighth_b // 2, eighth_b // 2),
    )

    def slice_of(rank):
        return rank % 2 * 4 + rank // 2 % 2 * 2 + rank // 4

    def piece_of(rank):
        return pl.ds(pl.multiple_of(slice_of(rank) * piece, piece), piece)

    mine = piece_of(r)

    def size(level, chunk):
        return ((nc - b) // 2 if chunk else b // 2) >> level

    def own(level, chunk):
        return pl.ds((b // 2 >> level) if chunk else 0, size(level, chunk))

    def part(level, chunk, upper):
        start = (b >> level) if chunk else 0
        return pl.ds(start + (size(level, chunk) if upper else 0), size(level, chunk))

    def parent(level):
        return cur[level - 1] if level else head

    def is_low(k):
        return g % (2 << k) == 0

    def is_high(k):
        return g % (2 << k) == (1 << k)

    def low_half(k):
        return is_low(k) if k < 2 else (y == 0) & (g // (1 << k) % 2 == 0)

    def high_half(k):
        return is_high(k) if k < 2 else (y == 0) & (g // (1 << k) % 2 == 1)

    def takes_fold(k):
        return is_low(k) if k < 2 else (y == 0) & jnp.logical_not(is_high(k))

    backs = [wback.at[k] for k in range(row_levels)]

    loads = {}
    for name, source, target in (
        ("tv", tv_hbm, tv_ref),
        ("tt", tt_hbm, tt_ref),
        ("lv", lv_hbm, lv_ref),
        ("c0", c_hbm.at[:, pl.ds(0, b)], c_ref.at[:, pl.ds(0, b)]),
        ("lt", lt_hbm, lt_ref),
        ("c1", c_hbm.at[:, pl.ds(b, nc - b)], c_ref.at[:, pl.ds(b, nc - b)]),
        ("inv", inv_hbm, inv_ref),
    ):
        loads[name] = pltpu.make_async_copy(source, target, local_sems.at[len(loads)])
        loads[name].start()

    barrier = pltpu.get_barrier_semaphore()

    def greet(other):
        pl.semaphore_signal(barrier, inc=1, device_id=(other,), device_id_type=MESH)

    for j in range(1, ROW):
        greet(base + (r + j) % ROW)
    for j in range(1, YDIM):
        greet(y_mate(j))
    for j in range(1, zdim):
        greet(z_mate(j))

    def entered():
        pl.semaphore_wait(barrier, ROW - 1 + YDIM - 1 + zdim - 1)

    numbers = {}
    pending = []

    def number(*name):
        return numbers.setdefault(name, len(numbers))

    def remote(source, target, receive, other):
        return pltpu.make_async_remote_copy(
            src_ref=source,
            dst_ref=target,
            send_sem=send_sem,
            recv_sem=recv_sems.at[receive],
            device_id=(other,),
            device_id_type=MESH,
        )

    def copy(source, target, name, other, condition=None):
        remote(source, target, number(*name), other).start()
        pending.append((condition, source))

    def arrived(target, name):
        remote(target, target, number(*name), neighbour).wait_recv()

    row_id = lax.broadcasted_iota(jnp.int32, (b, b), 0)
    col_id = lax.broadcasted_iota(jnp.int32, (b, b), 1)
    row_half = lax.broadcasted_iota(jnp.int32, (hb, hb), 0)
    col_half = lax.broadcasted_iota(jnp.int32, (hb, hb), 1)

    def t_of(ref):
        return jnp.where(row_id <= col_id, ref[:b, :], 0.0)

    def vt_of(ref):
        diagonal = jnp.where(row_id == col_id, ref[b : b + 1, :], 0.0)
        return jnp.where(row_id > col_id, ref[:b, :], diagonal)

    def make_fold(target, t):
        last = t[hb:, hb:]
        target[:hb, :hb] = jnp.where(row_half <= col_half, t[:hb, :hb], last.T)
        target[:hb, hb:] = t[:hb, hb:]
        diagonal = jnp.sum(
            jnp.where(row_half == col_half, last, 0.0), axis=0, keepdims=True
        )
        target[hb:, :hb] = jnp.broadcast_to(diagonal, (8, hb))
        target[hb:, hb:] = jnp.zeros((8, hb), F32)

    def store_t(index, value, rows, columns):
        high, low = halves(value)
        t_high[index, rows, columns] = high
        t_low[index, rows, columns] = low

    FIRST, LAST = pl.ds(0, hb), pl.ds(hb, hb)

    def t_from_fold(index):
        first = fold[index, :hb, :hb]
        store_t(index, jnp.where(row_half <= col_half, first, 0.0), FIRST, FIRST)
        store_t(index, fold[index, :hb, hb:], FIRST, LAST)
        store_t(index, jnp.zeros((hb, hb), F32), LAST, FIRST)
        diagonal = jnp.where(row_half == col_half, fold[index, hb : hb + 1, :hb], 0.0)
        last = jnp.where(row_half < col_half, first.T, diagonal)
        store_t(index, last, LAST, LAST)

    def t_from_slot(index):
        store_t(index, t_of(slot[index]), pl.ds(0, b), pl.ds(0, b))

    def make_bt(index):
        high, low = halves(dot3(vt_of(slot[index]).T, t_of(slot[index])))
        bt_high[index] = high
        bt_low[index] = low

    def times_bt(value, index):
        return dot_pairs(halves(value), (bt_high[index], bt_low[index]))

    def times_t(value, index):
        return dot_pairs(halves(value), (t_high[index], t_low[index]))

    loads["tv"].wait()
    loads["tt"].wait()
    tv = tv_ref[...]
    tt = tt_ref[...]
    pack[:b, :] = jnp.where(row_id <= col_id, tt, tv.T)
    diagonal = jnp.sum(jnp.where(row_id == col_id, tv, 0.0), axis=0, keepdims=True)
    pack[b:, :] = jnp.broadcast_to(diagonal, (8, b))
    make_fold(folded, tt)

    for condition, index in (
        (core == 1, 0), ((r == 2) | (r == 6), 1), (r == 4, 2), ((r == 0) & (g > 0), 3),
    ):
        @pl.when(condition)
        def _():
            slot[index][...] = pack[...]
            make_bt(index)
            if index < 3:
                t_from_slot(index)

    loads["lv"].wait()
    high, low = halves(lv_ref[...].T)
    lvt_high[...] = high
    lvt_low[...] = low

    def leaf_tile(tile):
        columns = pl.ds(tile * b, b)
        inner = dot_pairs((lvt_high[...], lvt_low[...]), halves(c_ref[:, columns]))
        coeffs = dot3(lt_ref[...].T, inner)
        coef[:, columns] = coeffs
        result = c_ref[:b, columns] - dot3(lv_ref[:b, :], coeffs)
        head[columns, :] = result.T

    loads["c0"].wait()
    loads["lt"].wait()
    leaf_tile(0)
    entered()

    @pl.when(core == 1)
    def _():
        copy(folded, folds[0], ("fold", 0), me - 1, lambda: core == 1)

    @pl.when((r == 2) | (r == 6))
    def _():
        c = lambda: (r == 2) | (r == 6)
        copy(pack, slot1, ("slot", 1), me + 1, c)
        copy(folded, folds[1], ("fold", 1), me - 2, c)

    @pl.when(r == 4)
    def _():
        copy(folded, folds[2], ("fold", 2), base, lambda: r == 4)
        copy(pack, slot2, ("slot", 2), base + 5, lambda: r == 4)
        copy(folded, folds[2], ("fold", 2), base + 2, lambda: r == 4)
        copy(pack, slot2, ("slot", 2), base + 6, lambda: r == 4)

    @pl.when((r == 0) & (g > 0))
    def _():
        for other in (1, 2, 6):
            copy(pack, slot3, ("slot", 3), base + other, lambda: (r == 0) & (g > 0))

    def send(level, chunk):
        bit, far = bits[level], 1 << level
        rows, name = own(level, chunk), ("x", level, chunk)
        target = ins[level].at[rows, :]
        low_rows, high_rows = part(level, chunk, False), part(level, chunk, True)

        @pl.when(bit == 0)
        def _():
            copy(
                parent(level).at[high_rows, :], target, name, me + far,
                lambda: bits[level] == 0,
            )

        source = zs[level].at[rows, :]

        @pl.when(bit == 1)
        def _():
            zs[level][rows, :] = times_bt(parent(level)[low_rows, :], level)
            copy(source, target, name, me - far, lambda: bits[level] == 1)

    def finish(level, chunk):
        bit = bits[level]
        rows, name = own(level, chunk), ("x", level, chunk)
        low_rows, high_rows = part(level, chunk, False), part(level, chunk, True)

        @pl.when(bit == 0)
        def _():
            value = parent(level)[low_rows, :]
            update = times_t(value, level)
            arrived(ins[level].at[rows, :], name)
            update = update + ins[level][rows, :]
            cur[level][rows, :] = value - update
            ws[level][rows, :] = update

        @pl.when(bit == 1)
        def _():
            update = times_bt(parent(level)[high_rows, :], level)
            arrived(ins[level].at[rows, :], name)
            value = ins[level][rows, :]
            update = update + times_t(value, level)
            cur[level][rows, :] = value - update
            ws[level][rows, :] = update

    def give_back(level, chunk):
        rows = own(level, chunk)

        @pl.when(bits[level] == 0)
        def _():
            copy(
                ws[level].at[rows, :], wbs[level].at[rows, :], ("w", level, chunk),
                me + (1 << level), lambda: bits[level] == 0,
            )

    def residual(level, result):
        @pl.when(bits[level] == 1)
        def _():
            vt = halves(vt_of(slot[level]))
            for chunk in CHUNKS:
                rows = own(level, chunk)
                low_rows, high_rows = part(level, chunk, False), part(level, chunk, True)
                result[high_rows, :] = parent(level)[high_rows, :] - dot_pairs(
                    halves(ws[level][rows, :]), vt
                )
                arrived(wbs[level].at[rows, :], ("w", level, chunk))
                result[low_rows, :] = parent(level)[low_rows, :] - dot_pairs(
                    halves(wbs[level][rows, :]), vt
                )

    def place(level, rank, chunk):
        start = b if chunk else 0
        for bit in range(level):
            start += (rank >> bit & 1) * size(bit, chunk)
        return pl.ds(start, size(level - 1, chunk))

    def buffer_rows(level, chunk):
        return pl.ds((b >> level) if chunk else 0, size(level - 1, chunk))

    def gather(level, result, rank, into, chunks, condition):
        for chunk in chunks:
            if rank == into:
                gathered[place(level, rank, chunk), :] = result[buffer_rows(level, chunk), :]
            else:
                copy(
                    result.at[buffer_rows(level, chunk), :],
                    gathered.at[place(level, rank, chunk), :],
                    ("gather",), base + into, condition,
                )

    yrows, zrows = b // YDIM, b // YDIM // zdim

    def block_y(other):
        return pl.ds(pl.multiple_of(other * yrows, yrows), yrows)

    def block_z(other):
        return pl.ds(pl.multiple_of(other * zrows, zrows), zrows)

    my_rows = pl.ds(pl.multiple_of(y * yrows + z * zrows, zrows), zrows)

    def gram_start():
        columns = c_ref[:, :b]
        gram_own[...] = dot3(columns.T, columns)
        for j in range(1, YDIM):
            copy(
                gram_own.at[block_y((y + j) % YDIM), :], gram_y.at[YDIM - j - 1],
                ("gram y",), y_mate(j),
            )

    def gram_sum_y():
        arrived(gram_y, ("gram y",))
        total = gram_own[block_y(y), :]
        for j in range(YDIM - 1):
            total = total + gram_y[j]
        gram_piece[...] = total
        for j in range(1, zdim):
            copy(
                gram_piece.at[block_z((z + j) % zdim), :], gram_z.at[zdim - j - 1],
                ("gram z",), z_mate(j),
            )

    mine_x = gram_x.at[r]

    def gram_sum_z():
        total = gram_piece[block_z(z), :]
        if zdim > 1:
            arrived(gram_z, ("gram z",))
        for j in range(zdim - 1):
            total = total + gram_z[j]
        gram_x[r] = total
        for j in range(1, ROW):
            copy(
                mine_x, mine_x, ("gram x",), base + (r + j) % ROW,
            )

    def gram_sum_x():
        arrived(gram_x.at[pl.ds(0, ROW - 1)], ("gram x",))
        total = gram_x[0]
        for j in range(1, ROW):
            total = total + gram_x[j]
        gram_all[my_rows, :] = total
        for j in range(1, zdim):
            copy(
                gram_all.at[my_rows, :], gram_all.at[my_rows, :], ("all z",), z_mate(j),
            )

    def gram_all_y():
        if zdim > 1:
            arrived(gram_all.at[pl.ds(0, yrows - zrows), :], ("all z",))
        for j in range(1, YDIM):
            copy(
                gram_all.at[block_y(y), :], gram_all.at[block_y(y), :], ("all y",),
                y_mate(j),
            )

    send(0, 0)
    loads["c1"].wait()
    for tile in range(1, nc // b):
        leaf_tile(tile)
    send(0, 1)

    @pl.when(core == 0)
    def _():
        arrived(folds[0], ("fold", 0))
        t_from_fold(0)

    finish(0, 0)

    @pl.when((r == 3) | (r == 7))
    def _():
        arrived(slot1, ("slot", 1))
        make_bt(1)
        t_from_slot(1)

    send(1, 0)

    finish(0, 1)
    send(1, 1)

    @pl.when((r == 0) & (g > 0))
    def _():
        copy(pack, slot3, ("slot", 3), base + 4, lambda: (r == 0) & (g > 0))

    @pl.when((r == 0) | (r == 4))
    def _():
        arrived(folds[1], ("fold", 1))
        copy(folds[1], folds[1], ("fold", 1), me + 1, lambda: (r == 0) | (r == 4))
        t_from_fold(1)

    give_back(0, 0)
    give_back(0, 1)
    gram_start()

    @pl.when(r == 6)
    def _():
        arrived(slot2, ("slot", 2))
        copy(slot2, slot2, ("slot", 2), me + 1, lambda: r == 6)
        make_bt(2)
        t_from_slot(2)

    @pl.when((r == 5) | (r == 7))
    def _():
        arrived(slot2, ("slot", 2))
        make_bt(2)
        t_from_slot(2)

    @pl.when((r == 1) | (r == 5))
    def _():
        arrived(folds[1], ("fold", 1))
        t_from_fold(1)

    finish(1, 0)
    send(2, 0)

    @pl.when((r == 0) | (r == 2))
    def _():
        arrived(folds[2], ("fold", 2))
        copy(folds[2], folds[2], ("fold", 2), me + 1, lambda: (r == 0) | (r == 2))
        t_from_fold(2)

    finish(1, 1)
    send(2, 1)

    @pl.when((g > 0) & (core == 0))
    def _():
        @pl.when(r > 0)
        def _():
            arrived(slot3, ("slot", 3))
            copy(
                slot3, slot3, ("slot", 3), me + 1,
                lambda: (g > 0) & (core == 0) & (r > 0),
            )

        make_fold(row_fold, t_of(slot3))

        @pl.when(r > 0)
        def _():
            make_bt(3)

        if row_levels > 2:
            make_fold(row_fold_bt, bt_high[3].astype(F32) + bt_low[3].astype(F32))
        for k in range(row_levels):
            @pl.when(is_high(k))
            def _():
                c = functools.partial(lambda k: is_high(k) & (core == 0), k)
                name = ("fold", 3 + k)
                for j in range(max(1, (1 << k) // YDIM)):
                    copy(
                        row_fold, folds[3 + k], name,
                        me - (ROW << k) + j * YDIM * ROW, c,
                    )
                    if j:
                        copy(row_fold_bt, folds[3 + k], name, me + j * YDIM * ROW, c)

    give_back(1, 0)
    give_back(1, 1)

    @pl.when((r == 1) | (r == 3))
    def _():
        arrived(folds[2], ("fold", 2))
        t_from_fold(2)

    def rest_tile(tile):
        columns = pl.ds(tile * b, b)
        rest[:, columns] = c_ref[b:, columns] - dot3(lv_ref[b:, :], coef[:, columns])

    gram_sum_y()
    rest_tile(0)
    loads["inv"].wait()
    rest_basis[...] = dot3(rest[:, :b], inv_ref[...])
    for tile in range(1, nc // b):
        rest_tile(tile)
    local = [
        pltpu.make_async_copy(rest, upd_out.at[pl.ds(b, b), :], local_sems.at[7]),
        pltpu.make_async_copy(rest_basis, basis_out.at[pl.ds(b, b), :], local_sems.at[8]),
    ]
    for made in local:
        made.start()

    @pl.when((g > 0) & (core == 1))
    def _():
        arrived(slot3, ("slot", 3))

    @pl.when((g > 0) & (core == 1))
    def _():
        make_bt(3)

    def send_z(k, chunk):
        rows = ROW_CHUNKS[chunk]
        source = zr.at[rows, :]

        @pl.when(is_high(k))
        def _():
            zr[rows, :] = times_bt(cur2[rows, :], 3)
            copy(
                source, inr.at[k, rows, :], ("z", k, chunk), me - (ROW << k),
                functools.partial(is_high, k),
            )

    def send_u(k, chunk):
        rows = ROW_CHUNKS[chunk]
        ahead = wr.at[k, rows, :]

        @pl.when(is_low(k))
        def _():
            wr[k, rows, :] = times_t(cur2[rows, :], 3 + k)
            copy(
                ahead, wbr.at[rows, :], ("wr", chunk), me + (ROW << k),
                functools.partial(is_low, k),
            )

    def finish_row(k, chunk):
        rows = ROW_CHUNKS[chunk]

        @pl.when(is_low(k))
        def _():
            arrived(inr.at[k, rows, :], ("z", k, chunk))
            cur2[rows, :] = cur2[rows, :] - (wr[k, rows, :] + inr[k, rows, :])

    PANEL = ROW_CHUNKS[0]

    def send_shared(k):
        ours = wr.at[k, PANEL, :]

        @pl.when(low_half(k))
        def _():
            value = cur2[PANEL, :]
            wr[k, PANEL, :] = value - times_t(value, 3 + k)
            copy(
                ours, inr.at[k, PANEL, :], ("z", k, 0), me + (ROW << k),
                functools.partial(low_half, k),
            )

        @pl.when(high_half(k))
        def _():
            wr[k, PANEL, :] = -times_t(cur2[PANEL, :], 3 + k)
            copy(
                ours, inr.at[k, PANEL, :], ("z", k, 0), me - (ROW << k),
                functools.partial(high_half, k),
            )

    def finish_shared(k):
        back = backs[k]

        @pl.when(y == 0)
        def _():
            arrived(inr.at[k, PANEL, :], ("z", k, 0))

        @pl.when(is_high(k))
        def _():
            res3[PANEL, :] = cur2[PANEL, :]

        @pl.when(is_low(k))
        def _():
            value = cur2[PANEL, :] - (wr[k, PANEL, :] + inr[k, PANEL, :])
            wback[k, :, :] = value
            copy(
                back, wbr.at[PANEL, :], ("wr", 0), me + (ROW << k),
                functools.partial(is_low, k),
            )

        @pl.when(y == 0)
        def _():
            cur2[PANEL, :] = wr[k, PANEL, :] + inr[k, PANEL, :]

    def send_level(k, chunk):
        if k > 1 and chunk == 0:
            send_shared(k)
        else:
            send_z(k, chunk)
            send_u(k, chunk)

    def finish_level(k, chunk):
        if k > 1 and chunk == 0:
            finish_shared(k)
        else:
            finish_row(k, chunk)

    def forward_operators(k):
        @pl.when(takes_fold(k) & (core == 0))
        def _():
            arrived(folds[3 + k], ("fold", 3 + k))
            copy(
                folds[3 + k], folds[3 + k], ("fold", 3 + k), me + 1,
                functools.partial(lambda k: takes_fold(k) & (core == 0), k),
            )

    def row_operators(k):
        @pl.when(takes_fold(k) & (core == 1))
        def _():
            arrived(folds[3 + k], ("fold", 3 + k))

        if k > 1:
            @pl.when(is_high(k))
            def _():
                make_fold(fold.at[3 + k], bt_high[3].astype(F32) + bt_low[3].astype(F32))

        @pl.when(takes_fold(k) if k < 2 else y == 0)
        def _():
            t_from_fold(3 + k)

    finish(2, 0)
    send_z(0, 0)
    finish(2, 1)
    send_z(0, 1)
    send_z(0, 2)
    forward_operators(0)
    give_back(2, 0)
    give_back(2, 1)

    gram_sum_z()
    row_operators(0)
    for chunk in range(3):
        send_u(0, chunk)

    def panel_to_row():
        for j in range(1, ROW):
            copy(
                panel.at[mine, :], panel.at[mine, :], ("panel",),
                base + (r + j) % ROW, lambda: y == 0,
            )

    def panel_out():
        @pl.when(y == 0)
        def _():
            panel[mine, :] = cur2[PANEL, :]
            for j in range(1, YDIM):
                copy(
                    panel.at[mine, :], panel.at[mine, :], ("panel y",), y_mate(j),
                    lambda: y == 0,
                )
            panel_to_row()

    def gather_row(result, chunk, condition):
        for rank in range(ROW):
            start = place(3, rank, min(chunk, 1)).start
            start += eighth_b // 2 if chunk == 2 else 0
            rows = pl.ds(start, ROW_CHUNKS[chunk].size)

            @pl.when(r == rank)
            def _():
                if rank == 0:
                    gathered[rows, :] = result[ROW_CHUNKS[chunk], :]
                else:
                    copy(
                        result.at[ROW_CHUNKS[chunk], :], gathered.at[rows, :],
                        ("gather",), base,
                        functools.partial(lambda o: condition() & (r == o), rank),
                    )

    events = []
    for k in range(row_levels):
        events += [(2.9 * k, k, 0), (2.0 + 4.2 * k, k, 1), (2.9 + 4.2 * k, k, 2)]
    done = set()
    last = row_levels - 1
    for _, k, chunk in sorted(events):
        if k < last and chunk == 0:
            forward_operators(k + 1)
        finish_level(k, chunk)
        if k < last:
            if chunk == 0:
                row_operators(k + 1)
            send_level(k + 1, chunk)
        done.add((k, chunk))
        if (k, chunk) == (last, 0):
            panel_out()
        if k == last:
            @pl.when(g == 0)
            def _():
                gather_row(cur2, chunk, lambda: g == 0)
        if (k, chunk) == (0, 2):
            residual(0, gathered)
            residual(1, res1)
            for rank, into in ((2, 2), (3, 2), (6, 6), (7, 6)):
                @pl.when(r == rank)
                def _():
                    gather(1, res1, rank, into, CHUNKS, functools.partial(lambda o: r == o, rank))
        if (k, chunk) == (1, 2):
            residual(2, res2)
            for rank in range(4, ROW):
                @pl.when(r == rank)
                def _():
                    gather(2, res2, rank, 4, CHUNKS, functools.partial(lambda o: r == o, rank))
            gram_sum_x()
        if (k, chunk) == (2, 2):
            gram_all_y()

    def row_result(chunk):
        rows = ROW_CHUNKS[chunk]

        @pl.when(g > 0)
        def _():
            vt = halves(vt_of(slot3))
            arrived(wbr.at[rows, :], ("wr", chunk))
            value = wbr[rows, :]
            if chunk or row_levels < 3:
                value = value + zr[rows, :]
                res3[rows, :] = cur2[rows, :] - dot_pairs(halves(value), vt)
            else:
                shared = y == 0
                value = jnp.where(shared, value, value + zr[rows, :])
                start = jnp.where(shared, res3[rows, :], cur2[rows, :])
                res3[rows, :] = start - dot_pairs(halves(value), vt)
            gather_row(res3, chunk, lambda: g > 0)

    for chunk in (1, 2, 0):
        row_result(chunk)

    @pl.when(y != 0)
    def _():
        arrived(panel.at[mine, :], ("panel y",))
        for j in range(1, ROW):
            copy(
                panel.at[mine, :], panel.at[mine, :], ("panel",),
                base + (r + j) % ROW, lambda: y != 0,
            )

    @pl.when((r == 2) | (r == 6))
    def _():
        arrived(gathered.at[pl.ds(0, nc // 2), :], ("gather",))

    @pl.when(r == 4)
    def _():
        arrived(gathered.at[pl.ds(0, 3 * nc // 4), :], ("gather",))

    @pl.when(r == 0)
    def _():
        arrived(gathered.at[pl.ds(0, 7 * nc // 8), :], ("gather",))

    head_rows[...] = gathered[...].T
    head_basis[...] = jnp.where(me == 0, 0.0, dot3(head_rows[:, :b], inv_ref[...]))
    local += [
        pltpu.make_async_copy(head_rows, upd_out.at[pl.ds(0, b), :], local_sems.at[9]),
        pltpu.make_async_copy(head_basis, basis_out.at[pl.ds(0, b), :], local_sems.at[10]),
    ]
    for made in local[2:]:
        made.start()
    arrived(gram_all.at[pl.ds(0, b - yrows), :], ("all y",))
    arrived(panel.at[pl.ds(0, b - piece), :], ("panel",))
    square = dot3(panel[...], panel[...], True)
    gram_total[...] = (gram_all[...] - square) / float(total_rows)
    local.append(pltpu.make_async_copy(gram_total, gram_out, local_sems.at[11]))
    local[-1].start()

    for condition, source in pending:
        made = functools.partial(
            lambda source: remote(source, source, 0, neighbour).wait_send(), source
        )
        if condition is None:
            made()
        else:
            @pl.when(condition())
            def _():
                made()
    for made in local:
        made.wait()
    assert len(numbers) <= recv_sems.shape[0]


def body(trailing, leaf_vectors, leaf_factors, tree_vectors, tree_factors, inverse_factor):
    b, nc = leaf_vectors.shape[1], trailing.shape[1]
    devices = lax.axis_size("rows")
    total_rows = trailing.shape[0] * devices
    levels = (devices // ROW).bit_length() - 1
    piece = b // ROW
    zdim = devices // ROW // YDIM

    def vmem(*shape, dtype=F32):
        return pltpu.VMEM(shape, dtype)

    arguments = (
        trailing, leaf_vectors, leaf_factors, tree_vectors, tree_factors, inverse_factor
    )
    per_level = [vmem(nc >> level, b) for level in (1, 2, 3)]
    scratch = [
        *[vmem(*argument.shape) for argument in arguments],
        vmem(b + 8, b),
        vmem(b // 2 + 8, b),
        *[vmem(b + 8, b)] * 4,
        vmem(3 + levels, b // 2 + 8, b),
        vmem(b // 2 + 8, b), vmem(b // 2 + 8, b),
        vmem(3 + levels, b, b, dtype=BF16),
        vmem(3 + levels, b, b, dtype=BF16),
        vmem(4, b, b, dtype=BF16),
        vmem(4, b, b, dtype=BF16),
        vmem(nc, b),
        *per_level,
        *per_level, *per_level, *per_level, *per_level,
        vmem(nc // 8, b), vmem(levels, nc // 8, b), vmem(levels, nc // 8, b),
        vmem(nc // 8, b),
        *per_level,
        vmem(nc, b),
        vmem(b, nc), vmem(b, nc), vmem(b, b), vmem(b, nc), vmem(b, b),
        vmem(b, 2 * b, dtype=BF16), vmem(b, 2 * b, dtype=BF16),
        vmem(b, b),
        vmem(b // YDIM, b),
        vmem(YDIM - 1, b // YDIM, b),
        vmem(max(zdim - 1, 1), b // YDIM // zdim, b),
        vmem(ROW, b // YDIM // zdim, b),
        vmem(b, b), vmem(b, b), vmem(b, b),
        vmem(levels, piece, b),
        pltpu.SemaphoreType.DMA,
        pltpu.SemaphoreType.DMA((RECEIVES,)),
        pltpu.SemaphoreType.DMA((12,)),
    ]
    return pl.pallas_call(
        functools.partial(tree_kernel, devices, total_rows),
        out_shape=(
            jax.ShapeDtypeStruct(trailing.shape, F32),
            jax.ShapeDtypeStruct(leaf_vectors.shape, F32),
            jax.ShapeDtypeStruct((b, b), F32),
        ),
        in_specs=[pl.BlockSpec(memory_space=pl.ANY)] * 6,
        out_specs=[pl.BlockSpec(memory_space=pl.ANY)] * 3,
        scratch_shapes=scratch,
        compiler_params=pltpu.CompilerParams(
            collective_id=0,
            has_side_effects=True,
            vmem_limit_bytes=56 * 1024 * 1024,
        ),
        name="tree",
    )(*arguments)


def solution(mesh):
    rows = P("rows", None)
    return jax.shard_map(
        body,
        mesh=mesh,
        in_specs=(rows, rows, rows, rows, rows, P()),
        out_specs=(rows, rows, P()),
        check_vma=False,
    )
```

```python
import functools

import jax
import jax.numpy as jnp
from jax import lax
from jax.experimental import pallas as pl
from jax.experimental.pallas import tpu as pltpu
from jax.sharding import PartitionSpec as P

F32 = jnp.float32
BF16 = jnp.bfloat16
ROW = 8
YDIM = 4
MESH = pl.DeviceIdType.MESH
RECEIVES = 56


def halves(value):
    high = value.astype(BF16)
    low = (value - high.astype(F32)).astype(BF16)
    return high, low


def dot_pairs(left, right, transposed=False):
    dims = (((1,), (1 if transposed else 0,)), ((), ()))

    def one(a, b):
        return lax.dot_general(a, b, dims, preferred_element_type=F32)

    return one(left[0], right[0]) + (one(left[0], right[1]) + one(left[1], right[0]))


def dot3(left_side, right_side, transposed=False):
    return dot_pairs(halves(left_side), halves(right_side), transposed)


def tree_kernel(
    devices,
    total_rows,
    c_hbm, lv_hbm, lt_hbm, tv_hbm, tt_hbm, inv_hbm,
    head_rows, rest, head_basis, rest_basis, gram_total,
    c_ref, lv_ref, lt_ref, tv_ref, tt_ref, inv_ref,
    pack,
    folded,
    slot0, slot1, slot2, slot3,
    fold,
    row_fold, row_fold_bt,
    t_high, t_low,
    bt_high, bt_low,
    head,
    cur0, cur1, cur2,
    z0, z1, z2, in0, in1, in2, w0, w1, w2, wb0, wb1, wb2,
    zr, inr, wr, wbr,
    res1, res2, res3,
    gathered,
    coef,
    lvt_high, lvt_low,
    gram_own, gram_piece, gram_y, gram_z, gram_x, panel, gram_all, wback,
    send_sem, recv_sems, local_sems,
):
    b = pack.shape[1]
    hb = b // 2
    nc = c_ref.shape[1]
    row_count = devices // ROW
    row_levels = row_count.bit_length() - 1
    zdim = row_count // YDIM
    piece = b // ROW
    me = lax.axis_index("rows")
    r = me % ROW
    g = me // ROW
    core = r % 2
    x0 = (r // 2) % 2
    x1 = r // 4
    bits = (core, x0, x1)
    base = g * ROW
    y = g % YDIM
    z = g // YDIM
    neighbour = base + (r + 1) % ROW

    def y_mate(j):
        return (z * YDIM + (y + j) % YDIM) * ROW + r

    def z_mate(j):
        return ((z + j) % zdim * YDIM + y) * ROW + r

    cur = (cur0, cur1, cur2)
    zs, ins, ws, wbs = (z0, z1, z2), (in0, in1, in2), (w0, w1, w2), (wb0, wb1, wb2)
    slot = (slot0, slot1, slot2, slot3)
    folds = [fold.at[i] for i in range(3 + row_levels)]
    CHUNKS = (0, 1)
    eighth_b = (nc - b) // 8
    ROW_CHUNKS = (
        pl.ds(0, piece),
        pl.ds(piece, eighth_b // 2),
        pl.ds(piece + eighth_b // 2, eighth_b // 2),
    )

    def slice_of(rank):
        return rank % 2 * 4 + rank // 2 % 2 * 2 + rank // 4

    def piece_of(rank):
        return pl.ds(pl.multiple_of(slice_of(rank) * piece, piece), piece)

    mine = piece_of(r)

    def size(level, chunk):
        return ((nc - b) // 2 if chunk else b // 2) >> level

    def own(level, chunk):
        return pl.ds((b // 2 >> level) if chunk else 0, size(level, chunk))

    def part(level, chunk, upper):
        start = (b >> level) if chunk else 0
        return pl.ds(start + (size(level, chunk) if upper else 0), size(level, chunk))

    def parent(level):
        return cur[level - 1] if level else head

    def is_low(k):
        return g % (2 << k) == 0

    def is_high(k):
        return g % (2 << k) == (1 << k)

    def low_half(k):
        return is_low(k) if k < 2 else (y == 0) & (g // (1 << k) % 2 == 0)

    def high_half(k):
        return is_high(k) if k < 2 else (y == 0) & (g // (1 << k) % 2 == 1)

    def takes_fold(k):
        return is_low(k) if k < 2 else (y == 0) & jnp.logical_not(is_high(k))

    backs = [wback.at[k] for k in range(row_levels)]

    loads = {}
    for name, source, target in (
        ("tv", tv_hbm, tv_ref),
        ("tt", tt_hbm, tt_ref),
        ("lv", lv_hbm, lv_ref),
        ("c0", c_hbm.at[:, pl.ds(0, b)], c_ref.at[:, pl.ds(0, b)]),
        ("lt", lt_hbm, lt_ref),
        ("c1", c_hbm.at[:, pl.ds(b, nc - b)], c_ref.at[:, pl.ds(b, nc - b)]),
        ("inv", inv_hbm, inv_ref),
    ):
        loads[name] = pltpu.make_async_copy(source, target, local_sems.at[len(loads)])
        loads[name].start()

    barrier = pltpu.get_barrier_semaphore()

    def greet(other):
        pl.semaphore_signal(barrier, inc=1, device_id=(other,), device_id_type=MESH)

    for j in range(1, ROW):
        greet(base + (r + j) % ROW)
    for j in range(1, YDIM):
        greet(y_mate(j))
    for j in range(1, zdim):
        greet(z_mate(j))

    def entered():
        pl.semaphore_wait(barrier, ROW - 1 + YDIM - 1 + zdim - 1)

    numbers = {}
    pending = []

    def number(*name):
        return numbers.setdefault(name, len(numbers))

    def remote(source, target, receive, other):
        return pltpu.make_async_remote_copy(
            src_ref=source,
            dst_ref=target,
            send_sem=send_sem,
            recv_sem=recv_sems.at[receive],
            device_id=(other,),
            device_id_type=MESH,
        )

    def copy(source, target, name, other, condition=None):
        remote(source, target, number(*name), other).start()
        pending.append((condition, source))

    def arrived(target, name):
        remote(target, target, number(*name), neighbour).wait_recv()

    row_id = lax.broadcasted_iota(jnp.int32, (b, b), 0)
    col_id = lax.broadcasted_iota(jnp.int32, (b, b), 1)
    row_half = lax.broadcasted_iota(jnp.int32, (hb, hb), 0)
    col_half = lax.broadcasted_iota(jnp.int32, (hb, hb), 1)

    def t_of(ref):
        return jnp.where(row_id <= col_id, ref[:b, :], 0.0)

    def vt_of(ref):
        diagonal = jnp.where(row_id == col_id, ref[b : b + 1, :], 0.0)
        return jnp.where(row_id > col_id, ref[:b, :], diagonal)

    def make_fold(target, t):
        last = t[hb:, hb:]
        target[:hb, :hb] = jnp.where(row_half <= col_half, t[:hb, :hb], last.T)
        target[:hb, hb:] = t[:hb, hb:]
        diagonal = jnp.sum(
            jnp.where(row_half == col_half, last, 0.0), axis=0, keepdims=True
        )
        target[hb:, :hb] = jnp.broadcast_to(diagonal, (8, hb))
        target[hb:, hb:] = jnp.zeros((8, hb), F32)

    def store_t(index, value, rows, columns):
        high, low = halves(value)
        t_high[index, rows, columns] = high
        t_low[index, rows, columns] = low

    FIRST, LAST = pl.ds(0, hb), pl.ds(hb, hb)

    def t_from_fold(index):
        first = fold[index, :hb, :hb]
        store_t(index, jnp.where(row_half <= col_half, first, 0.0), FIRST, FIRST)
        store_t(index, fold[index, :hb, hb:], FIRST, LAST)
        store_t(index, jnp.zeros((hb, hb), F32), LAST, FIRST)
        diagonal = jnp.where(row_half == col_half, fold[index, hb : hb + 1, :hb], 0.0)
        last = jnp.where(row_half < col_half, first.T, diagonal)
        store_t(index, last, LAST, LAST)

    def t_from_slot(index):
        store_t(index, t_of(slot[index]), pl.ds(0, b), pl.ds(0, b))

    def make_bt(index):
        high, low = halves(dot3(vt_of(slot[index]).T, t_of(slot[index])))
        bt_high[index] = high
        bt_low[index] = low

    def times_bt(value, index):
        return dot_pairs(halves(value), (bt_high[index], bt_low[index]))

    def times_t(value, index):
        return dot_pairs(halves(value), (t_high[index], t_low[index]))

    loads["tv"].wait()
    loads["tt"].wait()
    tv = tv_ref[...]
    tt = tt_ref[...]
    pack[:b, :] = jnp.where(row_id <= col_id, tt, tv.T)
    diagonal = jnp.sum(jnp.where(row_id == col_id, tv, 0.0), axis=0, keepdims=True)
    pack[b:, :] = jnp.broadcast_to(diagonal, (8, b))
    make_fold(folded, tt)

    for condition, index in (
        (core == 1, 0), ((r == 2) | (r == 6), 1), (r == 4, 2), ((r == 0) & (g > 0), 3),
    ):
        @pl.when(condition)
        def _():
            slot[index][...] = pack[...]
            make_bt(index)
            if index < 3:
                t_from_slot(index)

    loads["lv"].wait()
    high, low = halves(lv_ref[...].T)
    lvt_high[...] = high
    lvt_low[...] = low

    def leaf_tile(tile):
        columns = pl.ds(tile * b, b)
        inner = dot_pairs((lvt_high[...], lvt_low[...]), halves(c_ref[:, columns]))
        coeffs = dot3(lt_ref[...].T, inner)
        coef[:, columns] = coeffs
        result = c_ref[:b, columns] - dot3(lv_ref[:b, :], coeffs)
        head[columns, :] = result.T

    loads["c0"].wait()
    loads["lt"].wait()
    leaf_tile(0)
    entered()

    @pl.when(core == 1)
    def _():
        copy(folded, folds[0], ("fold", 0), me - 1, lambda: core == 1)

    @pl.when((r == 2) | (r == 6))
    def _():
        c = lambda: (r == 2) | (r == 6)
        copy(pack, slot1, ("slot", 1), me + 1, c)
        copy(folded, folds[1], ("fold", 1), me - 2, c)

    @pl.when(r == 4)
    def _():
        copy(folded, folds[2], ("fold", 2), base, lambda: r == 4)
        copy(pack, slot2, ("slot", 2), base + 5, lambda: r == 4)
        copy(folded, folds[2], ("fold", 2), base + 2, lambda: r == 4)
        copy(pack, slot2, ("slot", 2), base + 6, lambda: r == 4)

    @pl.when((r == 0) & (g > 0))
    def _():
        for other in (1, 2, 6):
            copy(pack, slot3, ("slot", 3), base + other, lambda: (r == 0) & (g > 0))

    def send(level, chunk):
        bit, far = bits[level], 1 << level
        rows, name = own(level, chunk), ("x", level, chunk)
        target = ins[level].at[rows, :]
        low_rows, high_rows = part(level, chunk, False), part(level, chunk, True)

        @pl.when(bit == 0)
        def _():
            copy(
                parent(level).at[high_rows, :], target, name, me + far,
                lambda: bits[level] == 0,
            )

        source = zs[level].at[rows, :]

        @pl.when(bit == 1)
        def _():
            zs[level][rows, :] = times_bt(parent(level)[low_rows, :], level)
            copy(source, target, name, me - far, lambda: bits[level] == 1)

    def finish(level, chunk):
        bit = bits[level]
        rows, name = own(level, chunk), ("x", level, chunk)
        low_rows, high_rows = part(level, chunk, False), part(level, chunk, True)

        @pl.when(bit == 0)
        def _():
            value = parent(level)[low_rows, :]
            update = times_t(value, level)
            arrived(ins[level].at[rows, :], name)
            update = update + ins[level][rows, :]
            cur[level][rows, :] = value - update
            ws[level][rows, :] = update

        @pl.when(bit == 1)
        def _():
            update = times_bt(parent(level)[high_rows, :], level)
            arrived(ins[level].at[rows, :], name)
            value = ins[level][rows, :]
            update = update + times_t(value, level)
            cur[level][rows, :] = value - update
            ws[level][rows, :] = update

    def give_back(level, chunk):
        rows = own(level, chunk)

        @pl.when(bits[level] == 0)
        def _():
            copy(
                ws[level].at[rows, :], wbs[level].at[rows, :], ("w", level, chunk),
                me + (1 << level), lambda: bits[level] == 0,
            )

    def residual(level, result):
        @pl.when(bits[level] == 1)
        def _():
            vt = halves(vt_of(slot[level]))
            for chunk in CHUNKS:
                rows = own(level, chunk)
                low_rows, high_rows = part(level, chunk, False), part(level, chunk, True)
                result[high_rows, :] = parent(level)[high_rows, :] - dot_pairs(
                    halves(ws[level][rows, :]), vt
                )
                arrived(wbs[level].at[rows, :], ("w", level, chunk))
                result[low_rows, :] = parent(level)[low_rows, :] - dot_pairs(
                    halves(wbs[level][rows, :]), vt
                )

    def place(level, rank, chunk):
        start = b if chunk else 0
        for bit in range(level):
            start += (rank >> bit & 1) * size(bit, chunk)
        return pl.ds(start, size(level - 1, chunk))

    def buffer_rows(level, chunk):
        return pl.ds((b >> level) if chunk else 0, size(level - 1, chunk))

    def gather(level, result, rank, into, chunks, condition):
        for chunk in chunks:
            if rank == into:
                gathered[place(level, rank, chunk), :] = result[buffer_rows(level, chunk), :]
            else:
                copy(
                    result.at[buffer_rows(level, chunk), :],
                    gathered.at[place(level, rank, chunk), :],
                    ("gather",), base + into, condition,
                )

    yrows, zrows = b // YDIM, b // YDIM // zdim

    def block_y(other):
        return pl.ds(pl.multiple_of(other * yrows, yrows), yrows)

    def block_z(other):
        return pl.ds(pl.multiple_of(other * zrows, zrows), zrows)

    my_rows = pl.ds(pl.multiple_of(y * yrows + z * zrows, zrows), zrows)

    def gram_start():
        columns = c_ref[:, :b]
        gram_own[...] = dot3(columns.T, columns)
        for j in range(1, YDIM):
            copy(
                gram_own.at[block_y((y + j) % YDIM), :], gram_y.at[YDIM - j - 1],
                ("gram y",), y_mate(j),
            )

    def gram_sum_y():
        arrived(gram_y, ("gram y",))
        total = gram_own[block_y(y), :]
        for j in range(YDIM - 1):
            total = total + gram_y[j]
        gram_piece[...] = total
        for j in range(1, zdim):
            copy(
                gram_piece.at[block_z((z + j) % zdim), :], gram_z.at[zdim - j - 1],
                ("gram z",), z_mate(j),
            )

    mine_x = gram_x.at[r]

    def gram_sum_z():
        total = gram_piece[block_z(z), :]
        if zdim > 1:
            arrived(gram_z, ("gram z",))
        for j in range(zdim - 1):
            total = total + gram_z[j]
        gram_x[r] = total
        for j in range(1, ROW):
            copy(
                mine_x, mine_x, ("gram x",), base + (r + j) % ROW,
            )

    def gram_sum_x():
        arrived(gram_x.at[pl.ds(0, ROW - 1)], ("gram x",))
        total = gram_x[0]
        for j in range(1, ROW):
            total = total + gram_x[j]
        gram_all[my_rows, :] = total
        for j in range(1, zdim):
            copy(
                gram_all.at[my_rows, :], gram_all.at[my_rows, :], ("all z",), z_mate(j),
            )

    def gram_all_y():
        if zdim > 1:
            arrived(gram_all.at[pl.ds(0, yrows - zrows), :], ("all z",))
        for j in range(1, YDIM):
            copy(
                gram_all.at[block_y(y), :], gram_all.at[block_y(y), :], ("all y",),
                y_mate(j),
            )

    send(0, 0)
    loads["c1"].wait()
    for tile in range(1, nc // b):
        leaf_tile(tile)
    send(0, 1)

    @pl.when(core == 0)
    def _():
        arrived(folds[0], ("fold", 0))
        t_from_fold(0)

    finish(0, 0)

    @pl.when((r == 3) | (r == 7))
    def _():
        arrived(slot1, ("slot", 1))
        make_bt(1)
        t_from_slot(1)

    send(1, 0)

    finish(0, 1)
    send(1, 1)

    @pl.when((r == 0) | (r == 4))
    def _():
        arrived(folds[1], ("fold", 1))
        copy(folds[1], folds[1], ("fold", 1), me + 1, lambda: (r == 0) | (r == 4))
        t_from_fold(1)

    give_back(0, 0)
    give_back(0, 1)
    gram_start()

    @pl.when(((r == 2) | (r == 6)) & (g > 0))
    def _():
        arrived(slot3, ("slot", 3))
        copy(slot3, slot3, ("slot", 3), me + 1, lambda: ((r == 2) | (r == 6)) & (g > 0))

        @pl.when(r == 2)
        def _():
            copy(slot3, slot3, ("slot", 3), me + 2, lambda: (r == 2) & (g > 0))

    @pl.when(r == 6)
    def _():
        arrived(slot2, ("slot", 2))
        copy(slot2, slot2, ("slot", 2), me + 1, lambda: r == 6)
        make_bt(2)
        t_from_slot(2)

    @pl.when((r == 5) | (r == 7))
    def _():
        arrived(slot2, ("slot", 2))
        make_bt(2)
        t_from_slot(2)

    @pl.when((r == 1) | (r == 5))
    def _():
        arrived(folds[1], ("fold", 1))
        t_from_fold(1)

    finish(1, 0)
    send(2, 0)

    @pl.when((r == 0) | (r == 2))
    def _():
        arrived(folds[2], ("fold", 2))
        copy(folds[2], folds[2], ("fold", 2), me + 1, lambda: (r == 0) | (r == 2))
        t_from_fold(2)

    finish(1, 1)
    send(2, 1)

    @pl.when((g > 0) & (core == 0))
    def _():
        @pl.when(r == 4)
        def _():
            arrived(slot3, ("slot", 3))
            copy(slot3, slot3, ("slot", 3), me + 1, lambda: (g > 0) & (r == 4))

        make_fold(row_fold, t_of(slot3))

        @pl.when(r > 0)
        def _():
            make_bt(3)

        if row_levels > 2:
            make_fold(row_fold_bt, bt_high[3].astype(F32) + bt_low[3].astype(F32))
        for k in range(row_levels):
            @pl.when(is_high(k))
            def _():
                c = functools.partial(lambda k: is_high(k) & (core == 0), k)
                name = ("fold", 3 + k)
                for j in range(max(1, (1 << k) // YDIM)):
                    copy(
                        row_fold, folds[3 + k], name,
                        me - (ROW << k) + j * YDIM * ROW, c,
                    )
                    if j:
                        copy(row_fold_bt, folds[3 + k], name, me + j * YDIM * ROW, c)

    give_back(1, 0)
    give_back(1, 1)

    @pl.when((r == 1) | (r == 3))
    def _():
        arrived(folds[2], ("fold", 2))
        t_from_fold(2)

    def rest_tile(tile):
        columns = pl.ds(tile * b, b)
        rest[:, columns] = c_ref[b:, columns] - dot3(lv_ref[b:, :], coef[:, columns])

    gram_sum_y()
    rest_tile(0)
    loads["inv"].wait()
    rest_basis[...] = dot3(rest[:, :b], inv_ref[...])
    for tile in range(1, nc // b):
        rest_tile(tile)

    @pl.when((g > 0) & (core == 1))
    def _():
        arrived(slot3, ("slot", 3))

    @pl.when((g > 0) & (core == 1))
    def _():
        make_bt(3)

    def send_z(k, chunk):
        rows = ROW_CHUNKS[chunk]
        source = zr.at[rows, :]

        @pl.when(is_high(k))
        def _():
            zr[rows, :] = times_bt(cur2[rows, :], 3)
            copy(
                source, inr.at[k, rows, :], ("z", k, chunk), me - (ROW << k),
                functools.partial(is_high, k),
            )

    def send_u(k, chunk):
        rows = ROW_CHUNKS[chunk]
        ahead = wr.at[k, rows, :]

        @pl.when(is_low(k))
        def _():
            wr[k, rows, :] = times_t(cur2[rows, :], 3 + k)
            copy(
                ahead, wbr.at[rows, :], ("wr", chunk), me + (ROW << k),
                functools.partial(is_low, k),
            )

    def finish_row(k, chunk):
        rows = ROW_CHUNKS[chunk]

        @pl.when(is_low(k))
        def _():
            arrived(inr.at[k, rows, :], ("z", k, chunk))
            cur2[rows, :] = cur2[rows, :] - (wr[k, rows, :] + inr[k, rows, :])

    PANEL = ROW_CHUNKS[0]

    def send_shared(k):
        ours = wr.at[k, PANEL, :]

        @pl.when(low_half(k))
        def _():
            value = cur2[PANEL, :]
            wr[k, PANEL, :] = value - times_t(value, 3 + k)
            copy(
                ours, inr.at[k, PANEL, :], ("z", k, 0), me + (ROW << k),
                functools.partial(low_half, k),
            )

        @pl.when(high_half(k))
        def _():
            wr[k, PANEL, :] = -times_t(cur2[PANEL, :], 3 + k)
            copy(
                ours, inr.at[k, PANEL, :], ("z", k, 0), me - (ROW << k),
                functools.partial(high_half, k),
            )

    def finish_shared(k):
        back = backs[k]

        @pl.when(y == 0)
        def _():
            arrived(inr.at[k, PANEL, :], ("z", k, 0))

        @pl.when(is_high(k))
        def _():
            res3[PANEL, :] = cur2[PANEL, :]

        @pl.when(is_low(k))
        def _():
            value = cur2[PANEL, :] - (wr[k, PANEL, :] + inr[k, PANEL, :])
            wback[k, :, :] = value
            copy(
                back, wbr.at[PANEL, :], ("wr", 0), me + (ROW << k),
                functools.partial(is_low, k),
            )

        @pl.when(y == 0)
        def _():
            cur2[PANEL, :] = wr[k, PANEL, :] + inr[k, PANEL, :]

    def send_level(k, chunk):
        if k > 1 and chunk == 0:
            send_shared(k)
        else:
            send_z(k, chunk)
            send_u(k, chunk)

    def finish_level(k, chunk):
        if k > 1 and chunk == 0:
            finish_shared(k)
        else:
            finish_row(k, chunk)

    def forward_operators(k):
        @pl.when(takes_fold(k) & (core == 0))
        def _():
            arrived(folds[3 + k], ("fold", 3 + k))
            copy(
                folds[3 + k], folds[3 + k], ("fold", 3 + k), me + 1,
                functools.partial(lambda k: takes_fold(k) & (core == 0), k),
            )

    def row_operators(k):
        @pl.when(takes_fold(k) & (core == 1))
        def _():
            arrived(folds[3 + k], ("fold", 3 + k))

        if k > 1:
            @pl.when(is_high(k))
            def _():
                make_fold(fold.at[3 + k], bt_high[3].astype(F32) + bt_low[3].astype(F32))

        @pl.when(takes_fold(k) if k < 2 else y == 0)
        def _():
            t_from_fold(3 + k)

    finish(2, 0)
    send_z(0, 0)
    finish(2, 1)
    send_z(0, 1)
    send_z(0, 2)
    forward_operators(0)
    give_back(2, 0)
    give_back(2, 1)

    row_operators(0)
    for chunk in range(3):
        send_u(0, chunk)

    def panel_to_row():
        for j in range(1, ROW):
            copy(
                panel.at[mine, :], panel.at[mine, :], ("panel",),
                base + (r + j) % ROW, lambda: y == 0,
            )

    def panel_out():
        @pl.when(y == 0)
        def _():
            panel[mine, :] = cur2[PANEL, :]
            for j in range(1, YDIM):
                copy(
                    panel.at[mine, :], panel.at[mine, :], ("panel y",), y_mate(j),
                    lambda: y == 0,
                )
            panel_to_row()

    def gather_row(result, chunk, condition):
        for rank in range(ROW):
            start = place(3, rank, min(chunk, 1)).start
            start += eighth_b // 2 if chunk == 2 else 0
            rows = pl.ds(start, ROW_CHUNKS[chunk].size)

            @pl.when(r == rank)
            def _():
                if rank == 0:
                    gathered[rows, :] = result[ROW_CHUNKS[chunk], :]
                else:
                    copy(
                        result.at[ROW_CHUNKS[chunk], :], gathered.at[rows, :],
                        ("gather",), base,
                        functools.partial(lambda o: condition() & (r == o), rank),
                    )

    events = []
    for k in range(row_levels):
        events += [(2.9 * k + (5.0 if k > 3 else 0.0), k, 0)]
        events += [(2.0 + 4.2 * k, k, 1), (2.9 + 4.2 * k, k, 2)]
    done = set()
    last = row_levels - 1
    for _, k, chunk in sorted(events):
        if k < last and chunk == 0:
            forward_operators(k + 1)
        finish_level(k, chunk)
        if k < last:
            if chunk == 0:
                row_operators(k + 1)
            send_level(k + 1, chunk)
        done.add((k, chunk))
        if (k, chunk) == (last, 0):
            panel_out()
        if k == last:
            @pl.when(g == 0)
            def _():
                gather_row(cur2, chunk, lambda: g == 0)
        if (k, chunk) == (0, 2):
            gram_sum_z()
            residual(0, gathered)
            residual(1, res1)
            for rank, into in ((2, 2), (3, 2), (6, 6), (7, 6)):
                @pl.when(r == rank)
                def _():
                    gather(1, res1, rank, into, CHUNKS, functools.partial(lambda o: r == o, rank))
        if (k, chunk) == (1, 2):
            residual(2, res2)
            for rank in range(4, ROW):
                @pl.when(r == rank)
                def _():
                    gather(2, res2, rank, 4, CHUNKS, functools.partial(lambda o: r == o, rank))
            gram_sum_x()
        if (k, chunk) == (min(last, 3), 2):
            gram_all_y()

    def row_result(chunk):
        rows = ROW_CHUNKS[chunk]

        @pl.when(g > 0)
        def _():
            vt = halves(vt_of(slot3))
            arrived(wbr.at[rows, :], ("wr", chunk))
            value = wbr[rows, :]
            if chunk or row_levels < 3:
                value = value + zr[rows, :]
                res3[rows, :] = cur2[rows, :] - dot_pairs(halves(value), vt)
            else:
                shared = y == 0
                value = jnp.where(shared, value, value + zr[rows, :])
                start = jnp.where(shared, res3[rows, :], cur2[rows, :])
                res3[rows, :] = start - dot_pairs(halves(value), vt)
            gather_row(res3, chunk, lambda: g > 0)

    for chunk in (1, 2, 0):
        row_result(chunk)

    @pl.when(y != 0)
    def _():
        arrived(panel.at[mine, :], ("panel y",))
        for j in range(1, ROW):
            copy(
                panel.at[mine, :], panel.at[mine, :], ("panel",),
                base + (r + j) % ROW, lambda: y != 0,
            )

    @pl.when((r == 2) | (r == 6))
    def _():
        arrived(gathered.at[pl.ds(0, nc // 2), :], ("gather",))

    @pl.when(r == 4)
    def _():
        arrived(gathered.at[pl.ds(0, 3 * nc // 4), :], ("gather",))

    @pl.when(r == 0)
    def _():
        arrived(gathered.at[pl.ds(0, 7 * nc // 8), :], ("gather",))

    head_rows[...] = gathered[...].T
    head_basis[...] = jnp.where(me == 0, 0.0, dot3(head_rows[:, :b], inv_ref[...]))
    arrived(gram_all.at[pl.ds(0, b - yrows), :], ("all y",))
    arrived(panel.at[pl.ds(0, b - piece), :], ("panel",))
    square = dot3(panel[...], panel[...], True)
    gram_total[...] = (gram_all[...] - square) / float(total_rows)

    for condition, source in pending:
        made = functools.partial(
            lambda source: remote(source, source, 0, neighbour).wait_send(), source
        )
        if condition is None:
            made()
        else:
            @pl.when(condition())
            def _():
                made()
    assert len(numbers) <= recv_sems.shape[0]


def write_kernel(
    head_rows, rest, head_basis, rest_basis, gram, upd_out, basis_out, gram_out, sems
):
    b = head_rows.shape[0]
    copies = [
        pltpu.make_async_copy(source, target, sems.at[index])
        for index, (source, target) in enumerate((
            (head_rows, upd_out.at[pl.ds(0, b), :]),
            (rest, upd_out.at[pl.ds(b, b), :]),
            (head_basis, basis_out.at[pl.ds(0, b), :]),
            (rest_basis, basis_out.at[pl.ds(b, b), :]),
            (gram, gram_out),
        ))
    ]
    for made in copies:
        made.start()
    for made in copies:
        made.wait()


def body(trailing, leaf_vectors, leaf_factors, tree_vectors, tree_factors, inverse_factor):
    b, nc = leaf_vectors.shape[1], trailing.shape[1]
    devices = lax.axis_size("rows")
    total_rows = trailing.shape[0] * devices
    levels = (devices // ROW).bit_length() - 1
    piece = b // ROW
    zdim = devices // ROW // YDIM

    def vmem(*shape, dtype=F32):
        return pltpu.VMEM(shape, dtype)

    arguments = (
        trailing, leaf_vectors, leaf_factors, tree_vectors, tree_factors, inverse_factor
    )
    per_level = [vmem(nc >> level, b) for level in (1, 2, 3)]
    scratch = [
        *[vmem(*argument.shape) for argument in arguments],
        vmem(b + 8, b),
        vmem(b // 2 + 8, b),
        *[vmem(b + 8, b)] * 4,
        vmem(3 + levels, b // 2 + 8, b),
        vmem(b // 2 + 8, b), vmem(b // 2 + 8, b),
        vmem(3 + levels, b, b, dtype=BF16),
        vmem(3 + levels, b, b, dtype=BF16),
        vmem(4, b, b, dtype=BF16),
        vmem(4, b, b, dtype=BF16),
        vmem(nc, b),
        *per_level,
        *per_level, *per_level, *per_level, *per_level,
        vmem(nc // 8, b), vmem(levels, nc // 8, b), vmem(levels, nc // 8, b),
        vmem(nc // 8, b),
        *per_level,
        vmem(nc, b),
        vmem(b, nc),
        vmem(b, 2 * b, dtype=BF16), vmem(b, 2 * b, dtype=BF16),
        vmem(b, b),
        vmem(b // YDIM, b),
        vmem(YDIM - 1, b // YDIM, b),
        vmem(max(zdim - 1, 1), b // YDIM // zdim, b),
        vmem(ROW, b // YDIM // zdim, b),
        vmem(b, b), vmem(b, b),
        vmem(levels, piece, b),
        pltpu.SemaphoreType.DMA,
        pltpu.SemaphoreType.DMA((RECEIVES,)),
        pltpu.SemaphoreType.DMA((7,)),
    ]
    results = pl.pallas_call(
        functools.partial(tree_kernel, devices, total_rows),
        out_shape=(
            vmem(b, nc), vmem(b, nc), vmem(b, b), vmem(b, b), vmem(b, b)
        ),
        in_specs=[pl.BlockSpec(memory_space=pltpu.HBM)] * 6,
        out_specs=[pl.BlockSpec(memory_space=pltpu.VMEM)] * 5,
        scratch_shapes=scratch,
        compiler_params=pltpu.CompilerParams(
            collective_id=0,
            has_side_effects=True,
            vmem_limit_bytes=56 * 1024 * 1024,
        ),
        name="tree",
    )(*arguments)
    return pl.pallas_call(
        write_kernel,
        out_shape=(
            jax.ShapeDtypeStruct(trailing.shape, F32),
            jax.ShapeDtypeStruct(leaf_vectors.shape, F32),
            jax.ShapeDtypeStruct((b, b), F32),
        ),
        in_specs=[pl.BlockSpec(memory_space=pltpu.VMEM)] * 5,
        out_specs=[pl.BlockSpec(memory_space=pl.ANY)] * 3,
        scratch_shapes=[pltpu.SemaphoreType.DMA((5,))],
        name="write",
    )(*[pltpu.with_memory_space_constraint(result, pltpu.VMEM) for result in results])


def solution(mesh):
    rows = P("rows", None)
    return jax.shard_map(
        body,
        mesh=mesh,
        in_specs=(rows, rows, rows, rows, rows, P()),
        out_specs=(rows, rows, P()),
        check_vma=False,
    )
```

```python
import functools

import jax
import jax.numpy as jnp
from jax import lax
from jax.experimental import pallas as pl
from jax.experimental.pallas import tpu as pltpu
from jax.sharding import PartitionSpec as P

F32 = jnp.float32
BF16 = jnp.bfloat16
ROW = 8
YDIM = 4
MESH = pl.DeviceIdType.MESH
RECEIVES = 56


def halves(value):
    high = value.astype(BF16)
    low = (value - high.astype(F32)).astype(BF16)
    return high, low


def dot_pairs(left, right, transposed=False):
    dims = (((1,), (1 if transposed else 0,)), ((), ()))

    def one(a, b):
        return lax.dot_general(a, b, dims, preferred_element_type=F32)

    return one(left[0], right[0]) + (one(left[0], right[1]) + one(left[1], right[0]))


def dot3(left_side, right_side, transposed=False):
    return dot_pairs(halves(left_side), halves(right_side), transposed)


def tree_kernel(
    devices,
    total_rows,
    c_hbm, lv_hbm, lt_hbm, tv_hbm, tt_hbm, inv_hbm,
    head_rows, rest, head_basis, rest_basis, gram_total,
    c_ref, lv_ref, lt_ref, tv_ref, tt_ref, inv_ref,
    pack,
    folded,
    slot0, slot1, slot2, slot3,
    fold,
    row_fold, row_fold_bt,
    t_high, t_low,
    bt_high, bt_low,
    head,
    cur0, cur1, cur2,
    z0, z1, z2, in0, in1, in2, w0, w1, w2, wb0, wb1, wb2,
    zr, inr, wr, wbr,
    res1, res2, res3,
    gathered,
    coef,
    lvt_high, lvt_low,
    gram_own, gram_piece, gram_y, gram_z, gram_x, panel, gram_all, wback,
    send_sem, recv_sems, local_sems,
):
    b = pack.shape[1]
    hb = b // 2
    nc = c_ref.shape[1]
    row_count = devices // ROW
    row_levels = row_count.bit_length() - 1
    zdim = row_count // YDIM
    piece = b // ROW
    me = lax.axis_index("rows")
    r = me % ROW
    g = me // ROW
    core = r % 2
    x0 = (r // 2) % 2
    x1 = r // 4
    bits = (core, x0, x1)
    base = g * ROW
    y = g % YDIM
    z = g // YDIM
    twin = base + r + 1 - 2 * core
    neighbour = base + (r + 1) % ROW

    def y_mate(j):
        return (z * YDIM + (y + j) % YDIM) * ROW + r

    def z_mate(j):
        return ((z + j) % zdim * YDIM + y) * ROW + r

    cur = (cur0, cur1, cur2)
    zs, ins, ws, wbs = (z0, z1, z2), (in0, in1, in2), (w0, w1, w2), (wb0, wb1, wb2)
    slot = (slot0, slot1, slot2, slot3)
    folds = [fold.at[i] for i in range(3 + row_levels)]
    CHUNKS = (0, 1)
    eighth_b = (nc - b) // 8
    ROW_CHUNKS = (
        pl.ds(0, piece),
        pl.ds(piece, eighth_b // 2),
        pl.ds(piece + eighth_b // 2, eighth_b // 2),
    )

    def slice_of(rank):
        return rank % 2 * 4 + rank // 2 % 2 * 2 + rank // 4

    def piece_of(rank):
        return pl.ds(pl.multiple_of(slice_of(rank) * piece, piece), piece)

    mine = piece_of(r)

    def size(level, chunk):
        return ((nc - b) // 2 if chunk else b // 2) >> level

    def own(level, chunk):
        return pl.ds((b // 2 >> level) if chunk else 0, size(level, chunk))

    def part(level, chunk, upper):
        start = (b >> level) if chunk else 0
        return pl.ds(start + (size(level, chunk) if upper else 0), size(level, chunk))

    def parent(level):
        return cur[level - 1] if level else head

    def is_low(k):
        return g % (2 << k) == 0

    def is_high(k):
        return g % (2 << k) == (1 << k)

    def low_half(k):
        return is_low(k) if k < 2 else (y == 0) & (g // (1 << k) % 2 == 0)

    def high_half(k):
        return is_high(k) if k < 2 else (y == 0) & (g // (1 << k) % 2 == 1)

    def takes_fold(k):
        return is_low(k) if k < 2 else (y == 0) & jnp.logical_not(is_high(k))

    backs = [wback.at[k] for k in range(row_levels)]

    loads = {}
    for name, source, target in (
        ("tv", tv_hbm, tv_ref),
        ("tt", tt_hbm, tt_ref),
        ("lv", lv_hbm, lv_ref),
        ("c0", c_hbm.at[:, pl.ds(0, b)], c_ref.at[:, pl.ds(0, b)]),
        ("lt", lt_hbm, lt_ref),
        ("c1", c_hbm.at[:, pl.ds(b, nc - b)], c_ref.at[:, pl.ds(b, nc - b)]),
        ("inv", inv_hbm, inv_ref),
    ):
        loads[name] = pltpu.make_async_copy(source, target, local_sems.at[len(loads)])
        loads[name].start()

    barrier = pltpu.get_barrier_semaphore()

    def greet(other):
        pl.semaphore_signal(barrier, inc=1, device_id=(other,), device_id_type=MESH)

    for j in range(1, ROW):
        greet(base + (r + j) % ROW)
    for j in range(1, YDIM):
        greet(y_mate(j))
    for j in range(1, zdim):
        greet(z_mate(j))

    def entered():
        pl.semaphore_wait(barrier, ROW - 1 + YDIM - 1 + zdim - 1)

    numbers = {}
    pending = []

    def number(*name):
        return numbers.setdefault(name, len(numbers))

    def remote(source, target, receive, other):
        return pltpu.make_async_remote_copy(
            src_ref=source,
            dst_ref=target,
            send_sem=send_sem,
            recv_sem=recv_sems.at[receive],
            device_id=(other,),
            device_id_type=MESH,
        )

    def copy(source, target, name, other, condition=None):
        remote(source, target, number(*name), other).start()
        pending.append((condition, source))

    def arrived(target, name):
        remote(target, target, number(*name), neighbour).wait_recv()

    row_id = lax.broadcasted_iota(jnp.int32, (b, b), 0)
    col_id = lax.broadcasted_iota(jnp.int32, (b, b), 1)
    row_half = lax.broadcasted_iota(jnp.int32, (hb, hb), 0)
    col_half = lax.broadcasted_iota(jnp.int32, (hb, hb), 1)

    def t_of(ref):
        return jnp.where(row_id <= col_id, ref[:b, :], 0.0)

    def vt_of(ref):
        diagonal = jnp.where(row_id == col_id, ref[b : b + 1, :], 0.0)
        return jnp.where(row_id > col_id, ref[:b, :], diagonal)

    def make_fold(target, t):
        last = t[hb:, hb:]
        target[:hb, :hb] = jnp.where(row_half <= col_half, t[:hb, :hb], last.T)
        target[:hb, hb:] = t[:hb, hb:]
        diagonal = jnp.sum(
            jnp.where(row_half == col_half, last, 0.0), axis=0, keepdims=True
        )
        target[hb:, :hb] = jnp.broadcast_to(diagonal, (8, hb))
        target[hb:, hb:] = jnp.zeros((8, hb), F32)

    def store_t(index, value, rows, columns):
        high, low = halves(value)
        t_high[index, rows, columns] = high
        t_low[index, rows, columns] = low

    FIRST, LAST = pl.ds(0, hb), pl.ds(hb, hb)

    def t_from_fold(index):
        first = fold[index, :hb, :hb]
        store_t(index, jnp.where(row_half <= col_half, first, 0.0), FIRST, FIRST)
        store_t(index, fold[index, :hb, hb:], FIRST, LAST)
        store_t(index, jnp.zeros((hb, hb), F32), LAST, FIRST)
        diagonal = jnp.where(row_half == col_half, fold[index, hb : hb + 1, :hb], 0.0)
        last = jnp.where(row_half < col_half, first.T, diagonal)
        store_t(index, last, LAST, LAST)

    def t_from_slot(index):
        store_t(index, t_of(slot[index]), pl.ds(0, b), pl.ds(0, b))

    def make_bt(index):
        high, low = halves(dot3(vt_of(slot[index]).T, t_of(slot[index])))
        bt_high[index] = high
        bt_low[index] = low

    def times_bt(value, index):
        return dot_pairs(halves(value), (bt_high[index], bt_low[index]))

    def times_t(value, index):
        return dot_pairs(halves(value), (t_high[index], t_low[index]))

    loads["tv"].wait()
    loads["tt"].wait()
    tv = tv_ref[...]
    tt = tt_ref[...]
    pack[:b, :] = jnp.where(row_id <= col_id, tt, tv.T)
    diagonal = jnp.sum(jnp.where(row_id == col_id, tv, 0.0), axis=0, keepdims=True)
    pack[b:, :] = jnp.broadcast_to(diagonal, (8, b))
    make_fold(folded, tt)

    for condition, index in (
        (core == 1, 0), ((r == 2) | (r == 6), 1), (r == 4, 2), ((r == 0) & (g > 0), 3),
    ):
        @pl.when(condition)
        def _():
            slot[index][...] = pack[...]
            make_bt(index)
            if index < 3:
                t_from_slot(index)

    loads["lv"].wait()
    high, low = halves(lv_ref[...].T)
    lvt_high[...] = high
    lvt_low[...] = low

    def leaf_tile(tile):
        columns = pl.ds(tile * b, b)
        inner = dot_pairs((lvt_high[...], lvt_low[...]), halves(c_ref[:, columns]))
        coeffs = dot3(lt_ref[...].T, inner)
        coef[:, columns] = coeffs
        result = c_ref[:b, columns] - dot3(lv_ref[:b, :], coeffs)
        head[columns, :] = result.T

    loads["c0"].wait()
    loads["lt"].wait()
    leaf_tile(0)
    entered()

    @pl.when(core == 1)
    def _():
        copy(folded, folds[0], ("fold", 0), me - 1, lambda: core == 1)

    @pl.when((r == 2) | (r == 6))
    def _():
        c = lambda: (r == 2) | (r == 6)
        copy(pack, slot1, ("slot", 1), me + 1, c)
        copy(folded, folds[1], ("fold", 1), me - 2, c)

    @pl.when(r == 4)
    def _():
        copy(folded, folds[2], ("fold", 2), base, lambda: r == 4)
        copy(pack, slot2, ("slot", 2), base + 5, lambda: r == 4)
        copy(folded, folds[2], ("fold", 2), base + 2, lambda: r == 4)
        copy(pack, slot2, ("slot", 2), base + 6, lambda: r == 4)

    @pl.when((r == 0) & (g > 0))
    def _():
        for other in (1, 2, 6):
            copy(pack, slot3, ("slot", 3), base + other, lambda: (r == 0) & (g > 0))

    def send(level, chunk):
        bit, far = bits[level], 1 << level
        rows, name = own(level, chunk), ("x", level, chunk)
        target = ins[level].at[rows, :]
        low_rows, high_rows = part(level, chunk, False), part(level, chunk, True)

        @pl.when(bit == 0)
        def _():
            copy(
                parent(level).at[high_rows, :], target, name, me + far,
                lambda: bits[level] == 0,
            )

        source = zs[level].at[rows, :]

        @pl.when(bit == 1)
        def _():
            zs[level][rows, :] = times_bt(parent(level)[low_rows, :], level)
            copy(source, target, name, me - far, lambda: bits[level] == 1)

    def finish(level, chunk):
        bit = bits[level]
        rows, name = own(level, chunk), ("x", level, chunk)
        low_rows, high_rows = part(level, chunk, False), part(level, chunk, True)

        @pl.when(bit == 0)
        def _():
            value = parent(level)[low_rows, :]
            update = times_t(value, level)
            arrived(ins[level].at[rows, :], name)
            update = update + ins[level][rows, :]
            cur[level][rows, :] = value - update
            ws[level][rows, :] = update

        @pl.when(bit == 1)
        def _():
            update = times_bt(parent(level)[high_rows, :], level)
            arrived(ins[level].at[rows, :], name)
            value = ins[level][rows, :]
            update = update + times_t(value, level)
            cur[level][rows, :] = value - update
            ws[level][rows, :] = update

    def give_back(level, chunk):
        rows = own(level, chunk)

        @pl.when(bits[level] == 0)
        def _():
            copy(
                ws[level].at[rows, :], wbs[level].at[rows, :], ("w", level, chunk),
                me + (1 << level), lambda: bits[level] == 0,
            )

    def residual(level, result):
        @pl.when(bits[level] == 1)
        def _():
            vt = halves(vt_of(slot[level]))
            for chunk in CHUNKS:
                rows = own(level, chunk)
                low_rows, high_rows = part(level, chunk, False), part(level, chunk, True)
                result[high_rows, :] = parent(level)[high_rows, :] - dot_pairs(
                    halves(ws[level][rows, :]), vt
                )
                arrived(wbs[level].at[rows, :], ("w", level, chunk))
                result[low_rows, :] = parent(level)[low_rows, :] - dot_pairs(
                    halves(wbs[level][rows, :]), vt
                )

    def place(level, rank, chunk):
        start = b if chunk else 0
        for bit in range(level):
            start += (rank >> bit & 1) * size(bit, chunk)
        return pl.ds(start, size(level - 1, chunk))

    def buffer_rows(level, chunk):
        return pl.ds((b >> level) if chunk else 0, size(level - 1, chunk))

    def gather(level, result, rank, into, chunks, condition):
        for chunk in chunks:
            if rank == into:
                gathered[place(level, rank, chunk), :] = result[buffer_rows(level, chunk), :]
            else:
                copy(
                    result.at[buffer_rows(level, chunk), :],
                    gathered.at[place(level, rank, chunk), :],
                    ("gather",), base + into, condition,
                )

    yrows, zrows = b // YDIM, b // YDIM // zdim

    def block_y(other):
        return pl.ds(pl.multiple_of(other * yrows, yrows), yrows)

    def block_z(other):
        return pl.ds(pl.multiple_of(other * zrows, zrows), zrows)

    my_rows = pl.ds(pl.multiple_of(y * yrows + z * zrows, zrows), zrows)

    def gram_start():
        columns = c_ref[:, :b]
        gram_own[...] = dot3(columns.T, columns)
        for j in range(1, YDIM):
            copy(
                gram_own.at[block_y((y + j) % YDIM), :], gram_y.at[YDIM - j - 1],
                ("gram y",), y_mate(j),
            )

    def gram_sum_y():
        arrived(gram_y, ("gram y",))
        total = gram_own[block_y(y), :]
        for j in range(YDIM - 1):
            total = total + gram_y[j]
        gram_piece[...] = total
        for j in range(1, zdim):
            copy(
                gram_piece.at[block_z((z + j) % zdim), :], gram_z.at[zdim - j - 1],
                ("gram z",), z_mate(j),
            )

    mine_x = gram_x.at[r]

    def gram_sum_z():
        total = gram_piece[block_z(z), :]
        if zdim > 1:
            arrived(gram_z, ("gram z",))
        for j in range(zdim - 1):
            total = total + gram_z[j]
        gram_x[r] = total
        for j in range(1, ROW):
            copy(
                mine_x, mine_x, ("gram x",), base + (r + j) % ROW,
            )

    def gram_sum_x():
        arrived(gram_x.at[pl.ds(0, ROW - 1)], ("gram x",))
        total = gram_x[0]
        for j in range(1, ROW):
            total = total + gram_x[j]
        gram_all[my_rows, :] = total
        for j in range(1, zdim):
            copy(
                gram_all.at[my_rows, :], gram_all.at[my_rows, :], ("all z",), z_mate(j),
            )

    def gram_all_y():
        if zdim > 1:
            arrived(gram_all.at[pl.ds(0, yrows - zrows), :], ("all z",))
        for j in range(1, YDIM):
            copy(
                gram_all.at[block_y(y), :], gram_all.at[block_y(y), :], ("all y",),
                y_mate(j),
            )

    send(0, 0)
    loads["c1"].wait()
    for tile in range(1, nc // b):
        leaf_tile(tile)
    send(0, 1)

    @pl.when(core == 0)
    def _():
        arrived(folds[0], ("fold", 0))
        t_from_fold(0)

    finish(0, 0)

    @pl.when((r == 3) | (r == 7))
    def _():
        arrived(slot1, ("slot", 1))
        make_bt(1)
        t_from_slot(1)

    send(1, 0)
    finish(0, 1)
    send(1, 1)

    @pl.when((r == 0) | (r == 4))
    def _():
        arrived(folds[1], ("fold", 1))
        copy(folds[1], folds[1], ("fold", 1), me + 1, lambda: (r == 0) | (r == 4))
        t_from_fold(1)

    give_back(0, 0)
    give_back(0, 1)
    gram_start()

    @pl.when(((r == 2) | (r == 6)) & (g > 0))
    def _():
        arrived(slot3, ("slot", 3))
        copy(slot3, slot3, ("slot", 3), me + 1, lambda: ((r == 2) | (r == 6)) & (g > 0))

        @pl.when(r == 2)
        def _():
            copy(slot3, slot3, ("slot", 3), me + 2, lambda: (r == 2) & (g > 0))

    @pl.when(r == 6)
    def _():
        arrived(slot2, ("slot", 2))
        copy(slot2, slot2, ("slot", 2), me + 1, lambda: r == 6)
        make_bt(2)
        t_from_slot(2)

    @pl.when((r == 5) | (r == 7))
    def _():
        arrived(slot2, ("slot", 2))
        make_bt(2)
        t_from_slot(2)

    @pl.when((r == 1) | (r == 5))
    def _():
        arrived(folds[1], ("fold", 1))
        t_from_fold(1)

    finish(1, 0)
    send(2, 0)

    @pl.when((r == 0) | (r == 2))
    def _():
        arrived(folds[2], ("fold", 2))
        copy(folds[2], folds[2], ("fold", 2), me + 1, lambda: (r == 0) | (r == 2))
        t_from_fold(2)

    finish(1, 1)
    send(2, 1)

    @pl.when((g > 0) & (core == 0))
    def _():
        @pl.when(r == 4)
        def _():
            arrived(slot3, ("slot", 3))
            copy(slot3, slot3, ("slot", 3), me + 1, lambda: (g > 0) & (r == 4))

        make_fold(row_fold, t_of(slot3))

        @pl.when(r > 0)
        def _():
            make_bt(3)

        if row_levels > 2:
            make_fold(row_fold_bt, bt_high[3].astype(F32) + bt_low[3].astype(F32))
        for k in range(row_levels):
            @pl.when(is_high(k))
            def _():
                c = functools.partial(lambda k: is_high(k) & (core == 0), k)
                name = ("fold", 3 + k)
                for j in range(max(1, (1 << k) // YDIM)):
                    copy(
                        row_fold, folds[3 + k], name,
                        me - (ROW << k) + j * YDIM * ROW, c,
                    )
                    if j:
                        copy(row_fold_bt, folds[3 + k], name, me + j * YDIM * ROW, c)

    give_back(1, 0)
    give_back(1, 1)

    @pl.when((r == 1) | (r == 3))
    def _():
        arrived(folds[2], ("fold", 2))
        t_from_fold(2)

    def rest_tile(tile):
        columns = pl.ds(tile * b, b)
        rest[:, columns] = c_ref[b:, columns] - dot3(lv_ref[b:, :], coef[:, columns])

    gram_sum_y()
    rest_tile(0)
    loads["inv"].wait()
    rest_basis[...] = dot3(rest[:, :b], inv_ref[...])
    for tile in range(1, nc // b):
        rest_tile(tile)

    @pl.when((g > 0) & (core == 1))
    def _():
        arrived(slot3, ("slot", 3))

    @pl.when((g > 0) & (core == 1))
    def _():
        make_bt(3)

    def send_z(k, chunk):
        rows = ROW_CHUNKS[chunk]
        source = zr.at[rows, :]

        @pl.when(is_high(k))
        def _():
            zr[rows, :] = times_bt(cur2[rows, :], 3)
            copy(
                source, inr.at[k, rows, :], ("z", k, chunk), me - (ROW << k),
                functools.partial(is_high, k),
            )

    def send_u(k, chunk):
        rows = ROW_CHUNKS[chunk]
        ahead = wr.at[k, rows, :]

        @pl.when(is_low(k))
        def _():
            wr[k, rows, :] = times_t(cur2[rows, :], 3 + k)
            copy(
                ahead, wbr.at[rows, :], ("wr", chunk), me + (ROW << k),
                functools.partial(is_low, k),
            )

    def finish_row(k, chunk):
        rows = ROW_CHUNKS[chunk]

        @pl.when(is_low(k))
        def _():
            arrived(inr.at[k, rows, :], ("z", k, chunk))
            cur2[rows, :] = cur2[rows, :] - (wr[k, rows, :] + inr[k, rows, :])

    PANEL = ROW_CHUNKS[0]

    def send_shared(k):
        ours, ahead = wr.at[k, PANEL, :], backs[k]

        @pl.when(low_half(k))
        def _():
            value = cur2[PANEL, :]
            update = times_t(value, 3 + k)
            wr[k, PANEL, :] = value - update
            if k != 4:
                copy(
                    ours, inr.at[k, PANEL, :], ("z", k, 0), me + (ROW << k),
                    functools.partial(low_half, k),
                )

            @pl.when(is_low(k))
            def _():
                wback[k, :, :] = update
                copy(
                    ahead, wbr.at[PANEL, :], ("wr", 0), me + (ROW << k),
                    functools.partial(is_low, k),
                )

        @pl.when(high_half(k))
        def _():
            update = times_t(cur2[PANEL, :], 3 + k)
            wr[k, PANEL, :] = -update

            @pl.when(is_high(k))
            def _():
                zr[PANEL, :] = update
                res3[PANEL, :] = cur2[PANEL, :]

            if k != 4:
                copy(
                    ours, inr.at[k, PANEL, :], ("z", k, 0), me - (ROW << k),
                    functools.partial(high_half, k),
                )

        if k == 4:
            for source, targets in ((7, (1, 0)), (4, (2, 3)), (3, (5, 4)), (0, (6, 7))):
                @pl.when((y == 0) & (z == source))
                def _():
                    for target in targets:
                        copy(
                            ours, inr.at[k, PANEL, :], ("z", k, 0),
                            target * YDIM * ROW + r,
                            functools.partial(lambda o: (y == 0) & (z == o), source),
                        )

    def finish_shared(k):
        @pl.when(y == 0)
        def _():
            arrived(inr.at[k, PANEL, :], ("z", k, 0))
            cur2[PANEL, :] = wr[k, PANEL, :] + inr[k, PANEL, :]

    def send_level(k, chunk):
        if k > 1 and chunk == 0:
            send_shared(k)
        else:
            send_z(k, chunk)
            send_u(k, chunk)

    def finish_level(k, chunk):
        if k > 1 and chunk == 0:
            finish_shared(k)
        else:
            finish_row(k, chunk)

    def forward_operators(k):
        @pl.when(takes_fold(k) & (core == 0))
        def _():
            arrived(folds[3 + k], ("fold", 3 + k))
            copy(
                folds[3 + k], folds[3 + k], ("fold", 3 + k), me + 1,
                functools.partial(lambda k: takes_fold(k) & (core == 0), k),
            )

    def row_operators(k):
        @pl.when(takes_fold(k) & (core == 1))
        def _():
            arrived(folds[3 + k], ("fold", 3 + k))

        if k > 1:
            @pl.when(is_high(k))
            def _():
                make_fold(fold.at[3 + k], bt_high[3].astype(F32) + bt_low[3].astype(F32))

        @pl.when(takes_fold(k) if k < 2 else y == 0)
        def _():
            t_from_fold(3 + k)

    finish(2, 0)
    send_z(0, 0)
    finish(2, 1)
    send_z(0, 1)
    send_z(0, 2)
    forward_operators(0)
    give_back(2, 0)
    give_back(2, 1)

    row_operators(0)
    for chunk in range(3):
        send_u(0, chunk)

    def panel_to_row(condition):
        copy(panel.at[mine, :], panel.at[mine, :], ("panel core",), twin, condition)
        for j in (4, 2, 6):
            copy(
                panel.at[mine, :], panel.at[mine, :], ("panel",),
                base + (r + j) % ROW, condition,
            )

    def panel_out():
        @pl.when(y == 0)
        def _():
            panel[mine, :] = cur2[PANEL, :]
            for j in range(1, YDIM):
                copy(
                    panel.at[mine, :], panel.at[mine, :], ("panel y",), y_mate(j),
                    lambda: y == 0,
                )
            panel_to_row(lambda: y == 0)

    def gather_row(result, chunk, condition):
        for rank in range(ROW):
            start = place(3, rank, min(chunk, 1)).start
            start += eighth_b // 2 if chunk == 2 else 0
            rows = pl.ds(start, ROW_CHUNKS[chunk].size)

            @pl.when(r == rank)
            def _():
                if rank == 0:
                    gathered[rows, :] = result[ROW_CHUNKS[chunk], :]
                else:
                    copy(
                        result.at[ROW_CHUNKS[chunk], :], gathered.at[rows, :],
                        ("gather",), base,
                        functools.partial(lambda o: condition() & (r == o), rank),
                    )

    def row_result(k):
        for chunk in (1, 2, 0):
            rows = ROW_CHUNKS[chunk]

            @pl.when(is_high(k))
            def _():
                vt = halves(vt_of(slot3))
                arrived(wbr.at[rows, :], ("wr", chunk))
                start = res3 if k > 1 and chunk == 0 else cur2
                res3[rows, :] = start[rows, :] - dot_pairs(
                    halves(wbr[rows, :] + zr[rows, :]), vt
                )
                gather_row(res3, chunk, functools.partial(is_high, k))

    events = []
    for k in range(row_levels):
        events += [(2.9 * k + (5.0 if k > 3 else 0.0), k, 0)]
        events += [(2.0 + 4.2 * k, k, 1), (2.9 + 4.2 * k, k, 2)]
    done = set()
    last = row_levels - 1
    for _, k, chunk in sorted(events):
        if k < last and chunk == 0:
            forward_operators(k + 1)
        finish_level(k, chunk)
        if k < last:
            if chunk == 0:
                row_operators(k + 1)
            send_level(k + 1, chunk)
        done.add((k, chunk))
        if (k, chunk) == (last, 0):
            panel_out()
        if (k, chunk) == (last, 0 if last > 3 else 2):
            gram_all_y()
        if k == last:
            @pl.when(g == 0)
            def _():
                gather_row(cur2, chunk, lambda: g == 0)
        if (k, chunk) == (0, 2):
            gram_sum_z()
            residual(0, gathered)
            residual(1, res1)
            for rank, into in ((2, 2), (3, 2), (6, 6), (7, 6)):
                @pl.when(r == rank)
                def _():
                    gather(1, res1, rank, into, CHUNKS, functools.partial(lambda o: r == o, rank))
        if (k, chunk) == (1, 2):
            residual(2, res2)
            for rank in range(4, ROW):
                @pl.when(r == rank)
                def _():
                    gather(2, res2, rank, 4, CHUNKS, functools.partial(lambda o: r == o, rank))
            gram_sum_x()
        if k and chunk == 2:
            row_result(k - 1)
        if (k, chunk) == (last, 2):
            row_result(last)

    @pl.when(y != 0)
    def _():
        arrived(panel.at[mine, :], ("panel y",))
        panel_to_row(lambda: y != 0)

    arrived(panel.at[pl.ds(0, 3 * piece), :], ("panel",))
    for j in (2, 6, 4):
        theirs = piece_of((r + j) % ROW)
        copy(panel.at[theirs, :], panel.at[theirs, :], ("panel core",), twin)

    @pl.when((r == 2) | (r == 6))
    def _():
        arrived(gathered.at[pl.ds(0, nc // 2), :], ("gather",))

    @pl.when(r == 4)
    def _():
        arrived(gathered.at[pl.ds(0, 3 * nc // 4), :], ("gather",))

    @pl.when(r == 0)
    def _():
        arrived(gathered.at[pl.ds(0, 7 * nc // 8), :], ("gather",))

    head_rows[...] = gathered[...].T
    head_basis[...] = jnp.where(me == 0, 0.0, dot3(head_rows[:, :b], inv_ref[...]))
    arrived(gram_all.at[pl.ds(0, b - yrows), :], ("all y",))
    arrived(panel.at[pl.ds(0, 4 * piece), :], ("panel core",))
    square = dot3(panel[...], panel[...], True)
    gram_total[...] = (gram_all[...] - square) / float(total_rows)

    for condition, source in pending:
        made = functools.partial(
            lambda source: remote(source, source, 0, neighbour).wait_send(), source
        )
        if condition is None:
            made()
        else:
            @pl.when(condition())
            def _():
                made()
    assert len(numbers) <= recv_sems.shape[0]


def write_kernel(
    head_rows, rest, head_basis, rest_basis, gram, upd_out, basis_out, gram_out, sems
):
    b = head_rows.shape[0]
    copies = [
        pltpu.make_async_copy(source, target, sems.at[index])
        for index, (source, target) in enumerate((
            (head_rows, upd_out.at[pl.ds(0, b), :]),
            (rest, upd_out.at[pl.ds(b, b), :]),
            (head_basis, basis_out.at[pl.ds(0, b), :]),
            (rest_basis, basis_out.at[pl.ds(b, b), :]),
            (gram, gram_out),
        ))
    ]
    for made in copies:
        made.start()
    for made in copies:
        made.wait()


def body(trailing, leaf_vectors, leaf_factors, tree_vectors, tree_factors, inverse_factor):
    b, nc = leaf_vectors.shape[1], trailing.shape[1]
    devices = lax.axis_size("rows")
    total_rows = trailing.shape[0] * devices
    levels = (devices // ROW).bit_length() - 1
    piece = b // ROW
    zdim = devices // ROW // YDIM

    def vmem(*shape, dtype=F32):
        return pltpu.VMEM(shape, dtype)

    arguments = (
        trailing, leaf_vectors, leaf_factors, tree_vectors, tree_factors, inverse_factor
    )
    per_level = [vmem(nc >> level, b) for level in (1, 2, 3)]
    scratch = [
        *[vmem(*argument.shape) for argument in arguments],
        vmem(b + 8, b),
        vmem(b // 2 + 8, b),
        *[vmem(b + 8, b)] * 4,
        vmem(3 + levels, b // 2 + 8, b),
        vmem(b // 2 + 8, b), vmem(b // 2 + 8, b),
        vmem(3 + levels, b, b, dtype=BF16),
        vmem(3 + levels, b, b, dtype=BF16),
        vmem(4, b, b, dtype=BF16),
        vmem(4, b, b, dtype=BF16),
        vmem(nc, b),
        *per_level,
        *per_level, *per_level, *per_level, *per_level,
        vmem(nc // 8, b), vmem(levels, nc // 8, b), vmem(levels, nc // 8, b),
        vmem(nc // 8, b),
        *per_level,
        vmem(nc, b),
        vmem(b, nc),
        vmem(b, 2 * b, dtype=BF16), vmem(b, 2 * b, dtype=BF16),
        vmem(b, b),
        vmem(b // YDIM, b),
        vmem(YDIM - 1, b // YDIM, b),
        vmem(max(zdim - 1, 1), b // YDIM // zdim, b),
        vmem(ROW, b // YDIM // zdim, b),
        vmem(b, b), vmem(b, b),
        vmem(levels, piece, b),
        pltpu.SemaphoreType.DMA,
        pltpu.SemaphoreType.DMA((RECEIVES,)),
        pltpu.SemaphoreType.DMA((7,)),
    ]
    results = pl.pallas_call(
        functools.partial(tree_kernel, devices, total_rows),
        out_shape=(
            vmem(b, nc), vmem(b, nc), vmem(b, b), vmem(b, b), vmem(b, b)
        ),
        in_specs=[pl.BlockSpec(memory_space=pltpu.HBM)] * 6,
        out_specs=[pl.BlockSpec(memory_space=pltpu.VMEM)] * 5,
        scratch_shapes=scratch,
        compiler_params=pltpu.CompilerParams(
            collective_id=0,
            has_side_effects=True,
            vmem_limit_bytes=56 * 1024 * 1024,
        ),
        name="tree",
    )(*arguments)
    return pl.pallas_call(
        write_kernel,
        out_shape=(
            jax.ShapeDtypeStruct(trailing.shape, F32),
            jax.ShapeDtypeStruct(leaf_vectors.shape, F32),
            jax.ShapeDtypeStruct((b, b), F32),
        ),
        in_specs=[pl.BlockSpec(memory_space=pltpu.VMEM)] * 5,
        out_specs=[pl.BlockSpec(memory_space=pl.ANY)] * 3,
        scratch_shapes=[pltpu.SemaphoreType.DMA((5,))],
        name="write",
    )(*[pltpu.with_memory_space_constraint(result, pltpu.VMEM) for result in results])


def solution(mesh):
    rows = P("rows", None)
    return jax.shard_map(
        body,
        mesh=mesh,
        in_specs=(rows, rows, rows, rows, rows, P()),
        out_specs=(rows, rows, P()),
        check_vma=False,
    )
```

```python
import functools

import jax
import jax.numpy as jnp
from jax import lax
from jax.experimental import pallas as pl
from jax.experimental.pallas import tpu as pltpu
from jax.sharding import PartitionSpec as P

F32 = jnp.float32
BF16 = jnp.bfloat16
ROW = 8
YDIM = 4
MESH = pl.DeviceIdType.MESH
RECEIVES = 56


def halves(value):
    high = value.astype(BF16)
    low = (value - high.astype(F32)).astype(BF16)
    return high, low


def dot_pairs(left, right, transposed=False):
    dims = (((1,), (1 if transposed else 0,)), ((), ()))

    def one(a, b):
        return lax.dot_general(a, b, dims, preferred_element_type=F32)

    return one(left[0], right[0]) + (one(left[0], right[1]) + one(left[1], right[0]))


def dot3(left_side, right_side, transposed=False):
    return dot_pairs(halves(left_side), halves(right_side), transposed)


def tree_kernel(
    devices,
    total_rows,
    c_hbm, lv_hbm, lt_hbm, tv_hbm, tt_hbm, inv_hbm,
    head_rows, rest, head_basis, rest_basis, gram_total,
    c_ref, lv_ref, lt_ref, tv_ref, tt_ref, inv_ref,
    pack,
    folded,
    slot0, slot1, slot2, slot3,
    fold,
    row_fold, row_fold_bt,
    t_high, t_low,
    bt_high, bt_low,
    head,
    cur0, cur1, cur2,
    z0, z1, z2, in0, in1, in2, w0, w1, w2, wb0, wb1, wb2,
    zr, inr, wr, wbr,
    res1, res2, res3,
    gathered,
    coef,
    lvt_high, lvt_low,
    gram_own, gram_piece, gram_y, gram_z, gram_x, panel, gram_all, wback,
    send_sem, recv_sems, local_sems,
):
    b = pack.shape[1]
    hb = b // 2
    nc = c_ref.shape[1]
    row_count = devices // ROW
    row_levels = row_count.bit_length() - 1
    zdim = row_count // YDIM
    piece = b // ROW
    me = lax.axis_index("rows")
    r = me % ROW
    g = me // ROW
    core = r % 2
    x0 = (r // 2) % 2
    x1 = r // 4
    bits = (core, x0, x1)
    base = g * ROW
    y = g % YDIM
    z = g // YDIM
    twin = base + r + 1 - 2 * core
    neighbour = base + (r + 1) % ROW

    def y_mate(j):
        return (z * YDIM + (y + j) % YDIM) * ROW + r

    def z_mate(j):
        return ((z + j) % zdim * YDIM + y) * ROW + r

    cur = (cur0, cur1, cur2)
    zs, ins, ws, wbs = (z0, z1, z2), (in0, in1, in2), (w0, w1, w2), (wb0, wb1, wb2)
    slot = (slot0, slot1, slot2, slot3)
    folds = [fold.at[i] for i in range(3 + row_levels)]
    CHUNKS = (0, 1)
    eighth_b = (nc - b) // 8
    ROW_CHUNKS = (
        pl.ds(0, piece),
        pl.ds(piece, eighth_b // 2),
        pl.ds(piece + eighth_b // 2, eighth_b // 2),
    )

    def slice_of(rank):
        return rank % 2 * 4 + rank // 2 % 2 * 2 + rank // 4

    def piece_of(rank):
        return pl.ds(pl.multiple_of(slice_of(rank) * piece, piece), piece)

    mine = piece_of(r)

    def size(level, chunk):
        return ((nc - b) // 2 if chunk else b // 2) >> level

    def own(level, chunk):
        return pl.ds((b // 2 >> level) if chunk else 0, size(level, chunk))

    def part(level, chunk, upper):
        start = (b >> level) if chunk else 0
        return pl.ds(start + (size(level, chunk) if upper else 0), size(level, chunk))

    def parent(level):
        return cur[level - 1] if level else head

    def is_low(k):
        return g % (2 << k) == 0

    def is_high(k):
        return g % (2 << k) == (1 << k)

    def low_half(k):
        return is_low(k) if k < 2 else (y == 0) & (g // (1 << k) % 2 == 0)

    def high_half(k):
        return is_high(k) if k < 2 else (y == 0) & (g // (1 << k) % 2 == 1)

    def takes_fold(k):
        return is_low(k) if k < 2 else (y == 0) & jnp.logical_not(is_high(k))

    backs = [wback.at[k] for k in range(row_levels)]

    loads = {}
    for name, source, target in (
        ("tv", tv_hbm, tv_ref),
        ("tt", tt_hbm, tt_ref),
        ("lv", lv_hbm, lv_ref),
        ("lt", lt_hbm, lt_ref),
        ("c0", c_hbm.at[:, pl.ds(0, b)], c_ref.at[:, pl.ds(0, b)]),
        ("c1", c_hbm.at[:, pl.ds(b, nc - b)], c_ref.at[:, pl.ds(b, nc - b)]),
        ("inv", inv_hbm, inv_ref),
    ):
        loads[name] = pltpu.make_async_copy(source, target, local_sems.at[len(loads)])
        if name not in ("c1", "inv"):
            loads[name].start()

    barrier = pltpu.get_barrier_semaphore()

    def greet(other):
        pl.semaphore_signal(barrier, inc=1, device_id=(other,), device_id_type=MESH)

    for j in range(1, ROW):
        greet(base + (r + j) % ROW)
    for j in range(1, YDIM):
        greet(y_mate(j))
    for j in range(1, zdim):
        greet(z_mate(j))

    def entered():
        pl.semaphore_wait(barrier, ROW - 1 + YDIM - 1 + zdim - 1)

    numbers = {}
    pending = []

    def number(*name):
        return numbers.setdefault(name, len(numbers))

    def remote(source, target, receive, other):
        return pltpu.make_async_remote_copy(
            src_ref=source,
            dst_ref=target,
            send_sem=send_sem,
            recv_sem=recv_sems.at[receive],
            device_id=(other,),
            device_id_type=MESH,
        )

    def copy(source, target, name, other, condition=None):
        remote(source, target, number(*name), other).start()
        pending.append((condition, source))

    def arrived(target, name):
        remote(target, target, number(*name), neighbour).wait_recv()

    row_id = lax.broadcasted_iota(jnp.int32, (b, b), 0)
    col_id = lax.broadcasted_iota(jnp.int32, (b, b), 1)
    row_half = lax.broadcasted_iota(jnp.int32, (hb, hb), 0)
    col_half = lax.broadcasted_iota(jnp.int32, (hb, hb), 1)

    def t_of(ref):
        return jnp.where(row_id <= col_id, ref[:b, :], 0.0)

    def vt_of(ref):
        diagonal = jnp.where(row_id == col_id, ref[b : b + 1, :], 0.0)
        return jnp.where(row_id > col_id, ref[:b, :], diagonal)

    def make_fold(target, t):
        last = t[hb:, hb:]
        target[:hb, :hb] = jnp.where(row_half <= col_half, t[:hb, :hb], last.T)
        target[:hb, hb:] = t[:hb, hb:]
        diagonal = jnp.sum(
            jnp.where(row_half == col_half, last, 0.0), axis=0, keepdims=True
        )
        target[hb:, :hb] = jnp.broadcast_to(diagonal, (8, hb))
        target[hb:, hb:] = jnp.zeros((8, hb), F32)

    def store_t(index, value, rows, columns):
        high, low = halves(value)
        t_high[index, rows, columns] = high
        t_low[index, rows, columns] = low

    FIRST, LAST = pl.ds(0, hb), pl.ds(hb, hb)

    def t_from_fold(index):
        first = fold[index, :hb, :hb]
        store_t(index, jnp.where(row_half <= col_half, first, 0.0), FIRST, FIRST)
        store_t(index, fold[index, :hb, hb:], FIRST, LAST)
        store_t(index, jnp.zeros((hb, hb), F32), LAST, FIRST)
        diagonal = jnp.where(row_half == col_half, fold[index, hb : hb + 1, :hb], 0.0)
        last = jnp.where(row_half < col_half, first.T, diagonal)
        store_t(index, last, LAST, LAST)

    def t_from_slot(index):
        store_t(index, t_of(slot[index]), pl.ds(0, b), pl.ds(0, b))

    def make_bt(index):
        high, low = halves(dot3(vt_of(slot[index]).T, t_of(slot[index])))
        bt_high[index] = high
        bt_low[index] = low

    def times_bt(value, index):
        return dot_pairs(halves(value), (bt_high[index], bt_low[index]))

    def times_t(value, index):
        return dot_pairs(halves(value), (t_high[index], t_low[index]))

    loads["tv"].wait()
    loads["tt"].wait()
    tv = tv_ref[...]
    tt = tt_ref[...]
    pack[:b, :] = jnp.where(row_id <= col_id, tt, tv.T)
    diagonal = jnp.sum(jnp.where(row_id == col_id, tv, 0.0), axis=0, keepdims=True)
    pack[b:, :] = jnp.broadcast_to(diagonal, (8, b))
    make_fold(folded, tt)

    def own_node(index):
        slot[index][...] = pack[...]
        make_bt(index)
        if index < 3:
            t_from_slot(index)

    for condition, index in (
        (core == 1, 0), ((r == 2) | (r == 6), 1), (r == 4, 2), ((r == 0) & (g > 0), 3),
    ):
        @pl.when(condition)
        def _():
            own_node(index)

    loads["lv"].wait()
    high, low = halves(lv_ref[...].T)
    lvt_high[...] = high
    lvt_low[...] = low

    def leaf_tile(tile):
        columns = pl.ds(tile * b, b)
        inner = dot_pairs((lvt_high[...], lvt_low[...]), halves(c_ref[:, columns]))
        coeffs = dot3(lt_ref[...].T, inner)
        coef[:, columns] = coeffs
        result = c_ref[:b, columns] - dot3(lv_ref[:b, :], coeffs)
        head[columns, :] = result.T

    loads["lt"].wait()
    loads["c0"].wait()
    loads["c1"].start()
    loads["inv"].start()
    leaf_tile(0)
    entered()

    @pl.when(core == 1)
    def _():
        copy(folded, folds[0], ("fold", 0), me - 1, lambda: core == 1)

    @pl.when((r == 2) | (r == 6))
    def _():
        c = lambda: (r == 2) | (r == 6)
        copy(pack, slot1, ("slot", 1), me + 1, c)
        copy(folded, folds[1], ("fold", 1), me - 2, c)

    @pl.when(r == 4)
    def _():
        copy(pack, slot2, ("slot", 2), base + 5, lambda: r == 4)
        copy(folded, folds[2], ("fold", 2), base + 2, lambda: r == 4)
        copy(pack, slot2, ("slot", 2), base + 6, lambda: r == 4)

    @pl.when((r == 0) & (g > 0))
    def _():
        for other in (1, 2, 6):
            copy(pack, slot3, ("slot", 3), base + other, lambda: (r == 0) & (g > 0))

    def send(level, chunk):
        bit, far = bits[level], 1 << level
        rows, name = own(level, chunk), ("x", level, chunk)
        target = ins[level].at[rows, :]
        low_rows, high_rows = part(level, chunk, False), part(level, chunk, True)

        @pl.when(bit == 0)
        def _():
            copy(
                parent(level).at[high_rows, :], target, name, me + far,
                lambda: bits[level] == 0,
            )

        source = zs[level].at[rows, :]

        @pl.when(bit == 1)
        def _():
            zs[level][rows, :] = times_bt(parent(level)[low_rows, :], level)
            copy(source, target, name, me - far, lambda: bits[level] == 1)

    def finish(level, chunk):
        bit = bits[level]
        rows, name = own(level, chunk), ("x", level, chunk)
        low_rows, high_rows = part(level, chunk, False), part(level, chunk, True)

        @pl.when(bit == 0)
        def _():
            value = parent(level)[low_rows, :]
            update = times_t(value, level)
            arrived(ins[level].at[rows, :], name)
            update = update + ins[level][rows, :]
            cur[level][rows, :] = value - update
            ws[level][rows, :] = update

        @pl.when(bit == 1)
        def _():
            update = times_bt(parent(level)[high_rows, :], level)
            arrived(ins[level].at[rows, :], name)
            value = ins[level][rows, :]
            update = update + times_t(value, level)
            cur[level][rows, :] = value - update
            ws[level][rows, :] = update

    def give_back(level, chunk):
        rows = own(level, chunk)

        @pl.when(bits[level] == 0)
        def _():
            copy(
                ws[level].at[rows, :], wbs[level].at[rows, :], ("w", level, chunk),
                me + (1 << level), lambda: bits[level] == 0,
            )

    def residual(level, result):
        @pl.when(bits[level] == 1)
        def _():
            vt = halves(vt_of(slot[level]))
            for chunk in CHUNKS:
                rows = own(level, chunk)
                low_rows, high_rows = part(level, chunk, False), part(level, chunk, True)
                result[high_rows, :] = parent(level)[high_rows, :] - dot_pairs(
                    halves(ws[level][rows, :]), vt
                )
                arrived(wbs[level].at[rows, :], ("w", level, chunk))
                result[low_rows, :] = parent(level)[low_rows, :] - dot_pairs(
                    halves(wbs[level][rows, :]), vt
                )

    def place(level, rank, chunk):
        start = b if chunk else 0
        for bit in range(level):
            start += (rank >> bit & 1) * size(bit, chunk)
        return pl.ds(start, size(level - 1, chunk))

    def buffer_rows(level, chunk):
        return pl.ds((b >> level) if chunk else 0, size(level - 1, chunk))

    def gather(level, result, rank, into, chunks, condition):
        for chunk in chunks:
            if rank == into:
                gathered[place(level, rank, chunk), :] = result[buffer_rows(level, chunk), :]
            else:
                copy(
                    result.at[buffer_rows(level, chunk), :],
                    gathered.at[place(level, rank, chunk), :],
                    ("gather",), base + into, condition,
                )

    yrows, zrows = b // YDIM, b // YDIM // zdim

    def block_y(other):
        return pl.ds(pl.multiple_of(other * yrows, yrows), yrows)

    def block_z(other):
        return pl.ds(pl.multiple_of(other * zrows, zrows), zrows)

    my_rows = pl.ds(pl.multiple_of(y * yrows + z * zrows, zrows), zrows)

    def gram_start():
        columns = c_ref[:, :b]
        gram_own[...] = dot3(columns.T, columns)
        for j in range(1, YDIM):
            copy(
                gram_own.at[block_y((y + j) % YDIM), :], gram_y.at[YDIM - j - 1],
                ("gram y",), y_mate(j),
            )

    def gram_sum_y():
        arrived(gram_y, ("gram y",))
        total = gram_own[block_y(y), :]
        for j in range(YDIM - 1):
            total = total + gram_y[j]
        gram_piece[...] = total
        for j in range(1, zdim):
            copy(
                gram_piece.at[block_z((z + j) % zdim), :], gram_z.at[zdim - j - 1],
                ("gram z",), z_mate(j),
            )

    mine_x = gram_x.at[r]

    def gram_sum_z():
        total = gram_piece[block_z(z), :]
        if zdim > 1:
            arrived(gram_z, ("gram z",))
        for j in range(zdim - 1):
            total = total + gram_z[j]
        gram_x[r] = total
        for j in range(1, ROW):
            copy(
                mine_x, mine_x, ("gram x",), base + (r + j) % ROW,
            )

    def gram_sum_x():
        arrived(gram_x.at[pl.ds(0, ROW - 1)], ("gram x",))
        total = gram_x[0]
        for j in range(1, ROW):
            total = total + gram_x[j]
        gram_all[my_rows, :] = total
        for j in range(1, zdim):
            copy(
                gram_all.at[my_rows, :], gram_all.at[my_rows, :], ("all z",), z_mate(j),
            )

    def gram_all_y():
        if zdim > 1:
            arrived(gram_all.at[pl.ds(0, yrows - zrows), :], ("all z",))
        for j in range(1, YDIM):
            copy(
                gram_all.at[block_y(y), :], gram_all.at[block_y(y), :], ("all y",),
                y_mate(j),
            )

    send(0, 0)
    loads["c1"].wait()
    for tile in range(1, nc // b):
        leaf_tile(tile)
    send(0, 1)

    @pl.when(core == 0)
    def _():
        arrived(folds[0], ("fold", 0))
        t_from_fold(0)

    finish(0, 0)

    @pl.when((r == 3) | (r == 7))
    def _():
        arrived(slot1, ("slot", 1))
        make_bt(1)
        t_from_slot(1)

    send(1, 0)
    finish(0, 1)
    send(1, 1)

    @pl.when((r == 0) | (r == 4))
    def _():
        arrived(folds[1], ("fold", 1))
        copy(folds[1], folds[1], ("fold", 1), me + 1, lambda: (r == 0) | (r == 4))
        t_from_fold(1)

    give_back(0, 0)
    give_back(0, 1)
    gram_start()

    @pl.when(r == 2)
    def _():
        arrived(folds[2], ("fold", 2))
        copy(folds[2], folds[2], ("fold", 2), me - 2, lambda: r == 2)
        copy(folds[2], folds[2], ("fold", 2), me + 1, lambda: r == 2)
        t_from_fold(2)

    @pl.when(((r == 2) | (r == 6)) & (g > 0))
    def _():
        arrived(slot3, ("slot", 3))
        copy(slot3, slot3, ("slot", 3), me + 1, lambda: ((r == 2) | (r == 6)) & (g > 0))

        @pl.when(r == 2)
        def _():
            copy(slot3, slot3, ("slot", 3), me + 2, lambda: (r == 2) & (g > 0))

    @pl.when(r == 6)
    def _():
        arrived(slot2, ("slot", 2))
        copy(slot2, slot2, ("slot", 2), me + 1, lambda: r == 6)
        make_bt(2)
        t_from_slot(2)

    @pl.when((r == 5) | (r == 7))
    def _():
        arrived(slot2, ("slot", 2))
        make_bt(2)
        t_from_slot(2)

    @pl.when((r == 1) | (r == 5))
    def _():
        arrived(folds[1], ("fold", 1))
        t_from_fold(1)

    finish(1, 0)
    send(2, 0)

    finish(1, 1)
    send(2, 1)

    @pl.when(r == 0)
    def _():
        arrived(folds[2], ("fold", 2))
        copy(folds[2], folds[2], ("fold", 2), me + 1, lambda: r == 0)
        t_from_fold(2)


    @pl.when((g > 0) & (core == 0))
    def _():
        @pl.when(r == 4)
        def _():
            arrived(slot3, ("slot", 3))
            copy(slot3, slot3, ("slot", 3), me + 1, lambda: (g > 0) & (r == 4))

        make_fold(row_fold, t_of(slot3))

        @pl.when(r > 0)
        def _():
            make_bt(3)

        if row_levels > 2:
            make_fold(row_fold_bt, bt_high[3].astype(F32) + bt_low[3].astype(F32))
        for k in range(row_levels):
            @pl.when(is_high(k))
            def _():
                c = functools.partial(lambda k: is_high(k) & (core == 0), k)
                name = ("fold", 3 + k)
                for j in range(max(1, (1 << k) // YDIM)):
                    copy(
                        row_fold, folds[3 + k], name,
                        me - (ROW << k) + j * YDIM * ROW, c,
                    )
                    if j:
                        copy(row_fold_bt, folds[3 + k], name, me + j * YDIM * ROW, c)

    give_back(1, 0)
    give_back(1, 1)

    @pl.when((r == 1) | (r == 3))
    def _():
        arrived(folds[2], ("fold", 2))
        t_from_fold(2)

    def rest_tile(tile):
        columns = pl.ds(tile * b, b)
        rest[:, columns] = c_ref[b:, columns] - dot3(lv_ref[b:, :], coef[:, columns])

    gram_sum_y()
    rest_tile(0)
    loads["inv"].wait()
    rest_basis[...] = dot3(rest[:, :b], inv_ref[...])
    for tile in range(1, nc // b):
        rest_tile(tile)

    @pl.when((g > 0) & (core == 1))
    def _():
        arrived(slot3, ("slot", 3))

    @pl.when((g > 0) & (core == 1))
    def _():
        make_bt(3)

    def send_z(k, chunk):
        rows = ROW_CHUNKS[chunk]
        source = zr.at[rows, :]

        @pl.when(is_high(k))
        def _():
            zr[rows, :] = times_bt(cur2[rows, :], 3)
            copy(
                source, inr.at[k, rows, :], ("z", k, chunk), me - (ROW << k),
                functools.partial(is_high, k),
            )

    def send_u(k, chunk):
        rows = ROW_CHUNKS[chunk]
        ahead = wr.at[k, rows, :]

        @pl.when(is_low(k))
        def _():
            wr[k, rows, :] = times_t(cur2[rows, :], 3 + k)
            copy(
                ahead, wbr.at[rows, :], ("wr", chunk), me + (ROW << k),
                functools.partial(is_low, k),
            )

    def finish_row(k, chunk):
        rows = ROW_CHUNKS[chunk]

        @pl.when(is_low(k))
        def _():
            arrived(inr.at[k, rows, :], ("z", k, chunk))
            cur2[rows, :] = cur2[rows, :] - (wr[k, rows, :] + inr[k, rows, :])

    PANEL = ROW_CHUNKS[0]

    def send_shared(k):
        ours, ahead = wr.at[k, PANEL, :], backs[k]

        @pl.when(low_half(k))
        def _():
            value = cur2[PANEL, :]
            update = times_t(value, 3 + k)
            wr[k, PANEL, :] = value - update
            if k != 4:
                copy(
                    ours, inr.at[k, PANEL, :], ("z", k, 0), me + (ROW << k),
                    functools.partial(low_half, k),
                )

            @pl.when(is_low(k))
            def _():
                wback[k, :, :] = update
                copy(
                    ahead, wbr.at[PANEL, :], ("wr", 0), me + (ROW << k),
                    functools.partial(is_low, k),
                )

        @pl.when(high_half(k))
        def _():
            update = times_t(cur2[PANEL, :], 3 + k)
            wr[k, PANEL, :] = -update

            @pl.when(is_high(k))
            def _():
                zr[PANEL, :] = update
                res3[PANEL, :] = cur2[PANEL, :]

            if k != 4:
                copy(
                    ours, inr.at[k, PANEL, :], ("z", k, 0), me - (ROW << k),
                    functools.partial(high_half, k),
                )

        if k == 4:
            for source, targets in ((7, (1, 0)), (4, (2, 3)), (3, (5, 4)), (0, (6, 7))):
                @pl.when((y == 0) & (z == source))
                def _():
                    for target in targets:
                        copy(
                            ours, inr.at[k, PANEL, :], ("z", k, 0),
                            target * YDIM * ROW + r,
                            functools.partial(lambda o: (y == 0) & (z == o), source),
                        )

    def finish_shared(k):
        @pl.when(y == 0)
        def _():
            arrived(inr.at[k, PANEL, :], ("z", k, 0))
            cur2[PANEL, :] = wr[k, PANEL, :] + inr[k, PANEL, :]

    def send_level(k, chunk):
        if k > 1 and chunk == 0:
            send_shared(k)
        else:
            send_z(k, chunk)
            send_u(k, chunk)

    def finish_level(k, chunk):
        if k > 1 and chunk == 0:
            finish_shared(k)
        else:
            finish_row(k, chunk)

    def forward_operators(k):
        @pl.when(takes_fold(k) & (core == 0))
        def _():
            arrived(folds[3 + k], ("fold", 3 + k))
            copy(
                folds[3 + k], folds[3 + k], ("fold", 3 + k), me + 1,
                functools.partial(lambda k: takes_fold(k) & (core == 0), k),
            )

    def row_operators(k):
        @pl.when(takes_fold(k) & (core == 1))
        def _():
            arrived(folds[3 + k], ("fold", 3 + k))

        if k > 1:
            @pl.when(is_high(k))
            def _():
                make_fold(fold.at[3 + k], bt_high[3].astype(F32) + bt_low[3].astype(F32))

        @pl.when(takes_fold(k) if k < 2 else y == 0)
        def _():
            t_from_fold(3 + k)

    finish(2, 0)
    send_z(0, 0)
    finish(2, 1)
    send_z(0, 1)
    send_z(0, 2)
    forward_operators(0)
    give_back(2, 0)
    give_back(2, 1)

    row_operators(0)
    for chunk in range(3):
        send_u(0, chunk)

    def panel_to_row(condition):
        copy(panel.at[mine, :], panel.at[mine, :], ("panel core",), twin, condition)
        for j in (4, 2, 6):
            copy(
                panel.at[mine, :], panel.at[mine, :], ("panel",),
                base + (r + j) % ROW, condition,
            )

    def panel_out():
        @pl.when(y == 0)
        def _():
            panel[mine, :] = cur2[PANEL, :]
            for j in range(1, YDIM):
                copy(
                    panel.at[mine, :], panel.at[mine, :], ("panel y",), y_mate(j),
                    lambda: y == 0,
                )
            panel_to_row(lambda: y == 0)

    def gather_row(result, chunk, condition):
        for rank in range(ROW):
            start = place(3, rank, min(chunk, 1)).start
            start += eighth_b // 2 if chunk == 2 else 0
            rows = pl.ds(start, ROW_CHUNKS[chunk].size)

            @pl.when(r == rank)
            def _():
                if rank == 0:
                    gathered[rows, :] = result[ROW_CHUNKS[chunk], :]
                else:
                    copy(
                        result.at[ROW_CHUNKS[chunk], :], gathered.at[rows, :],
                        ("gather",), base,
                        functools.partial(lambda o: condition() & (r == o), rank),
                    )

    def row_result(k):
        for chunk in (1, 2, 0):
            rows = ROW_CHUNKS[chunk]

            @pl.when(is_high(k))
            def _():
                vt = halves(vt_of(slot3))
                arrived(wbr.at[rows, :], ("wr", chunk))
                start = res3 if k > 1 and chunk == 0 else cur2
                res3[rows, :] = start[rows, :] - dot_pairs(
                    halves(wbr[rows, :] + zr[rows, :]), vt
                )
                gather_row(res3, chunk, functools.partial(is_high, k))

    events = []
    for k in range(row_levels):
        events += [(2.9 * k + (5.0 if k > 3 else 0.0), k, 0)]
        events += [(2.0 + 4.2 * k, k, 1), (2.9 + 4.2 * k, k, 2)]
    done = set()
    last = row_levels - 1
    for _, k, chunk in sorted(events):
        if k < last and chunk == 0:
            forward_operators(k + 1)
        finish_level(k, chunk)
        if k < last:
            if chunk == 0:
                row_operators(k + 1)
            send_level(k + 1, chunk)
        done.add((k, chunk))
        if (k, chunk) == (last, 0):
            panel_out()
        if (k, chunk) == (last, 0 if last > 3 else 2):
            gram_all_y()
        if k == last:
            @pl.when(g == 0)
            def _():
                gather_row(cur2, chunk, lambda: g == 0)
        if (k, chunk) == (0, 2):
            gram_sum_z()
            residual(0, gathered)
            residual(1, res1)
            for rank, into in ((2, 2), (3, 2), (6, 6), (7, 6)):
                @pl.when(r == rank)
                def _():
                    gather(1, res1, rank, into, CHUNKS, functools.partial(lambda o: r == o, rank))
        if (k, chunk) == (1, 2):
            residual(2, res2)
            for rank in range(4, ROW):
                @pl.when(r == rank)
                def _():
                    gather(2, res2, rank, 4, CHUNKS, functools.partial(lambda o: r == o, rank))
            gram_sum_x()
        if k and chunk == 2:
            row_result(k - 1)
        if (k, chunk) == (last, 2):
            row_result(last)

    @pl.when(y != 0)
    def _():
        arrived(panel.at[mine, :], ("panel y",))
        panel_to_row(lambda: y != 0)

    arrived(panel.at[pl.ds(0, 3 * piece), :], ("panel",))
    for j in (2, 6, 4):
        theirs = piece_of((r + j) % ROW)
        copy(panel.at[theirs, :], panel.at[theirs, :], ("panel core",), twin)

    @pl.when((r == 2) | (r == 6))
    def _():
        arrived(gathered.at[pl.ds(0, nc // 2), :], ("gather",))

    @pl.when(r == 4)
    def _():
        arrived(gathered.at[pl.ds(0, 3 * nc // 4), :], ("gather",))

    @pl.when(r == 0)
    def _():
        arrived(gathered.at[pl.ds(0, 7 * nc // 8), :], ("gather",))

    head_rows[...] = gathered[...].T
    head_basis[...] = jnp.where(me == 0, 0.0, dot3(head_rows[:, :b], inv_ref[...]))
    arrived(gram_all.at[pl.ds(0, b - yrows), :], ("all y",))
    arrived(panel.at[pl.ds(0, 4 * piece), :], ("panel core",))
    square = dot3(panel[...], panel[...], True)
    gram_total[...] = (gram_all[...] - square) / float(total_rows)

    for condition, source in pending:
        made = functools.partial(
            lambda source: remote(source, source, 0, neighbour).wait_send(), source
        )
        if condition is None:
            made()
        else:
            @pl.when(condition())
            def _():
                made()
    assert len(numbers) <= recv_sems.shape[0]


def write_kernel(
    head_rows, rest, head_basis, rest_basis, gram, upd_out, basis_out, gram_out, sems
):
    b = head_rows.shape[0]
    copies = [
        pltpu.make_async_copy(source, target, sems.at[index])
        for index, (source, target) in enumerate((
            (head_rows, upd_out.at[pl.ds(0, b), :]),
            (rest, upd_out.at[pl.ds(b, b), :]),
            (head_basis, basis_out.at[pl.ds(0, b), :]),
            (rest_basis, basis_out.at[pl.ds(b, b), :]),
            (gram, gram_out),
        ))
    ]
    for made in copies:
        made.start()
    for made in copies:
        made.wait()


def body(trailing, leaf_vectors, leaf_factors, tree_vectors, tree_factors, inverse_factor):
    b, nc = leaf_vectors.shape[1], trailing.shape[1]
    devices = lax.axis_size("rows")
    total_rows = trailing.shape[0] * devices
    levels = (devices // ROW).bit_length() - 1
    piece = b // ROW
    zdim = devices // ROW // YDIM

    def vmem(*shape, dtype=F32):
        return pltpu.VMEM(shape, dtype)

    arguments = (
        trailing, leaf_vectors, leaf_factors, tree_vectors, tree_factors, inverse_factor
    )
    per_level = [vmem(nc >> level, b) for level in (1, 2, 3)]
    scratch = [
        *[vmem(*argument.shape) for argument in arguments],
        vmem(b + 8, b),
        vmem(b // 2 + 8, b),
        *[vmem(b + 8, b)] * 4,
        vmem(3 + levels, b // 2 + 8, b),
        vmem(b // 2 + 8, b), vmem(b // 2 + 8, b),
        vmem(3 + levels, b, b, dtype=BF16),
        vmem(3 + levels, b, b, dtype=BF16),
        vmem(4, b, b, dtype=BF16),
        vmem(4, b, b, dtype=BF16),
        vmem(nc, b),
        *per_level,
        *per_level, *per_level, *per_level, *per_level,
        vmem(nc // 8, b), vmem(levels, nc // 8, b), vmem(levels, nc // 8, b),
        vmem(nc // 8, b),
        *per_level,
        vmem(nc, b),
        vmem(b, nc),
        vmem(b, 2 * b, dtype=BF16), vmem(b, 2 * b, dtype=BF16),
        vmem(b, b),
        vmem(b // YDIM, b),
        vmem(YDIM - 1, b // YDIM, b),
        vmem(max(zdim - 1, 1), b // YDIM // zdim, b),
        vmem(ROW, b // YDIM // zdim, b),
        vmem(b, b), vmem(b, b),
        vmem(levels, piece, b),
        pltpu.SemaphoreType.DMA,
        pltpu.SemaphoreType.DMA((RECEIVES,)),
        pltpu.SemaphoreType.DMA((7,)),
    ]
    results = pl.pallas_call(
        functools.partial(tree_kernel, devices, total_rows),
        out_shape=(
            vmem(b, nc), vmem(b, nc), vmem(b, b), vmem(b, b), vmem(b, b)
        ),
        in_specs=[pl.BlockSpec(memory_space=pltpu.HBM)] * 6,
        out_specs=[pl.BlockSpec(memory_space=pltpu.VMEM)] * 5,
        scratch_shapes=scratch,
        compiler_params=pltpu.CompilerParams(
            collective_id=0,
            has_side_effects=True,
            vmem_limit_bytes=56 * 1024 * 1024,
        ),
        name="tree",
    )(*arguments)
    return pl.pallas_call(
        write_kernel,
        out_shape=(
            jax.ShapeDtypeStruct(trailing.shape, F32),
            jax.ShapeDtypeStruct(leaf_vectors.shape, F32),
            jax.ShapeDtypeStruct((b, b), F32),
        ),
        in_specs=[pl.BlockSpec(memory_space=pltpu.VMEM)] * 5,
        out_specs=[pl.BlockSpec(memory_space=pl.ANY)] * 3,
        scratch_shapes=[pltpu.SemaphoreType.DMA((5,))],
        name="write",
    )(*[pltpu.with_memory_space_constraint(result, pltpu.VMEM) for result in results])


def solution(mesh):
    rows = P("rows", None)
    return jax.shard_map(
        body,
        mesh=mesh,
        in_specs=(rows, rows, rows, rows, rows, P()),
        out_specs=(rows, rows, P()),
        check_vma=False,
    )
```

```python
import functools

import jax
import jax.numpy as jnp
from jax import lax
from jax.experimental import pallas as pl
from jax.experimental.pallas import tpu as pltpu
from jax.sharding import PartitionSpec as P

F32 = jnp.float32
BF16 = jnp.bfloat16
ROW = 8
YDIM = 4
MESH = pl.DeviceIdType.MESH
RECEIVES = 56


def halves(value):
    high = value.astype(BF16)
    low = (value - high.astype(F32)).astype(BF16)
    return high, low


def dot_pairs(left, right, transposed=False):
    dims = (((1,), (1 if transposed else 0,)), ((), ()))

    def one(a, b):
        return lax.dot_general(a, b, dims, preferred_element_type=F32)

    return one(left[0], right[0]) + (one(left[0], right[1]) + one(left[1], right[0]))


def dot3(left_side, right_side, transposed=False):
    return dot_pairs(halves(left_side), halves(right_side), transposed)


def tree_kernel(
    devices,
    total_rows,
    c_hbm, lv_hbm, lt_hbm, tv_hbm, tt_hbm, inv_hbm,
    head_rows, rest, head_basis, rest_basis, gram_total,
    c_ref, lv_ref, lt_ref, tv_ref, tt_ref, inv_ref,
    pack,
    folded,
    slot0, slot1, slot2, slot3,
    fold,
    row_fold, row_fold_bt,
    t_high, t_low,
    bt_high, bt_low,
    head,
    cur0, cur1, cur2,
    z0, z1, z2, in0, in1, in2, w0, w1, w2, wb0, wb1, wb2,
    zr, inr, wr, wbr,
    res1, res2, res3,
    gathered,
    coef,
    lvt_high, lvt_low,
    gram_own, gram_piece, gram_y, gram_z, gram_x, panel, gram_all, wback,
    send_sem, recv_sems, local_sems,
):
    b = pack.shape[1]
    hb = b // 2
    nc = c_ref.shape[1]
    row_count = devices // ROW
    row_levels = row_count.bit_length() - 1
    zdim = row_count // YDIM
    piece = b // ROW
    me = lax.axis_index("rows")
    r = me % ROW
    g = me // ROW
    core = r % 2
    x0 = (r // 2) % 2
    x1 = r // 4
    bits = (core, x0, x1)
    base = g * ROW
    y = g % YDIM
    z = g // YDIM
    twin = base + r + 1 - 2 * core
    neighbour = base + (r + 1) % ROW

    def y_mate(j):
        return (z * YDIM + (y + j) % YDIM) * ROW + r

    def z_mate(j):
        return ((z + j) % zdim * YDIM + y) * ROW + r

    cur = (cur0, cur1, cur2)
    zs, ins, ws, wbs = (z0, z1, z2), (in0, in1, in2), (w0, w1, w2), (wb0, wb1, wb2)
    slot = (slot0, slot1, slot2, slot3)
    folds = [fold.at[i] for i in range(3 + row_levels)]
    CHUNKS = (0, 1)
    eighth_b = (nc - b) // 8
    ROW_CHUNKS = (
        pl.ds(0, piece),
        pl.ds(piece, eighth_b // 2),
        pl.ds(piece + eighth_b // 2, eighth_b // 2),
    )

    def slice_of(rank):
        return rank % 2 * 4 + rank // 2 % 2 * 2 + rank // 4

    def piece_of(rank):
        return pl.ds(pl.multiple_of(slice_of(rank) * piece, piece), piece)

    mine = piece_of(r)

    def size(level, chunk):
        return ((nc - b) // 2 if chunk else b // 2) >> level

    def own(level, chunk):
        return pl.ds((b // 2 >> level) if chunk else 0, size(level, chunk))

    def part(level, chunk, upper):
        start = (b >> level) if chunk else 0
        return pl.ds(start + (size(level, chunk) if upper else 0), size(level, chunk))

    def parent(level):
        return cur[level - 1] if level else head

    def is_low(k):
        return g % (2 << k) == 0

    def is_high(k):
        return g % (2 << k) == (1 << k)

    def low_half(k):
        return is_low(k) if k < 2 else (y == 0) & (g // (1 << k) % 2 == 0)

    def high_half(k):
        return is_high(k) if k < 2 else (y == 0) & (g // (1 << k) % 2 == 1)

    def takes_fold(k):
        return is_low(k) if k < 2 else (y == 0) & jnp.logical_not(is_high(k))

    backs = [wback.at[k] for k in range(row_levels)]

    loads = {}
    for name, source, target in (
        ("tv", tv_hbm, tv_ref),
        ("tt", tt_hbm, tt_ref),
        ("lv", lv_hbm, lv_ref),
        ("lt", lt_hbm, lt_ref),
        ("c0", c_hbm.at[:, pl.ds(0, b)], c_ref.at[:, pl.ds(0, b)]),
        ("c1", c_hbm.at[:, pl.ds(b, nc - b)], c_ref.at[:, pl.ds(b, nc - b)]),
        ("inv", inv_hbm, inv_ref),
    ):
        loads[name] = pltpu.make_async_copy(source, target, local_sems.at[len(loads)])
        if name not in ("c1", "inv"):
            loads[name].start()

    barrier = pltpu.get_barrier_semaphore()

    def greet(other):
        pl.semaphore_signal(barrier, inc=1, device_id=(other,), device_id_type=MESH)

    for j in range(1, ROW):
        greet(base + (r + j) % ROW)
    for j in range(1, YDIM):
        greet(y_mate(j))
    for j in range(1, zdim):
        greet(z_mate(j))

    def entered():
        pl.semaphore_wait(barrier, ROW - 1 + YDIM - 1 + zdim - 1)

    numbers = {}
    pending = []

    def number(*name):
        return numbers.setdefault(name, len(numbers))

    def remote(source, target, receive, other):
        return pltpu.make_async_remote_copy(
            src_ref=source,
            dst_ref=target,
            send_sem=send_sem,
            recv_sem=recv_sems.at[receive],
            device_id=(other,),
            device_id_type=MESH,
        )

    def copy(source, target, name, other, condition=None):
        remote(source, target, number(*name), other).start()
        pending.append((condition, source))

    def arrived(target, name):
        remote(target, target, number(*name), neighbour).wait_recv()

    row_id = lax.broadcasted_iota(jnp.int32, (b, b), 0)
    col_id = lax.broadcasted_iota(jnp.int32, (b, b), 1)
    row_half = lax.broadcasted_iota(jnp.int32, (hb, hb), 0)
    col_half = lax.broadcasted_iota(jnp.int32, (hb, hb), 1)

    def t_of(ref):
        return jnp.where(row_id <= col_id, ref[:b, :], 0.0)

    def vt_of(ref):
        diagonal = jnp.where(row_id == col_id, ref[b : b + 1, :], 0.0)
        return jnp.where(row_id > col_id, ref[:b, :], diagonal)

    def make_fold(target, t):
        last = t[hb:, hb:]
        target[:hb, :hb] = jnp.where(row_half <= col_half, t[:hb, :hb], last.T)
        target[:hb, hb:] = t[:hb, hb:]
        diagonal = jnp.sum(
            jnp.where(row_half == col_half, last, 0.0), axis=0, keepdims=True
        )
        target[hb:, :hb] = jnp.broadcast_to(diagonal, (8, hb))
        target[hb:, hb:] = jnp.zeros((8, hb), F32)

    def store_t(index, value, rows, columns):
        high, low = halves(value)
        t_high[index, rows, columns] = high
        t_low[index, rows, columns] = low

    FIRST, LAST = pl.ds(0, hb), pl.ds(hb, hb)

    def t_from_fold(index):
        first = fold[index, :hb, :hb]
        store_t(index, jnp.where(row_half <= col_half, first, 0.0), FIRST, FIRST)
        store_t(index, fold[index, :hb, hb:], FIRST, LAST)
        store_t(index, jnp.zeros((hb, hb), F32), LAST, FIRST)
        diagonal = jnp.where(row_half == col_half, fold[index, hb : hb + 1, :hb], 0.0)
        last = jnp.where(row_half < col_half, first.T, diagonal)
        store_t(index, last, LAST, LAST)

    def t_from_slot(index):
        store_t(index, t_of(slot[index]), pl.ds(0, b), pl.ds(0, b))

    def make_bt(index):
        high, low = halves(dot3(vt_of(slot[index]).T, t_of(slot[index])))
        bt_high[index] = high
        bt_low[index] = low

    def times_bt(value, index):
        return dot_pairs(halves(value), (bt_high[index], bt_low[index]))

    def times_t(value, index):
        return dot_pairs(halves(value), (t_high[index], t_low[index]))

    loads["tv"].wait()
    loads["tt"].wait()
    tv = tv_ref[...]
    tt = tt_ref[...]
    pack[:b, :] = jnp.where(row_id <= col_id, tt, tv.T)
    diagonal = jnp.sum(jnp.where(row_id == col_id, tv, 0.0), axis=0, keepdims=True)
    pack[b:, :] = jnp.broadcast_to(diagonal, (8, b))
    make_fold(folded, tt)

    def own_node(index):
        slot[index][...] = pack[...]
        make_bt(index)
        if index < 3:
            t_from_slot(index)

    for condition, index in (
        (core == 1, 0), ((r == 2) | (r == 6), 1), (r == 4, 2), ((r == 0) & (g > 0), 3),
    ):
        @pl.when(condition)
        def _():
            own_node(index)

    loads["lv"].wait()
    high, low = halves(lv_ref[...].T)
    lvt_high[...] = high
    lvt_low[...] = low

    def leaf_tile(tile):
        columns = pl.ds(tile * b, b)
        inner = dot_pairs((lvt_high[...], lvt_low[...]), halves(c_ref[:, columns]))
        coeffs = dot3(lt_ref[...].T, inner)
        coef[:, columns] = coeffs
        result = c_ref[:b, columns] - dot3(lv_ref[:b, :], coeffs)
        head[columns, :] = result.T

    loads["lt"].wait()
    loads["c0"].wait()
    loads["c1"].start()
    loads["inv"].start()
    leaf_tile(0)
    entered()

    @pl.when(core == 1)
    def _():
        copy(folded, folds[0], ("fold", 0), me - 1, lambda: core == 1)

    @pl.when((r == 2) | (r == 6))
    def _():
        c = lambda: (r == 2) | (r == 6)
        copy(pack, slot1, ("slot", 1), me + 1, c)
        copy(folded, folds[1], ("fold", 1), me - 2, c)

    @pl.when(r == 4)
    def _():
        copy(pack, slot2, ("slot", 2), base + 5, lambda: r == 4)
        copy(folded, folds[2], ("fold", 2), base + 2, lambda: r == 4)
        copy(pack, slot2, ("slot", 2), base + 6, lambda: r == 4)

    @pl.when((r == 0) & (g > 0))
    def _():
        for other in (1, 2, 6):
            copy(pack, slot3, ("slot", 3), base + other, lambda: (r == 0) & (g > 0))

    def send(level, chunk):
        bit, far = bits[level], 1 << level
        rows, name = own(level, chunk), ("x", level, chunk)
        target = ins[level].at[rows, :]
        low_rows, high_rows = part(level, chunk, False), part(level, chunk, True)

        @pl.when(bit == 0)
        def _():
            copy(
                parent(level).at[high_rows, :], target, name, me + far,
                lambda: bits[level] == 0,
            )

        source = zs[level].at[rows, :]

        @pl.when(bit == 1)
        def _():
            zs[level][rows, :] = times_bt(parent(level)[low_rows, :], level)
            copy(source, target, name, me - far, lambda: bits[level] == 1)

    def finish(level, chunk):
        bit = bits[level]
        rows, name = own(level, chunk), ("x", level, chunk)
        low_rows, high_rows = part(level, chunk, False), part(level, chunk, True)

        @pl.when(bit == 0)
        def _():
            value = parent(level)[low_rows, :]
            update = times_t(value, level)
            arrived(ins[level].at[rows, :], name)
            update = update + ins[level][rows, :]
            cur[level][rows, :] = value - update
            ws[level][rows, :] = update

        @pl.when(bit == 1)
        def _():
            update = times_bt(parent(level)[high_rows, :], level)
            arrived(ins[level].at[rows, :], name)
            value = ins[level][rows, :]
            update = update + times_t(value, level)
            cur[level][rows, :] = value - update
            ws[level][rows, :] = update

    def give_back(level, chunk):
        rows = own(level, chunk)

        @pl.when(bits[level] == 0)
        def _():
            copy(
                ws[level].at[rows, :], wbs[level].at[rows, :], ("w", level, chunk),
                me + (1 << level), lambda: bits[level] == 0,
            )

    def residual(level, result):
        @pl.when(bits[level] == 1)
        def _():
            vt = halves(vt_of(slot[level]))
            for chunk in CHUNKS:
                rows = own(level, chunk)
                low_rows, high_rows = part(level, chunk, False), part(level, chunk, True)
                result[high_rows, :] = parent(level)[high_rows, :] - dot_pairs(
                    halves(ws[level][rows, :]), vt
                )
                arrived(wbs[level].at[rows, :], ("w", level, chunk))
                result[low_rows, :] = parent(level)[low_rows, :] - dot_pairs(
                    halves(wbs[level][rows, :]), vt
                )

    def place(level, rank, chunk):
        start = b if chunk else 0
        for bit in range(level):
            start += (rank >> bit & 1) * size(bit, chunk)
        return pl.ds(start, size(level - 1, chunk))

    def buffer_rows(level, chunk):
        return pl.ds((b >> level) if chunk else 0, size(level - 1, chunk))

    def gather(level, result, rank, into, chunks, condition):
        for chunk in chunks:
            if rank == into:
                gathered[place(level, rank, chunk), :] = result[buffer_rows(level, chunk), :]
            else:
                copy(
                    result.at[buffer_rows(level, chunk), :],
                    gathered.at[place(level, rank, chunk), :],
                    ("gather",), base + into, condition,
                )

    yrows, zrows = b // YDIM, b // YDIM // zdim

    def block_y(other):
        return pl.ds(pl.multiple_of(other * yrows, yrows), yrows)

    def block_z(other):
        return pl.ds(pl.multiple_of(other * zrows, zrows), zrows)

    my_rows = pl.ds(pl.multiple_of(y * yrows + z * zrows, zrows), zrows)

    def gram_start():
        columns = c_ref[:, :b]
        gram_own[...] = dot3(columns.T, columns)
        for j in range(1, YDIM):
            copy(
                gram_own.at[block_y((y + j) % YDIM), :], gram_y.at[YDIM - j - 1],
                ("gram y",), y_mate(j),
            )

    def gram_sum_y():
        arrived(gram_y, ("gram y",))
        total = gram_own[block_y(y), :]
        for j in range(YDIM - 1):
            total = total + gram_y[j]
        gram_piece[...] = total
        for j in range(1, zdim):
            copy(
                gram_piece.at[block_z((z + j) % zdim), :], gram_z.at[zdim - j - 1],
                ("gram z",), z_mate(j),
            )

    mine_x = gram_x.at[r]

    def gram_sum_z():
        total = gram_piece[block_z(z), :]
        if zdim > 1:
            arrived(gram_z, ("gram z",))
        for j in range(zdim - 1):
            total = total + gram_z[j]
        gram_x[r] = total
        for j in range(1, ROW):
            copy(
                mine_x, mine_x, ("gram x",), base + (r + j) % ROW,
            )

    def gram_sum_x():
        arrived(gram_x.at[pl.ds(0, ROW - 1)], ("gram x",))
        total = gram_x[0]
        for j in range(1, ROW):
            total = total + gram_x[j]
        gram_all[my_rows, :] = total
        for j in range(1, zdim):
            copy(
                gram_all.at[my_rows, :], gram_all.at[my_rows, :], ("all z",), z_mate(j),
            )

    def gram_all_y():
        if zdim > 1:
            arrived(gram_all.at[pl.ds(0, yrows - zrows), :], ("all z",))
        for j in range(1, YDIM):
            copy(
                gram_all.at[block_y(y), :], gram_all.at[block_y(y), :], ("all y",),
                y_mate(j),
            )

    send(0, 0)
    loads["c1"].wait()
    for tile in range(1, nc // b):
        leaf_tile(tile)
    send(0, 1)

    @pl.when(core == 0)
    def _():
        arrived(folds[0], ("fold", 0))
        t_from_fold(0)

    finish(0, 0)

    @pl.when((r == 3) | (r == 7))
    def _():
        arrived(slot1, ("slot", 1))
        make_bt(1)
        t_from_slot(1)

    send(1, 0)
    finish(0, 1)
    send(1, 1)

    @pl.when((r == 0) | (r == 4))
    def _():
        arrived(folds[1], ("fold", 1))
        copy(folds[1], folds[1], ("fold", 1), me + 1, lambda: (r == 0) | (r == 4))
        t_from_fold(1)

    give_back(0, 0)
    give_back(0, 1)
    gram_start()

    @pl.when(r == 2)
    def _():
        arrived(folds[2], ("fold", 2))
        copy(folds[2], folds[2], ("fold", 2), me - 2, lambda: r == 2)
        copy(folds[2], folds[2], ("fold", 2), me + 1, lambda: r == 2)
        t_from_fold(2)

    @pl.when(((r == 2) | (r == 6)) & (g > 0))
    def _():
        arrived(slot3, ("slot", 3))
        copy(slot3, slot3, ("slot", 3), me + 1, lambda: ((r == 2) | (r == 6)) & (g > 0))

        @pl.when(r == 2)
        def _():
            copy(slot3, slot3, ("slot", 3), me + 2, lambda: (r == 2) & (g > 0))

    def row_node(condition):
        @pl.when(condition())
        def _():
            make_fold(row_fold, t_of(slot3))

            @pl.when(r > 0)
            def _():
                make_bt(3)

            if row_levels > 2:
                make_fold(row_fold_bt, bt_high[3].astype(F32) + bt_low[3].astype(F32))
            for k in range(row_levels):
                @pl.when(is_high(k))
                def _():
                    c = functools.partial(lambda k: is_high(k) & condition(), k)
                    name = ("fold", 3 + k)
                    for j in range(max(1, (1 << k) // YDIM)):
                        copy(
                            row_fold, folds[3 + k], name,
                            me - (ROW << k) + j * YDIM * ROW, c,
                        )
                        if j:
                            copy(row_fold_bt, folds[3 + k], name, me + j * YDIM * ROW, c)

    row_node(lambda: (g > 0) & (core == 0) & (r != 4))

    @pl.when(r == 6)
    def _():
        arrived(slot2, ("slot", 2))
        copy(slot2, slot2, ("slot", 2), me + 1, lambda: r == 6)
        make_bt(2)
        t_from_slot(2)

    @pl.when((r == 5) | (r == 7))
    def _():
        arrived(slot2, ("slot", 2))
        make_bt(2)
        t_from_slot(2)

    @pl.when((r == 1) | (r == 5))
    def _():
        arrived(folds[1], ("fold", 1))
        t_from_fold(1)

    finish(1, 0)
    send(2, 0)

    finish(1, 1)
    send(2, 1)

    @pl.when(r == 0)
    def _():
        arrived(folds[2], ("fold", 2))
        copy(folds[2], folds[2], ("fold", 2), me + 1, lambda: r == 0)
        t_from_fold(2)


    @pl.when((g > 0) & (r == 4))
    def _():
        arrived(slot3, ("slot", 3))
        copy(slot3, slot3, ("slot", 3), me + 1, lambda: (g > 0) & (r == 4))

    row_node(lambda: (g > 0) & (r == 4))

    give_back(1, 0)
    give_back(1, 1)

    @pl.when((r == 1) | (r == 3))
    def _():
        arrived(folds[2], ("fold", 2))
        t_from_fold(2)

    def rest_tile(tile):
        columns = pl.ds(tile * b, b)
        rest[:, columns] = c_ref[b:, columns] - dot3(lv_ref[b:, :], coef[:, columns])

    gram_sum_y()
    rest_tile(0)
    loads["inv"].wait()
    rest_basis[...] = dot3(rest[:, :b], inv_ref[...])
    for tile in range(1, nc // b):
        rest_tile(tile)

    @pl.when((g > 0) & (core == 1))
    def _():
        arrived(slot3, ("slot", 3))

    @pl.when((g > 0) & (core == 1))
    def _():
        make_bt(3)

    def send_z(k, chunk):
        rows = ROW_CHUNKS[chunk]
        source = zr.at[rows, :]

        @pl.when(is_high(k))
        def _():
            zr[rows, :] = times_bt(cur2[rows, :], 3)
            copy(
                source, inr.at[k, rows, :], ("z", k, chunk), me - (ROW << k),
                functools.partial(is_high, k),
            )

    def send_u(k, chunk):
        rows = ROW_CHUNKS[chunk]
        ahead = wr.at[k, rows, :]

        @pl.when(is_low(k))
        def _():
            wr[k, rows, :] = times_t(cur2[rows, :], 3 + k)
            copy(
                ahead, wbr.at[rows, :], ("wr", chunk), me + (ROW << k),
                functools.partial(is_low, k),
            )

    def finish_row(k, chunk):
        rows = ROW_CHUNKS[chunk]

        @pl.when(is_low(k))
        def _():
            arrived(inr.at[k, rows, :], ("z", k, chunk))
            cur2[rows, :] = cur2[rows, :] - (wr[k, rows, :] + inr[k, rows, :])

    PANEL = ROW_CHUNKS[0]

    def send_shared(k):
        ours, ahead = wr.at[k, PANEL, :], backs[k]

        @pl.when(low_half(k))
        def _():
            value = cur2[PANEL, :]
            update = times_t(value, 3 + k)
            wr[k, PANEL, :] = value - update
            if k != 4:
                copy(
                    ours, inr.at[k, PANEL, :], ("z", k, 0), me + (ROW << k),
                    functools.partial(low_half, k),
                )

            @pl.when(is_low(k))
            def _():
                wback[k, :, :] = update
                copy(
                    ahead, wbr.at[PANEL, :], ("wr", 0), me + (ROW << k),
                    functools.partial(is_low, k),
                )

        @pl.when(high_half(k))
        def _():
            update = times_t(cur2[PANEL, :], 3 + k)
            wr[k, PANEL, :] = -update

            @pl.when(is_high(k))
            def _():
                zr[PANEL, :] = update
                res3[PANEL, :] = cur2[PANEL, :]

            if k != 4:
                copy(
                    ours, inr.at[k, PANEL, :], ("z", k, 0), me - (ROW << k),
                    functools.partial(high_half, k),
                )

        if k == 4:
            for source, targets in ((7, (1, 0)), (4, (2, 3)), (3, (5, 4)), (0, (6, 7))):
                @pl.when((y == 0) & (z == source))
                def _():
                    for target in targets:
                        copy(
                            ours, inr.at[k, PANEL, :], ("z", k, 0),
                            target * YDIM * ROW + r,
                            functools.partial(lambda o: (y == 0) & (z == o), source),
                        )

    def finish_shared(k):
        @pl.when(y == 0)
        def _():
            arrived(inr.at[k, PANEL, :], ("z", k, 0))
            cur2[PANEL, :] = wr[k, PANEL, :] + inr[k, PANEL, :]

    def send_level(k, chunk):
        if k > 1 and chunk == 0:
            send_shared(k)
        else:
            send_z(k, chunk)
            send_u(k, chunk)

    def finish_level(k, chunk):
        if k > 1 and chunk == 0:
            finish_shared(k)
        else:
            finish_row(k, chunk)

    def forward_operators(k):
        @pl.when(takes_fold(k) & (core == 0))
        def _():
            arrived(folds[3 + k], ("fold", 3 + k))
            copy(
                folds[3 + k], folds[3 + k], ("fold", 3 + k), me + 1,
                functools.partial(lambda k: takes_fold(k) & (core == 0), k),
            )

    def row_operators(k):
        @pl.when(takes_fold(k) & (core == 1))
        def _():
            arrived(folds[3 + k], ("fold", 3 + k))

        if k > 1:
            @pl.when(is_high(k))
            def _():
                make_fold(fold.at[3 + k], bt_high[3].astype(F32) + bt_low[3].astype(F32))

        @pl.when(takes_fold(k) if k < 2 else y == 0)
        def _():
            t_from_fold(3 + k)

    finish(2, 0)
    send_z(0, 0)
    finish(2, 1)
    send_z(0, 1)
    send_z(0, 2)
    forward_operators(0)
    give_back(2, 0)
    give_back(2, 1)

    row_operators(0)
    for chunk in range(3):
        send_u(0, chunk)

    def panel_to_row(condition):
        copy(panel.at[mine, :], panel.at[mine, :], ("panel core",), twin, condition)
        for j in (4, 2, 6):
            copy(
                panel.at[mine, :], panel.at[mine, :], ("panel",),
                base + (r + j) % ROW, condition,
            )

    def panel_out():
        @pl.when(y == 0)
        def _():
            panel[mine, :] = cur2[PANEL, :]
            for j in range(1, YDIM):
                copy(
                    panel.at[mine, :], panel.at[mine, :], ("panel y",), y_mate(j),
                    lambda: y == 0,
                )
            panel_to_row(lambda: y == 0)

    def gather_row(result, chunk, condition):
        for rank in range(ROW):
            start = place(3, rank, min(chunk, 1)).start
            start += eighth_b // 2 if chunk == 2 else 0
            rows = pl.ds(start, ROW_CHUNKS[chunk].size)

            @pl.when(r == rank)
            def _():
                if rank == 0:
                    gathered[rows, :] = result[ROW_CHUNKS[chunk], :]
                else:
                    copy(
                        result.at[ROW_CHUNKS[chunk], :], gathered.at[rows, :],
                        ("gather",), base,
                        functools.partial(lambda o: condition() & (r == o), rank),
                    )

    def row_result(k):
        for chunk in (1, 2, 0):
            rows = ROW_CHUNKS[chunk]

            @pl.when(is_high(k))
            def _():
                vt = halves(vt_of(slot3))
                arrived(wbr.at[rows, :], ("wr", chunk))
                start = res3 if k > 1 and chunk == 0 else cur2
                res3[rows, :] = start[rows, :] - dot_pairs(
                    halves(wbr[rows, :] + zr[rows, :]), vt
                )
                gather_row(res3, chunk, functools.partial(is_high, k))

    events = []
    for k in range(row_levels):
        events += [(2.9 * k + (5.0 if k > 3 else 0.0), k, 0)]
        events += [(2.0 + 4.2 * k, k, 1), (2.9 + 4.2 * k, k, 2)]
    done = set()
    last = row_levels - 1
    for _, k, chunk in sorted(events):
        if k < last and chunk == 0:
            forward_operators(k + 1)
            row_operators(k + 1)
        finish_level(k, chunk)
        if k < last:
            send_level(k + 1, chunk)
        done.add((k, chunk))
        if (k, chunk) == (last, 0):
            panel_out()
        if (k, chunk) == (last, 0 if last > 3 else 2):
            gram_all_y()
        if k == last:
            @pl.when(g == 0)
            def _():
                gather_row(cur2, chunk, lambda: g == 0)
        if (k, chunk) == (0, 2):
            gram_sum_z()
            residual(0, gathered)
            residual(1, res1)
            for rank, into in ((2, 2), (3, 2), (6, 6), (7, 6)):
                @pl.when(r == rank)
                def _():
                    gather(1, res1, rank, into, CHUNKS, functools.partial(lambda o: r == o, rank))
        if (k, chunk) == (1, 2):
            residual(2, res2)
            for rank in range(4, ROW):
                @pl.when(r == rank)
                def _():
                    gather(2, res2, rank, 4, CHUNKS, functools.partial(lambda o: r == o, rank))
            gram_sum_x()
        if k and chunk == 2:
            row_result(k - 1)
        if (k, chunk) == (last, 2):
            row_result(last)

    @pl.when(y != 0)
    def _():
        arrived(panel.at[mine, :], ("panel y",))
        panel_to_row(lambda: y != 0)

    arrived(panel.at[pl.ds(0, 3 * piece), :], ("panel",))
    for j in (2, 6, 4):
        theirs = piece_of((r + j) % ROW)
        copy(panel.at[theirs, :], panel.at[theirs, :], ("panel core",), twin)

    @pl.when((r == 2) | (r == 6))
    def _():
        arrived(gathered.at[pl.ds(0, nc // 2), :], ("gather",))

    @pl.when(r == 4)
    def _():
        arrived(gathered.at[pl.ds(0, 3 * nc // 4), :], ("gather",))

    @pl.when(r == 0)
    def _():
        arrived(gathered.at[pl.ds(0, 7 * nc // 8), :], ("gather",))

    head_rows[...] = gathered[...].T
    head_basis[...] = jnp.where(me == 0, 0.0, dot3(head_rows[:, :b], inv_ref[...]))
    arrived(gram_all.at[pl.ds(0, b - yrows), :], ("all y",))
    arrived(panel.at[pl.ds(0, 4 * piece), :], ("panel core",))
    square = dot3(panel[...], panel[...], True)
    gram_total[...] = (gram_all[...] - square) / float(total_rows)

    for condition, source in pending:
        made = functools.partial(
            lambda source: remote(source, source, 0, neighbour).wait_send(), source
        )
        if condition is None:
            made()
        else:
            @pl.when(condition())
            def _():
                made()
    assert len(numbers) <= recv_sems.shape[0]


def write_kernel(
    head_rows, rest, head_basis, rest_basis, gram, upd_out, basis_out, gram_out, sems
):
    b = head_rows.shape[0]
    copies = [
        pltpu.make_async_copy(source, target, sems.at[index])
        for index, (source, target) in enumerate((
            (head_rows, upd_out.at[pl.ds(0, b), :]),
            (rest, upd_out.at[pl.ds(b, b), :]),
            (head_basis, basis_out.at[pl.ds(0, b), :]),
            (rest_basis, basis_out.at[pl.ds(b, b), :]),
            (gram, gram_out),
        ))
    ]
    for made in copies:
        made.start()
    for made in copies:
        made.wait()


def body(trailing, leaf_vectors, leaf_factors, tree_vectors, tree_factors, inverse_factor):
    b, nc = leaf_vectors.shape[1], trailing.shape[1]
    devices = lax.axis_size("rows")
    total_rows = trailing.shape[0] * devices
    levels = (devices // ROW).bit_length() - 1
    piece = b // ROW
    zdim = devices // ROW // YDIM

    def vmem(*shape, dtype=F32):
        return pltpu.VMEM(shape, dtype)

    arguments = (
        trailing, leaf_vectors, leaf_factors, tree_vectors, tree_factors, inverse_factor
    )
    per_level = [vmem(nc >> level, b) for level in (1, 2, 3)]
    scratch = [
        *[vmem(*argument.shape) for argument in arguments],
        vmem(b + 8, b),
        vmem(b // 2 + 8, b),
        *[vmem(b + 8, b)] * 4,
        vmem(3 + levels, b // 2 + 8, b),
        vmem(b // 2 + 8, b), vmem(b // 2 + 8, b),
        vmem(3 + levels, b, b, dtype=BF16),
        vmem(3 + levels, b, b, dtype=BF16),
        vmem(4, b, b, dtype=BF16),
        vmem(4, b, b, dtype=BF16),
        vmem(nc, b),
        *per_level,
        *per_level, *per_level, *per_level, *per_level,
        vmem(nc // 8, b), vmem(levels, nc // 8, b), vmem(levels, nc // 8, b),
        vmem(nc // 8, b),
        *per_level,
        vmem(nc, b),
        vmem(b, nc),
        vmem(b, 2 * b, dtype=BF16), vmem(b, 2 * b, dtype=BF16),
        vmem(b, b),
        vmem(b // YDIM, b),
        vmem(YDIM - 1, b // YDIM, b),
        vmem(max(zdim - 1, 1), b // YDIM // zdim, b),
        vmem(ROW, b // YDIM // zdim, b),
        vmem(b, b), vmem(b, b),
        vmem(levels, piece, b),
        pltpu.SemaphoreType.DMA,
        pltpu.SemaphoreType.DMA((RECEIVES,)),
        pltpu.SemaphoreType.DMA((7,)),
    ]
    results = pl.pallas_call(
        functools.partial(tree_kernel, devices, total_rows),
        out_shape=(
            vmem(b, nc), vmem(b, nc), vmem(b, b), vmem(b, b), vmem(b, b)
        ),
        in_specs=[pl.BlockSpec(memory_space=pltpu.HBM)] * 6,
        out_specs=[pl.BlockSpec(memory_space=pltpu.VMEM)] * 5,
        scratch_shapes=scratch,
        compiler_params=pltpu.CompilerParams(
            collective_id=0,
            has_side_effects=True,
            vmem_limit_bytes=56 * 1024 * 1024,
        ),
        name="tree",
    )(*arguments)
    return pl.pallas_call(
        write_kernel,
        out_shape=(
            jax.ShapeDtypeStruct(trailing.shape, F32),
            jax.ShapeDtypeStruct(leaf_vectors.shape, F32),
            jax.ShapeDtypeStruct((b, b), F32),
        ),
        in_specs=[pl.BlockSpec(memory_space=pltpu.VMEM)] * 5,
        out_specs=[pl.BlockSpec(memory_space=pl.ANY)] * 3,
        scratch_shapes=[pltpu.SemaphoreType.DMA((5,))],
        name="write",
    )(*[pltpu.with_memory_space_constraint(result, pltpu.VMEM) for result in results])


def solution(mesh):
    rows = P("rows", None)
    return jax.shard_map(
        body,
        mesh=mesh,
        in_specs=(rows, rows, rows, rows, rows, P()),
        out_specs=(rows, rows, P()),
        check_vma=False,
    )
```
